256 devices in a mesh: dp: 2 (over core), ctx: 32 (over z, y), head: 4 (over x).
Axes of the slice: x: 4, y: 4, z: 8, core: 2. Of those that a mesh axis runs over, the one named last changes fastest.
Arguments:
- queries: bfloat16 [2, 32768, 2048], P('dp', 'ctx', 'head'), may hold values from -6 to 6
- keys_raw: bfloat16 [2, 32768, 2048], P('dp', 'ctx', 'head'), may hold values from -0.625 to 0.625
- values: bfloat16 [2, 32768, 2048], P('dp', 'ctx', 'head'), may hold values from -6 to 6
- gates: float32 [2, 16, 32768], P('dp', 'head', 'ctx'), as said below
- lengths: int32 [2, 16], P('dp'), may hold values from 1 to 8192, 32768 in all within a row
- key_gain: float32 [16, 128], P('head'), may hold values from 0.1 to 1.9
- cotangent: bfloat16 [2, 32768, 2048], P('dp', 'ctx', 'head'), may hold values from -6 to 6
Outputs:
- attended: bfloat16 [2, 32768, 2048], P('dp', 'ctx', 'head')
- grad_queries: bfloat16 [2, 32768, 2048], P('dp', 'ctx', 'head')
- grad_keys: bfloat16 [2, 32768, 2048], P('dp', 'ctx', 'head')
- grad_values: bfloat16 [2, 32768, 2048], P('dp', 'ctx', 'head')
- grad_gates: float32 [2, 16, 32768], P('dp', 'head', 'ctx')
- grad_gain: float32 [16, 128], P('head', 'dp')
The draws below stay inside these ranges and needn't reach their ends.
Inputs may be any that keep to these rules, and one draw needn't show every extreme that they name: Each row of lengths gives its documents in packing order and sums to 32768. `gates`: every entry is negative.
All inputs are finite; a program needn't handle non-finite values.
Results may differ from the reference program's by a relative error of at most 0.009.
Values sent between devices are 32-bit elements; how exact they have to be, the bound alone decides.
A program may use at most 128 MiB of HBM per device.

```python
import math
import jax
import jax.numpy as jnp
import numpy as np
from jax import lax

LOCAL_HEADS = 16
DH = 128
TOK_DEV = 1024
BLOCK = 512
DOCS = 16
SEQUENCE_LENGTH = 32768
BATCH_SEQUENCES = 2
DOC_MOST = 8192


def draw_gates(key, part):
    parallel_lanes = jax.random.split(key, 7)
    shards = SEQUENCE_LENGTH // TOK_DEV
    fast_share = 0.5
    is_fast = jax.random.uniform(parallel_lanes[0], (BATCH_SEQUENCES, LOCAL_HEADS, 1, 1)) < fast_share
    fast_rate = jnp.exp(jax.random.uniform(parallel_lanes[1], (BATCH_SEQUENCES, LOCAL_HEADS, 1, 1), minval=jnp.log(1.0 / 50.0), maxval=jnp.log(1.0 / 30.0)))
    slow_rate = jnp.exp(jax.random.uniform(parallel_lanes[2], (BATCH_SEQUENCES, LOCAL_HEADS, 1, 1), minval=jnp.log(0.05), maxval=jnp.log(0.3))) / DOC_MOST
    base_rate = jnp.where(is_fast, fast_rate, slow_rate)
    shard_factor = jnp.exp(jax.random.uniform(parallel_lanes[3], (BATCH_SEQUENCES, LOCAL_HEADS, shards, 1), minval=-0.7, maxval=0.7))
    jitter = jnp.exp(jax.random.uniform(parallel_lanes[4], (BATCH_SEQUENCES, LOCAL_HEADS, shards, TOK_DEV), minval=-0.7, maxval=0.7))
    gentle_gate = -(base_rate * shard_factor * jitter).reshape(BATCH_SEQUENCES, LOCAL_HEADS, SEQUENCE_LENGTH)
    spike_gate = jax.random.uniform(parallel_lanes[5], (BATCH_SEQUENCES, LOCAL_HEADS, SEQUENCE_LENGTH)) < 4.0 / SEQUENCE_LENGTH
    spike_gate_value = jnp.log(jax.random.uniform(parallel_lanes[6], (BATCH_SEQUENCES, LOCAL_HEADS, SEQUENCE_LENGTH), minval=0.5, maxval=0.8))
    return jnp.where(spike_gate, spike_gate_value, gentle_gate).astype(jnp.float32)


def block_levels(rng, extent, pieces, smallest, top_value):
    def one(axis_at, shards_of):
        draws = jax.random.uniform(jax.random.fold_in(jax.random.fold_in(rng, 6), axis_at), (shards_of,), jnp.float32, smallest / len(pieces), top_value / len(pieces))
        return jnp.repeat(jnp.exp(draws), extent[axis_at] // shards_of).reshape((-1,) + (1,) * (len(extent) - axis_at - 1))

    level = one(*pieces[0])
    for cut in pieces[1:]:
        level = level * one(*cut)
    return level


def length_profile(count, total, reach, skew):
    weights = [(1 << 20) // math.isqrt(grade ** skew) + 1 for grade in range(2, count + 1)]
    spare, given = total - reach - (count - 1), [1] * (count - 1)
    while spare > 0:
        movable = [i for i in range(count - 1) if given[i] < reach]
        whole, left = sum([weights[i] for i in movable]), spare
        for i in movable:
            addition = min(reach - given[i], max(1, left * weights[i] // whole), spare)
            given[i] = given[i] + addition
            spare = spare - addition
    return np.array([reach] + given)


def ragged_sizes(key, number_of, total, most, slope):
    if number_of == 2:
        one = jax.random.randint(key, (), max(1, total - most), min(most, total - 1) + 1)
        return jnp.stack([one, total - one])
    sizes = jnp.asarray(length_profile(number_of, total, most, slope), jnp.int32)
    twos = (number_of - 1) // 2
    giver, sink = sizes[1:1 + 2 * twos:2], sizes[2:2 + 2 * twos:2]
    slack = jnp.minimum(giver - 1, most - sink)
    passed = jax.random.randint(jax.random.fold_in(key, 1), (twos,), 0, 1 << 20) % (slack + 1)
    sizes = sizes.at[1:1 + 2 * twos:2].set(giver - passed).at[2:2 + 2 * twos:2].set(sink + passed)
    return sizes[jax.random.permutation(jax.random.fold_in(key, 2), number_of)]


def centred(stream_key, shape, scale, limit, cuts=(), held_as=jnp.bfloat16):
    loudness = block_levels(stream_key, shape, cuts, -0.22, 0.18) if cuts else 1.0
    result = jax.random.normal(stream_key, shape, jnp.float32) * scale * loudness
    return jnp.minimum(jnp.maximum(result, -limit), limit).astype(held_as)


def setup_inputs(seed: int = 0) -> dict:
    keys = jax.random.split(jax.random.key(seed), 8)
    queries = centred(keys[0], (BATCH_SEQUENCES, SEQUENCE_LENGTH, LOCAL_HEADS * DH), 1.0, 6.0, ((0, 2), (1, 32), (2, 4)))
    keys_raw = centred(keys[1], (BATCH_SEQUENCES, SEQUENCE_LENGTH, LOCAL_HEADS * DH), 0.1, 0.625, ((0, 2), (1, 32), (2, 4)))
    values = centred(keys[2], (BATCH_SEQUENCES, SEQUENCE_LENGTH, LOCAL_HEADS * DH), 1.0, 6.0, ((0, 2), (1, 32), (2, 4)))
    gates = draw_gates(jax.random.fold_in(keys[7], 71), 0)
    lengths = jax.vmap(lambda own: ragged_sizes(own, DOCS, SEQUENCE_LENGTH, DOC_MOST, 2))(jax.random.split(keys[4], BATCH_SEQUENCES)).reshape((BATCH_SEQUENCES, DOCS)).astype(jnp.int32)
    key_gain = jnp.clip(1.0 + 0.18 * jax.random.normal(keys[5], (LOCAL_HEADS, DH), jnp.float32), 0.1, 1.9)
    cotangent = centred(keys[6], (BATCH_SEQUENCES, SEQUENCE_LENGTH, LOCAL_HEADS * DH), 1.0, 6.0, ((0, 2), (1, 32), (2, 4)))
    return dict(queries=queries, keys_raw=keys_raw, values=values, gates=gates, lengths=lengths, key_gain=key_gain, cotangent=cotangent)


PRECISE = lax.Precision.HIGHEST

def start_flags(doc_lengths, first_pos, num_rows):
    starts = jnp.cumsum(doc_lengths, dtype=jnp.int32) - doc_lengths
    positions = first_pos + jnp.arange(num_rows, dtype=jnp.int32)
    matches = jnp.any(positions[:, None] == starts[None, :], axis=1)
    return matches.astype(jnp.float32)

def make_step(key_gain, head_width):
    q_scale = head_width ** (-0.5)

    def block_step(carried, inputs):
        q_block, k_block, v_block, gate_block, flag_block = inputs
        k_bf = (k_block.astype(jnp.float32) * key_gain[None]).astype(jnp.bfloat16)
        q_float = q_block.astype(jnp.float32) * q_scale
        k_float = lax.optimization_barrier(k_bf).astype(jnp.float32)
        v_float = v_block.astype(jnp.float32)
        segment = jnp.cumsum(flag_block)
        positions = jnp.arange(flag_block.shape[0])
        same_doc = (segment[:, None] == segment[None, :]) & (positions[:, None] >= positions[None, :])
        cum_decay = jnp.cumsum(gate_block, axis=1)
        exponent = cum_decay[:, :, None] - cum_decay[:, None, :]
        decays = jnp.where(same_doc[None], jnp.exp(jnp.where(same_doc[None], exponent, 0.0)), 0.0)
        scores = jnp.einsum('thd,shd->hts', q_block, k_bf, preferred_element_type=jnp.float32)
        weights = (scores * q_scale * decays).astype(jnp.bfloat16)
        within = jnp.einsum('hts,she->the', weights, v_block, preferred_element_type=jnp.float32)
        opened = (segment == 0).astype(cum_decay.dtype)
        carry_in = jnp.exp(cum_decay) * opened[None, :]
        across = jnp.einsum('thd,hde->the', q_float, carried, precision=PRECISE) * carry_in.T[:, :, None]
        tail_mask = (segment == segment[-1]).astype(cum_decay.dtype)
        to_end = jnp.exp(cum_decay[:, -1:] - cum_decay) * tail_mask[None, :]
        written = jnp.einsum('shd,she->hde', k_float * to_end.T[:, :, None], v_float, precision=PRECISE)
        end_state = carried * carry_in[:, -1][:, None, None] + written
        return (end_state, within + across)
    return block_step

def run_blocks(q_rows, k_rows, v_rows, gate_rows, flags, key_gain, start_state):
    num_rows = q_rows.shape[0]
    head_count = key_gain.shape[0]
    head_width = key_gain.shape[1]
    num_blocks = num_rows // BLOCK

    def to_blocks(tensor):
        return tensor.reshape(num_blocks, BLOCK, head_count, head_width)
    gate_blocks = gate_rows.reshape(head_count, num_blocks, BLOCK).transpose(1, 0, 2)
    flag_blocks = flags.reshape(num_blocks, BLOCK)
    end_state, outputs = lax.scan(jax.checkpoint(make_step(key_gain, head_width)), start_state, (to_blocks(q_rows), to_blocks(k_rows), to_blocks(v_rows), gate_blocks, flag_blocks))
    return (outputs.reshape(num_rows, head_count * head_width), end_state)

def reference(queries, keys_raw, values, gates, lengths, key_gain, cotangent):
    attended, grad_q, grad_k, grad_v, grad_a = ([], [], [], [], [])
    grad_gain = jnp.zeros((LOCAL_HEADS, DH), jnp.float32)
    for batch_row in range(BATCH_SEQUENCES):
        flags = start_flags(lengths[batch_row], 0, SEQUENCE_LENGTH)
        zero_state = jnp.zeros((LOCAL_HEADS, DH, DH), jnp.float32)

        def forward(q_rows, k_rows, v_rows, gate_rows, gain_rows):
            return run_blocks(q_rows, k_rows, v_rows, gate_rows, flags, gain_rows, zero_state)[0]
        primal, pullback = jax.vjp(forward, queries[batch_row], keys_raw[batch_row], values[batch_row], gates[batch_row], key_gain)
        grads = pullback(cotangent[batch_row].astype(jnp.float32))
        attended.append(primal.astype(jnp.bfloat16))
        grad_q.append(grads[0])
        grad_k.append(grads[1])
        grad_v.append(grads[2])
        grad_a.append(grads[3])
        grad_gain = grad_gain + grads[4]
    return (jnp.stack(attended), jnp.stack(grad_q), jnp.stack(grad_k), jnp.stack(grad_v), jnp.stack(grad_a), grad_gain)
```

```python
import jax
import jax.numpy as jnp
from jax import lax
from jax.sharding import PartitionSpec as P

BLOCK = 512


PRECISE = lax.Precision.HIGHEST


def passed_along(value, axis, steps):
    count = lax.axis_size(axis)
    first, last = (max(0, -steps), min(count, count - steps))
    return lax.ppermute(value, axis, [(source, source + steps) for source in range(first, last)])


def local_incoming_grad(q_rows, cot_rows, cum_decay, opened, head_count, head_width):
    tok_rows = q_rows.shape[0]
    factor = jnp.exp(cum_decay) * opened[None, :]
    weighted = (
        q_rows.reshape(tok_rows, head_count, head_width).astype(jnp.float32)
        * head_width ** (-0.5)
        * factor.T[:, :, None]
    )
    cot_float = cot_rows.astype(jnp.float32)
    return jnp.einsum(
        "thd,the->hde",
        weighted,
        cot_float.reshape(tok_rows, head_count, head_width),
        precision=PRECISE,
    )


def pack(decay, term):
    lane = jnp.broadcast_to(decay[:, None, None], (term.shape[0], 1, term.shape[2]))
    return jnp.concatenate([term, lane], axis=1)


def both_scans(decay, fwd_term, bwd_term, count):
    rows = fwd_term.shape[1]
    scans = []
    for term in (fwd_term, bwd_term):
        scans.append([decay, term, jnp.ones_like(decay), jnp.zeros_like(term)])
    shift = 1
    while shift < count:
        got = [
            passed_along(pack(agg_a, agg_b), "ctx", shift * sign)
            for (agg_a, agg_b, _, _), sign in zip(scans, (1, -1))
        ]
        for index, received in enumerate(got):
            agg_a, agg_b, ex_a, ex_b = scans[index]
            r_b, r_a = received[:, :rows], received[:, rows, 0]
            ex_b = ex_a[:, None, None] * r_b + ex_b
            ex_a = ex_a * r_a
            agg_b = agg_a[:, None, None] * r_b + agg_b
            agg_a = agg_a * r_a
            scans[index] = [agg_a, agg_b, ex_a, ex_b]
        shift *= 2
    return scans[0][3], scans[1][3]


def start_flags(doc_lengths, first_pos, num_rows):
    starts = jnp.cumsum(doc_lengths, dtype=jnp.int32) - doc_lengths
    positions = first_pos + jnp.arange(num_rows, dtype=jnp.int32)
    matches = jnp.any(positions[:, None] == starts[None, :], axis=1)
    return matches.astype(jnp.float32)


def make_step(key_gain, head_width):
    q_scale = head_width ** (-0.5)

    def block_step(carried, inputs):
        q_block, k_block, v_block, gate_block, flag_block = inputs
        k_bf = (k_block.astype(jnp.float32) * key_gain[None]).astype(jnp.bfloat16)
        q_float = q_block.astype(jnp.float32) * q_scale
        k_float = lax.optimization_barrier(k_bf).astype(jnp.float32)
        v_float = v_block.astype(jnp.float32)
        segment = jnp.cumsum(flag_block)
        positions = jnp.arange(flag_block.shape[0])
        same_doc = (segment[:, None] == segment[None, :]) & (
            positions[:, None] >= positions[None, :]
        )
        cum_decay = jnp.cumsum(gate_block, axis=1)
        exponent = cum_decay[:, :, None] - cum_decay[:, None, :]
        decays = jnp.where(same_doc[None], jnp.exp(jnp.where(same_doc[None], exponent, 0.0)), 0.0)
        scores = jnp.einsum("thd,shd->hts", q_block, k_bf, preferred_element_type=jnp.float32)
        weights = (scores * q_scale * decays).astype(jnp.bfloat16)
        within = jnp.einsum("hts,she->the", weights, v_block, preferred_element_type=jnp.float32)
        opened = (segment == 0).astype(cum_decay.dtype)
        carry_in = jnp.exp(cum_decay) * opened[None, :]
        across = (
            jnp.einsum("thd,hde->the", q_float, carried, precision=PRECISE) * carry_in.T[:, :, None]
        )
        tail_mask = (segment == segment[-1]).astype(cum_decay.dtype)
        to_end = jnp.exp(cum_decay[:, -1:] - cum_decay) * tail_mask[None, :]
        written = jnp.einsum(
            "shd,she->hde", k_float * to_end.T[:, :, None], v_float, precision=PRECISE
        )
        end_state = carried * carry_in[:, -1][:, None, None] + written
        return (end_state, within + across)

    return block_step


def run_blocks(q_rows, k_rows, v_rows, gate_rows, flags, key_gain, start_state):
    num_rows = q_rows.shape[0]
    head_count = key_gain.shape[0]
    head_width = key_gain.shape[1]
    num_blocks = num_rows // BLOCK

    def to_blocks(tensor):
        return tensor.reshape(num_blocks, BLOCK, head_count, head_width)

    gate_blocks = gate_rows.reshape(head_count, num_blocks, BLOCK).transpose(1, 0, 2)
    flag_blocks = flags.reshape(num_blocks, BLOCK)
    end_state, outputs = lax.scan(
        jax.checkpoint(make_step(key_gain, head_width)),
        start_state,
        (to_blocks(q_rows), to_blocks(k_rows), to_blocks(v_rows), gate_blocks, flag_blocks),
    )
    return (outputs.reshape(num_rows, head_count * head_width), end_state)


def shards(queries, keys_raw, values, gates, lengths, key_gain, cotangent):
    tok_rows = queries.shape[1]
    head_count = key_gain.shape[0]
    head_width = key_gain.shape[1]
    flags = start_flags(lengths[0], lax.axis_index("ctx") * tok_rows, tok_rows)
    q_rows, k_rows, v_rows, gate_rows = (queries[0], keys_raw[0], values[0], gates[0])
    segment = jnp.cumsum(flags)
    opened = (segment == 0).astype(jnp.float32)
    tail_mask = (segment == segment[-1]).astype(jnp.float32)
    cum_decay = jnp.cumsum(gate_rows, axis=1)
    shard_decay = jnp.exp(cum_decay[:, -1]) * opened[-1]
    to_end = jnp.exp(cum_decay[:, -1:] - cum_decay) * tail_mask[None, :]
    k_bf = (
        k_rows.reshape(tok_rows, head_count, head_width).astype(jnp.float32) * key_gain[None]
    ).astype(jnp.bfloat16)
    k_float = lax.optimization_barrier(k_bf).astype(jnp.float32)
    v_float = v_rows.reshape(tok_rows, head_count, head_width).astype(jnp.float32)
    local_end = jnp.einsum(
        "shd,she->hde", k_float * to_end.T[:, :, None], v_float, precision=PRECISE
    )
    ctx_size = lax.axis_size("ctx")
    local_grad = local_incoming_grad(q_rows, cotangent[0], cum_decay, opened, head_count, head_width)
    state_in, later_grad = both_scans(shard_decay, local_end, local_grad, ctx_size)

    def forward(q_part, k_part, v_part, gate_part, gain_part):
        return run_blocks(q_part, k_part, v_part, gate_part, flags, gain_part, state_in)

    (primal, end_state), pullback = jax.vjp(forward, q_rows, k_rows, v_rows, gate_rows, key_gain)
    cot_float = cotangent[0].astype(jnp.float32)
    grad_q, grad_k, grad_v, grad_a, gain_term = pullback((cot_float, later_grad))
    gain_total = lax.psum(gain_term, "ctx")
    grad_gain = lax.psum_scatter(gain_total, "dp", scatter_dimension=1, tiled=True)
    return (
        primal.astype(jnp.bfloat16)[None],
        grad_q[None],
        grad_k[None],
        grad_v[None],
        grad_a[None],
        grad_gain,
    )


def solution(mesh):
    placed = (
        P("dp", "ctx", "head"),
        P("dp", "ctx", "head"),
        P("dp", "ctx", "head"),
        P("dp", "head", "ctx"),
        P("dp", None),
        P("head", None),
        P("dp", "ctx", "head"),
    )
    return jax.shard_map(
        shards,
        mesh=mesh,
        in_specs=placed,
        out_specs=(
            P("dp", "ctx", "head"),
            P("dp", "ctx", "head"),
            P("dp", "ctx", "head"),
            P("dp", "ctx", "head"),
            P("dp", "head", "ctx"),
            P("head", "dp"),
        ),
        check_vma=False,
    )
```

```python
import jax
import jax.numpy as jnp
from jax import lax
from jax.sharding import PartitionSpec as P

BLOCK = 512


PRECISE = lax.Precision.HIGHEST


def passed_along(value, axis, steps):
    count = lax.axis_size(axis)
    first, last = (max(0, -steps), min(count, count - steps))
    return lax.ppermute(value, axis, [(source, source + steps) for source in range(first, last)])


def local_incoming_grad(q_rows, cot_rows, cum_decay, opened, head_count, head_width):
    tok_rows = q_rows.shape[0]
    factor = jnp.exp(cum_decay) * opened[None, :]
    weighted = (
        q_rows.reshape(tok_rows, head_count, head_width).astype(jnp.float32)
        * head_width ** (-0.5)
        * factor.T[:, :, None]
    )
    cot_float = cot_rows.astype(jnp.float32)
    return jnp.einsum(
        "thd,the->hde",
        weighted,
        cot_float.reshape(tok_rows, head_count, head_width),
        precision=PRECISE,
    )


def pack(decay, term):
    lane = jnp.broadcast_to(decay[:, None, None], (term.shape[0], 1, term.shape[2]))
    return jnp.concatenate([term, lane], axis=1)


def both_scans(decay, fwd_term, bwd_term, count):
    rows = fwd_term.shape[1]
    scans = []
    for term in (fwd_term, bwd_term):
        scans.append([decay, term, jnp.ones_like(decay), jnp.zeros_like(term)])
    shift = 1
    while shift < count:
        got = [
            passed_along(pack(agg_a, agg_b), "ctx", shift * sign)
            for (agg_a, agg_b, _, _), sign in zip(scans, (1, -1))
        ]
        for index, received in enumerate(got):
            agg_a, agg_b, ex_a, ex_b = scans[index]
            r_b, r_a = received[:, :rows], received[:, rows, 0]
            ex_b = ex_a[:, None, None] * r_b + ex_b
            ex_a = ex_a * r_a
            agg_b = agg_a[:, None, None] * r_b + agg_b
            agg_a = agg_a * r_a
            scans[index] = [agg_a, agg_b, ex_a, ex_b]
        shift *= 2
    return scans[0][3], scans[1][3]


def start_flags(doc_lengths, first_pos, num_rows):
    starts = jnp.cumsum(doc_lengths, dtype=jnp.int32) - doc_lengths
    positions = first_pos + jnp.arange(num_rows, dtype=jnp.int32)
    matches = jnp.any(positions[:, None] == starts[None, :], axis=1)
    return matches.astype(jnp.float32)


def make_step(key_gain, head_width):
    q_scale = head_width ** (-0.5)

    def block_step(carried, inputs):
        q_block, k_block, v_block, gate_block, flag_block = inputs
        k_bf = (k_block.astype(jnp.float32) * key_gain[None]).astype(jnp.bfloat16)
        q_float = q_block.astype(jnp.float32) * q_scale
        k_float = lax.optimization_barrier(k_bf).astype(jnp.float32)
        v_float = v_block.astype(jnp.float32)
        segment = jnp.cumsum(flag_block)
        positions = jnp.arange(flag_block.shape[0])
        same_doc = (segment[:, None] == segment[None, :]) & (
            positions[:, None] >= positions[None, :]
        )
        cum_decay = jnp.cumsum(gate_block, axis=1)
        exponent = cum_decay[:, :, None] - cum_decay[:, None, :]
        decays = jnp.where(same_doc[None], jnp.exp(jnp.where(same_doc[None], exponent, 0.0)), 0.0)
        scores = jnp.einsum("thd,shd->hts", q_block, k_bf, preferred_element_type=jnp.float32)
        weights = (scores * q_scale * decays).astype(jnp.bfloat16)
        within = jnp.einsum("hts,she->the", weights, v_block, preferred_element_type=jnp.float32)
        opened = (segment == 0).astype(cum_decay.dtype)
        carry_in = jnp.exp(cum_decay) * opened[None, :]
        across = (
            jnp.einsum("thd,hde->the", q_float, carried, precision=PRECISE) * carry_in.T[:, :, None]
        )
        tail_mask = (segment == segment[-1]).astype(cum_decay.dtype)
        to_end = jnp.exp(cum_decay[:, -1:] - cum_decay) * tail_mask[None, :]
        written = jnp.einsum(
            "shd,she->hde", k_float * to_end.T[:, :, None], v_float, precision=PRECISE
        )
        end_state = carried * carry_in[:, -1][:, None, None] + written
        return (end_state, within + across)

    return block_step


def run_blocks(q_rows, k_rows, v_rows, gate_rows, flags, key_gain, start_state):
    num_rows = q_rows.shape[0]
    head_count = key_gain.shape[0]
    head_width = key_gain.shape[1]
    num_blocks = num_rows // BLOCK

    def to_blocks(tensor):
        return tensor.reshape(num_blocks, BLOCK, head_count, head_width)

    gate_blocks = gate_rows.reshape(head_count, num_blocks, BLOCK).transpose(1, 0, 2)
    flag_blocks = flags.reshape(num_blocks, BLOCK)
    end_state, outputs = lax.scan(
        jax.checkpoint(make_step(key_gain, head_width)),
        start_state,
        (to_blocks(q_rows), to_blocks(k_rows), to_blocks(v_rows), gate_blocks, flag_blocks),
    )
    return (outputs.reshape(num_rows, head_count * head_width), end_state)


def shards(queries, keys_raw, values, gates, lengths, key_gain, cotangent):
    tok_rows = queries.shape[1]
    head_count = key_gain.shape[0]
    head_width = key_gain.shape[1]
    flags = start_flags(lengths[0], lax.axis_index("ctx") * tok_rows, tok_rows)
    q_rows, k_rows, v_rows, gate_rows = (queries[0], keys_raw[0], values[0], gates[0])
    segment = jnp.cumsum(flags)
    opened = (segment == 0).astype(jnp.float32)
    tail_mask = (segment == segment[-1]).astype(jnp.float32)
    cum_decay = jnp.cumsum(gate_rows, axis=1)
    shard_decay = jnp.exp(cum_decay[:, -1]) * opened[-1]
    to_end = jnp.exp(cum_decay[:, -1:] - cum_decay) * tail_mask[None, :]
    k_bf = (
        k_rows.reshape(tok_rows, head_count, head_width).astype(jnp.float32) * key_gain[None]
    ).astype(jnp.bfloat16)
    k_float = lax.optimization_barrier(k_bf).astype(jnp.float32)
    v_float = v_rows.reshape(tok_rows, head_count, head_width).astype(jnp.float32)
    local_end = jnp.einsum(
        "shd,she->hde", k_float * to_end.T[:, :, None], v_float, precision=PRECISE
    )
    ctx_size = lax.axis_size("ctx")
    local_grad = local_incoming_grad(q_rows, cotangent[0], cum_decay, opened, head_count, head_width)
    state_in, later_grad = both_scans(shard_decay, local_end, local_grad, ctx_size)

    def forward(q_part, k_part, v_part, gate_part, gain_part):
        return run_blocks(q_part, k_part, v_part, gate_part, flags, gain_part, state_in)

    (primal, end_state), pullback = jax.vjp(forward, q_rows, k_rows, v_rows, gate_rows, key_gain)
    cot_float = cotangent[0].astype(jnp.float32)
    grad_q, grad_k, grad_v, grad_a, gain_term = pullback((cot_float, later_grad))
    gain_half = lax.psum_scatter(gain_term, "dp", scatter_dimension=1, tiled=True)
    grad_gain = jnp.sum(lax.all_gather(gain_half, "ctx"), axis=0)
    return (
        primal.astype(jnp.bfloat16)[None],
        grad_q[None],
        grad_k[None],
        grad_v[None],
        grad_a[None],
        grad_gain,
    )


def solution(mesh):
    placed = (
        P("dp", "ctx", "head"),
        P("dp", "ctx", "head"),
        P("dp", "ctx", "head"),
        P("dp", "head", "ctx"),
        P("dp", None),
        P("head", None),
        P("dp", "ctx", "head"),
    )
    return jax.shard_map(
        shards,
        mesh=mesh,
        in_specs=placed,
        out_specs=(
            P("dp", "ctx", "head"),
            P("dp", "ctx", "head"),
            P("dp", "ctx", "head"),
            P("dp", "ctx", "head"),
            P("dp", "head", "ctx"),
            P("head", "dp"),
        ),
        check_vma=False,
    )
```

```python
import jax
import jax.numpy as jnp
from jax import lax
from jax.sharding import PartitionSpec as P
from jax.experimental import pallas as pl
from jax.experimental.pallas import tpu as pltpu

BLOCK = 512


PRECISE = lax.Precision.HIGHEST


def passed_along(value, axis, steps):
    count = lax.axis_size(axis)
    first, last = (max(0, -steps), min(count, count - steps))
    return lax.ppermute(value, axis, [(source, source + steps) for source in range(first, last)])


def local_incoming_grad(q_rows, cot_rows, cum_decay, opened, head_count, head_width):
    tok_rows = q_rows.shape[0]
    factor = jnp.exp(cum_decay) * opened[None, :]
    weighted = (
        q_rows.reshape(tok_rows, head_count, head_width).astype(jnp.float32)
        * head_width ** (-0.5)
        * factor.T[:, :, None]
    )
    cot_float = cot_rows.astype(jnp.float32)
    return jnp.einsum(
        "thd,the->hde",
        weighted,
        cot_float.reshape(tok_rows, head_count, head_width),
        precision=PRECISE,
    )


def pack(decay, term):
    lane = jnp.broadcast_to(decay[:, None, None], (term.shape[0], 1, term.shape[2]))
    return jnp.concatenate([term, lane], axis=1)


def both_scans(decay, fwd_term, bwd_term, count):
    rows = fwd_term.shape[1]
    scans = []
    for term in (fwd_term, bwd_term):
        scans.append([decay, term, jnp.ones_like(decay), jnp.zeros_like(term)])
    shift = 1
    while shift < count:
        got = [
            passed_along(pack(agg_a, agg_b), "ctx", shift * sign)
            for (agg_a, agg_b, _, _), sign in zip(scans, (1, -1))
        ]
        for index, received in enumerate(got):
            agg_a, agg_b, ex_a, ex_b = scans[index]
            r_b, r_a = received[:, :rows], received[:, rows, 0]
            ex_b = ex_a[:, None, None] * r_b + ex_b
            ex_a = ex_a * r_a
            agg_b = agg_a[:, None, None] * r_b + agg_b
            agg_a = agg_a * r_a
            scans[index] = [agg_a, agg_b, ex_a, ex_b]
        shift *= 2
    return scans[0][3], scans[1][3]


def gain_sum_kernel(part_ref, total_ref, slots, send_sem, recv_sem):
    count = slots.shape[0]
    me = lax.axis_index("ctx")
    row, col = lax.axis_index("dp"), lax.axis_index("head")

    def peer_of(step):
        return lax.rem(me + step, count)

    barrier = pltpu.get_barrier_semaphore()
    for step in range(1, count):
        pl.semaphore_signal(
            barrier, inc=1, device_id=(row, peer_of(step), col), device_id_type=pl.DeviceIdType.MESH
        )
    pl.semaphore_wait(barrier, count - 1)

    copies = []
    for step in range(1, count):
        peer = peer_of(step)
        copy = pltpu.make_async_remote_copy(
            src_ref=part_ref,
            dst_ref=slots.at[me],
            send_sem=send_sem.at[peer],
            recv_sem=recv_sem.at[me],
            device_id=(row, peer, col),
            device_id_type=pl.DeviceIdType.MESH,
        )
        copy.start()
        copies.append(copy)
    slots[me] = part_ref[...]
    for step in range(1, count):
        copies[step - 1].wait_send()
        source = lax.rem(me + count - step, count)
        pltpu.make_async_remote_copy(
            src_ref=part_ref,
            dst_ref=slots.at[source],
            send_sem=send_sem.at[source],
            recv_sem=recv_sem.at[source],
            device_id=(row, source, col),
            device_id_type=pl.DeviceIdType.MESH,
        ).wait_recv()
    total = slots[0]
    for index in range(1, count):
        total = total + slots[index]
    total_ref[...] = total


def gain_sum(part, count):
    return pl.pallas_call(
        gain_sum_kernel,
        out_shape=jax.ShapeDtypeStruct(part.shape, part.dtype),
        in_specs=[pl.BlockSpec(memory_space=pltpu.VMEM)],
        out_specs=pl.BlockSpec(memory_space=pltpu.VMEM),
        scratch_shapes=[
            pltpu.VMEM((count,) + part.shape, part.dtype),
            pltpu.SemaphoreType.DMA((count,)),
            pltpu.SemaphoreType.DMA((count,)),
        ],
        compiler_params=pltpu.CompilerParams(collective_id=0, has_side_effects=True),
    )(part)


def start_flags(doc_lengths, first_pos, num_rows):
    starts = jnp.cumsum(doc_lengths, dtype=jnp.int32) - doc_lengths
    positions = first_pos + jnp.arange(num_rows, dtype=jnp.int32)
    matches = jnp.any(positions[:, None] == starts[None, :], axis=1)
    return matches.astype(jnp.float32)


def make_step(key_gain, head_width):
    q_scale = head_width ** (-0.5)

    def block_step(carried, inputs):
        q_block, k_block, v_block, gate_block, flag_block = inputs
        k_bf = (k_block.astype(jnp.float32) * key_gain[None]).astype(jnp.bfloat16)
        q_float = q_block.astype(jnp.float32) * q_scale
        k_float = lax.optimization_barrier(k_bf).astype(jnp.float32)
        v_float = v_block.astype(jnp.float32)
        segment = jnp.cumsum(flag_block)
        positions = jnp.arange(flag_block.shape[0])
        same_doc = (segment[:, None] == segment[None, :]) & (
            positions[:, None] >= positions[None, :]
        )
        cum_decay = jnp.cumsum(gate_block, axis=1)
        exponent = cum_decay[:, :, None] - cum_decay[:, None, :]
        decays = jnp.where(same_doc[None], jnp.exp(jnp.where(same_doc[None], exponent, 0.0)), 0.0)
        scores = jnp.einsum("thd,shd->hts", q_block, k_bf, preferred_element_type=jnp.float32)
        weights = (scores * q_scale * decays).astype(jnp.bfloat16)
        within = jnp.einsum("hts,she->the", weights, v_block, preferred_element_type=jnp.float32)
        opened = (segment == 0).astype(cum_decay.dtype)
        carry_in = jnp.exp(cum_decay) * opened[None, :]
        across = (
            jnp.einsum("thd,hde->the", q_float, carried, precision=PRECISE) * carry_in.T[:, :, None]
        )
        tail_mask = (segment == segment[-1]).astype(cum_decay.dtype)
        to_end = jnp.exp(cum_decay[:, -1:] - cum_decay) * tail_mask[None, :]
        written = jnp.einsum(
            "shd,she->hde", k_float * to_end.T[:, :, None], v_float, precision=PRECISE
        )
        end_state = carried * carry_in[:, -1][:, None, None] + written
        return (end_state, within + across)

    return block_step


def run_blocks(q_rows, k_rows, v_rows, gate_rows, flags, key_gain, start_state):
    num_rows = q_rows.shape[0]
    head_count = key_gain.shape[0]
    head_width = key_gain.shape[1]
    num_blocks = num_rows // BLOCK

    def to_blocks(tensor):
        return tensor.reshape(num_blocks, BLOCK, head_count, head_width)

    gate_blocks = gate_rows.reshape(head_count, num_blocks, BLOCK).transpose(1, 0, 2)
    flag_blocks = flags.reshape(num_blocks, BLOCK)
    end_state, outputs = lax.scan(
        jax.checkpoint(make_step(key_gain, head_width)),
        start_state,
        (to_blocks(q_rows), to_blocks(k_rows), to_blocks(v_rows), gate_blocks, flag_blocks),
    )
    return (outputs.reshape(num_rows, head_count * head_width), end_state)


def shards(queries, keys_raw, values, gates, lengths, key_gain, cotangent):
    tok_rows = queries.shape[1]
    head_count = key_gain.shape[0]
    head_width = key_gain.shape[1]
    flags = start_flags(lengths[0], lax.axis_index("ctx") * tok_rows, tok_rows)
    q_rows, k_rows, v_rows, gate_rows = (queries[0], keys_raw[0], values[0], gates[0])
    segment = jnp.cumsum(flags)
    opened = (segment == 0).astype(jnp.float32)
    tail_mask = (segment == segment[-1]).astype(jnp.float32)
    cum_decay = jnp.cumsum(gate_rows, axis=1)
    shard_decay = jnp.exp(cum_decay[:, -1]) * opened[-1]
    to_end = jnp.exp(cum_decay[:, -1:] - cum_decay) * tail_mask[None, :]
    k_bf = (
        k_rows.reshape(tok_rows, head_count, head_width).astype(jnp.float32) * key_gain[None]
    ).astype(jnp.bfloat16)
    k_float = lax.optimization_barrier(k_bf).astype(jnp.float32)
    v_float = v_rows.reshape(tok_rows, head_count, head_width).astype(jnp.float32)
    local_end = jnp.einsum(
        "shd,she->hde", k_float * to_end.T[:, :, None], v_float, precision=PRECISE
    )
    ctx_size = lax.axis_size("ctx")
    local_grad = local_incoming_grad(q_rows, cotangent[0], cum_decay, opened, head_count, head_width)
    state_in, later_grad = both_scans(shard_decay, local_end, local_grad, ctx_size)

    def forward(q_part, k_part, v_part, gate_part, gain_part):
        return run_blocks(q_part, k_part, v_part, gate_part, flags, gain_part, state_in)

    (primal, end_state), pullback = jax.vjp(forward, q_rows, k_rows, v_rows, gate_rows, key_gain)
    cot_float = cotangent[0].astype(jnp.float32)
    grad_q, grad_k, grad_v, grad_a, gain_term = pullback((cot_float, later_grad))
    gain_half = lax.psum_scatter(gain_term, "dp", scatter_dimension=1, tiled=True)
    grad_gain = gain_sum(gain_half, ctx_size)
    return (
        primal.astype(jnp.bfloat16)[None],
        grad_q[None],
        grad_k[None],
        grad_v[None],
        grad_a[None],
        grad_gain,
    )


def solution(mesh):
    placed = (
        P("dp", "ctx", "head"),
        P("dp", "ctx", "head"),
        P("dp", "ctx", "head"),
        P("dp", "head", "ctx"),
        P("dp", None),
        P("head", None),
        P("dp", "ctx", "head"),
    )
    return jax.shard_map(
        shards,
        mesh=mesh,
        in_specs=placed,
        out_specs=(
            P("dp", "ctx", "head"),
            P("dp", "ctx", "head"),
            P("dp", "ctx", "head"),
            P("dp", "ctx", "head"),
            P("dp", "head", "ctx"),
            P("head", "dp"),
        ),
        check_vma=False,
    )
```

```python
import jax
import jax.numpy as jnp
from jax import lax
from jax.sharding import PartitionSpec as P
from jax.experimental import pallas as pl
from jax.experimental.pallas import tpu as pltpu

BLOCK = 512


PRECISE = lax.Precision.HIGHEST


def passed_along(value, axis, steps):
    count = lax.axis_size(axis)
    first, last = (max(0, -steps), min(count, count - steps))
    return lax.ppermute(value, axis, [(source, source + steps) for source in range(first, last)])


def local_incoming_grad(q_rows, cot_rows, cum_decay, opened, head_count, head_width):
    tok_rows = q_rows.shape[0]
    factor = jnp.exp(cum_decay) * opened[None, :]
    weighted = (
        q_rows.reshape(tok_rows, head_count, head_width).astype(jnp.float32)
        * head_width ** (-0.5)
        * factor.T[:, :, None]
    )
    cot_float = cot_rows.astype(jnp.float32)
    return jnp.einsum(
        "thd,the->hde",
        weighted,
        cot_float.reshape(tok_rows, head_count, head_width),
        precision=PRECISE,
    )


def pack(decay, term):
    lane = jnp.broadcast_to(decay[:, None, None], (term.shape[0], 1, term.shape[2]))
    return jnp.concatenate([term, lane], axis=1)


def both_scans(decay, fwd_term, bwd_term, count):
    rows = fwd_term.shape[1]
    scans = []
    for term in (fwd_term, bwd_term):
        scans.append([decay, term, jnp.ones_like(decay), jnp.zeros_like(term)])
    shift = 1
    while shift < count:
        got = [
            passed_along(pack(agg_a, agg_b), "ctx", shift * sign)
            for (agg_a, agg_b, _, _), sign in zip(scans, (1, -1))
        ]
        for index, received in enumerate(got):
            agg_a, agg_b, ex_a, ex_b = scans[index]
            r_b, r_a = received[:, :rows], received[:, rows, 0]
            ex_b = ex_a[:, None, None] * r_b + ex_b
            ex_a = ex_a * r_a
            agg_b = agg_a[:, None, None] * r_b + agg_b
            agg_a = agg_a * r_a
            scans[index] = [agg_a, agg_b, ex_a, ex_b]
        shift *= 2
    return scans[0][3], scans[1][3]


def gain_sum_kernel(part_ref, total_ref, slots, send_sem, recv_sem):
    count = slots.shape[0]
    me = lax.axis_index("ctx")
    row, col = lax.axis_index("dp"), lax.axis_index("head")

    def peer_of(step):
        return lax.rem(me + step, count)

    barrier = pltpu.get_barrier_semaphore()
    for step in range(1, count):
        pl.semaphore_signal(
            barrier, inc=1, device_id=(row, peer_of(step), col), device_id_type=pl.DeviceIdType.MESH
        )
    pl.semaphore_wait(barrier, count - 1)

    copies = []
    for step in range(1, count):
        peer = peer_of(step)
        copy = pltpu.make_async_remote_copy(
            src_ref=part_ref,
            dst_ref=slots.at[me],
            send_sem=send_sem.at[peer],
            recv_sem=recv_sem.at[me],
            device_id=(row, peer, col),
            device_id_type=pl.DeviceIdType.MESH,
        )
        copy.start()
        copies.append(copy)
    slots[me] = part_ref[...]
    for step in range(1, count):
        copies[step - 1].wait_send()
        source = lax.rem(me + count - step, count)
        pltpu.make_async_remote_copy(
            src_ref=part_ref,
            dst_ref=slots.at[source],
            send_sem=send_sem.at[source],
            recv_sem=recv_sem.at[source],
            device_id=(row, source, col),
            device_id_type=pl.DeviceIdType.MESH,
        ).wait_recv()
    total = slots[0]
    for index in range(1, count):
        total = total + slots[index]
    total_ref[...] = total


def gain_sum(part, count):
    return pl.pallas_call(
        gain_sum_kernel,
        out_shape=jax.ShapeDtypeStruct(part.shape, part.dtype),
        in_specs=[pl.BlockSpec(memory_space=pltpu.VMEM)],
        out_specs=pl.BlockSpec(memory_space=pltpu.VMEM),
        scratch_shapes=[
            pltpu.VMEM((count,) + part.shape, part.dtype),
            pltpu.SemaphoreType.DMA((count,)),
            pltpu.SemaphoreType.DMA((count,)),
        ],
        compiler_params=pltpu.CompilerParams(collective_id=0, has_side_effects=True),
    )(part)


def scan_kernel(fwd_ref, bwd_ref, fwd_out, bwd_out, aggs, exs, slots, send_sem, recv_sem):
    count = lax.axis_size("ctx")
    me = lax.axis_index("ctx")
    row, col = lax.axis_index("dp"), lax.axis_index("head")
    rows = fwd_out.shape[1]
    shifts = []
    shift = 1
    while shift < count:
        shifts.append(shift)
        shift *= 2

    def device(index):
        return (row, index, col)

    barrier = pltpu.get_barrier_semaphore()
    for shift in shifts:
        for peer, present in ((me + shift, me + shift < count), (me - shift, me >= shift)):
            @pl.when(present)
            def _():
                pl.semaphore_signal(
                    barrier, inc=1, device_id=device(peer), device_id_type=pl.DeviceIdType.MESH
                )

    def at_least(bound):
        span = (count - 1) // bound + 1
        return (me // bound + span - 1) // span

    peers = 0
    for shift in shifts:
        peers = peers + at_least(shift) + 1 - at_least(count - shift)
    pl.semaphore_wait(barrier, peers)

    aggs[0] = fwd_ref[...]
    aggs[1] = bwd_ref[...]
    exs[...] = jnp.zeros_like(exs)
    exs[:, :, rows:, :] = jnp.ones_like(exs[:, :, rows:, :])

    for round_index, shift in enumerate(shifts):
        sends = (me + shift < count, me >= shift)
        targets = (me + shift, me - shift)
        sources = (me - shift, me + shift)

        def copy_of(side, peer):
            return pltpu.make_async_remote_copy(
                src_ref=aggs.at[side],
                dst_ref=slots.at[side, round_index],
                send_sem=send_sem.at[side, round_index],
                recv_sem=recv_sem.at[side, round_index],
                device_id=device(peer),
                device_id_type=pl.DeviceIdType.MESH,
            )

        for side in range(2):
            @pl.when(sends[side])
            def _():
                copy_of(side, targets[side]).start()

        for side in range(2):
            @pl.when(sends[side])
            def _():
                copy_of(side, targets[side]).wait_send()

        for side in range(2):
            @pl.when(sends[1 - side])
            def _():
                copy_of(side, sources[side]).wait_recv()
                got = slots[side, round_index]
                ex = exs[side]
                agg = aggs[side]
                ex_a = ex[:, rows:rows + 1, :]
                agg_a = agg[:, rows:rows + 1, :]
                exs[side, :, :rows, :] = ex_a * got[:, :rows, :] + ex[:, :rows, :]
                exs[side, :, rows:, :] = ex[:, rows:, :] * got[:, rows:, :]
                aggs[side, :, :rows, :] = agg_a * got[:, :rows, :] + agg[:, :rows, :]
                aggs[side, :, rows:, :] = agg[:, rows:, :] * got[:, rows:, :]

    fwd_out[...] = exs[0, :, :rows, :]
    bwd_out[...] = exs[1, :, :rows, :]


def both_scans_kernel(decay, fwd_term, bwd_term, count):
    heads, rows, width = fwd_term.shape
    rounds = max(1, (count - 1).bit_length())
    lane = jnp.broadcast_to(decay[:, None, None], (heads, 8, width))
    fwd = jnp.concatenate([fwd_term, lane], axis=1)
    bwd = jnp.concatenate([bwd_term, lane], axis=1)
    packed = fwd.shape
    out = jax.ShapeDtypeStruct(fwd_term.shape, jnp.float32)
    return pl.pallas_call(
        scan_kernel,
        out_shape=(out, out),
        in_specs=[pl.BlockSpec(memory_space=pltpu.VMEM)] * 2,
        out_specs=(pl.BlockSpec(memory_space=pltpu.VMEM),) * 2,
        scratch_shapes=[
            pltpu.VMEM((2,) + packed, jnp.float32),
            pltpu.VMEM((2,) + packed, jnp.float32),
            pltpu.VMEM((2, rounds) + packed, jnp.float32),
            pltpu.SemaphoreType.DMA((2, rounds)),
            pltpu.SemaphoreType.DMA((2, rounds)),
        ],
        compiler_params=pltpu.CompilerParams(collective_id=1, has_side_effects=True),
    )(fwd, bwd)


def start_flags(doc_lengths, first_pos, num_rows):
    starts = jnp.cumsum(doc_lengths, dtype=jnp.int32) - doc_lengths
    positions = first_pos + jnp.arange(num_rows, dtype=jnp.int32)
    matches = jnp.any(positions[:, None] == starts[None, :], axis=1)
    return matches.astype(jnp.float32)


def make_step(key_gain, head_width):
    q_scale = head_width ** (-0.5)

    def block_step(carried, inputs):
        q_block, k_block, v_block, gate_block, flag_block = inputs
        k_bf = (k_block.astype(jnp.float32) * key_gain[None]).astype(jnp.bfloat16)
        q_float = q_block.astype(jnp.float32) * q_scale
        k_float = lax.optimization_barrier(k_bf).astype(jnp.float32)
        v_float = v_block.astype(jnp.float32)
        segment = jnp.cumsum(flag_block)
        positions = jnp.arange(flag_block.shape[0])
        same_doc = (segment[:, None] == segment[None, :]) & (
            positions[:, None] >= positions[None, :]
        )
        cum_decay = jnp.cumsum(gate_block, axis=1)
        exponent = cum_decay[:, :, None] - cum_decay[:, None, :]
        decays = jnp.where(same_doc[None], jnp.exp(jnp.where(same_doc[None], exponent, 0.0)), 0.0)
        scores = jnp.einsum("thd,shd->hts", q_block, k_bf, preferred_element_type=jnp.float32)
        weights = (scores * q_scale * decays).astype(jnp.bfloat16)
        within = jnp.einsum("hts,she->the", weights, v_block, preferred_element_type=jnp.float32)
        opened = (segment == 0).astype(cum_decay.dtype)
        carry_in = jnp.exp(cum_decay) * opened[None, :]
        across = (
            jnp.einsum("thd,hde->the", q_float, carried, precision=PRECISE) * carry_in.T[:, :, None]
        )
        tail_mask = (segment == segment[-1]).astype(cum_decay.dtype)
        to_end = jnp.exp(cum_decay[:, -1:] - cum_decay) * tail_mask[None, :]
        written = jnp.einsum(
            "shd,she->hde", k_float * to_end.T[:, :, None], v_float, precision=PRECISE
        )
        end_state = carried * carry_in[:, -1][:, None, None] + written
        return (end_state, within + across)

    return block_step


def run_blocks(q_rows, k_rows, v_rows, gate_rows, flags, key_gain, start_state):
    num_rows = q_rows.shape[0]
    head_count = key_gain.shape[0]
    head_width = key_gain.shape[1]
    num_blocks = num_rows // BLOCK

    def to_blocks(tensor):
        return tensor.reshape(num_blocks, BLOCK, head_count, head_width)

    gate_blocks = gate_rows.reshape(head_count, num_blocks, BLOCK).transpose(1, 0, 2)
    flag_blocks = flags.reshape(num_blocks, BLOCK)
    end_state, outputs = lax.scan(
        jax.checkpoint(make_step(key_gain, head_width)),
        start_state,
        (to_blocks(q_rows), to_blocks(k_rows), to_blocks(v_rows), gate_blocks, flag_blocks),
    )
    return (outputs.reshape(num_rows, head_count * head_width), end_state)


def shards(queries, keys_raw, values, gates, lengths, key_gain, cotangent):
    tok_rows = queries.shape[1]
    head_count = key_gain.shape[0]
    head_width = key_gain.shape[1]
    flags = start_flags(lengths[0], lax.axis_index("ctx") * tok_rows, tok_rows)
    q_rows, k_rows, v_rows, gate_rows = (queries[0], keys_raw[0], values[0], gates[0])
    segment = jnp.cumsum(flags)
    opened = (segment == 0).astype(jnp.float32)
    tail_mask = (segment == segment[-1]).astype(jnp.float32)
    cum_decay = jnp.cumsum(gate_rows, axis=1)
    shard_decay = jnp.exp(cum_decay[:, -1]) * opened[-1]
    to_end = jnp.exp(cum_decay[:, -1:] - cum_decay) * tail_mask[None, :]
    k_bf = (
        k_rows.reshape(tok_rows, head_count, head_width).astype(jnp.float32) * key_gain[None]
    ).astype(jnp.bfloat16)
    k_float = lax.optimization_barrier(k_bf).astype(jnp.float32)
    v_float = v_rows.reshape(tok_rows, head_count, head_width).astype(jnp.float32)
    local_end = jnp.einsum(
        "shd,she->hde", k_float * to_end.T[:, :, None], v_float, precision=PRECISE
    )
    ctx_size = lax.axis_size("ctx")
    local_grad = local_incoming_grad(q_rows, cotangent[0], cum_decay, opened, head_count, head_width)
    state_in, later_grad = both_scans_kernel(shard_decay, local_end, local_grad, ctx_size)

    def forward(q_part, k_part, v_part, gate_part, gain_part):
        return run_blocks(q_part, k_part, v_part, gate_part, flags, gain_part, state_in)

    (primal, end_state), pullback = jax.vjp(forward, q_rows, k_rows, v_rows, gate_rows, key_gain)
    cot_float = cotangent[0].astype(jnp.float32)
    grad_q, grad_k, grad_v, grad_a, gain_term = pullback((cot_float, later_grad))
    gain_half = lax.psum_scatter(gain_term, "dp", scatter_dimension=1, tiled=True)
    grad_gain = gain_sum(gain_half, ctx_size)
    return (
        primal.astype(jnp.bfloat16)[None],
        grad_q[None],
        grad_k[None],
        grad_v[None],
        grad_a[None],
        grad_gain,
    )


def solution(mesh):
    placed = (
        P("dp", "ctx", "head"),
        P("dp", "ctx", "head"),
        P("dp", "ctx", "head"),
        P("dp", "head", "ctx"),
        P("dp", None),
        P("head", None),
        P("dp", "ctx", "head"),
    )
    return jax.shard_map(
        shards,
        mesh=mesh,
        in_specs=placed,
        out_specs=(
            P("dp", "ctx", "head"),
            P("dp", "ctx", "head"),
            P("dp", "ctx", "head"),
            P("dp", "ctx", "head"),
            P("dp", "head", "ctx"),
            P("head", "dp"),
        ),
        check_vma=False,
    )
```

```python
import jax
import jax.numpy as jnp
from jax import lax
from jax.sharding import PartitionSpec as P
from jax.experimental import pallas as pl
from jax.experimental.pallas import tpu as pltpu

BLOCK = 512


PRECISE = lax.Precision.HIGHEST


def passed_along(value, axis, steps):
    count = lax.axis_size(axis)
    first, last = (max(0, -steps), min(count, count - steps))
    return lax.ppermute(value, axis, [(source, source + steps) for source in range(first, last)])


def local_incoming_grad(q_rows, cot_rows, cum_decay, opened, head_count, head_width):
    tok_rows = q_rows.shape[0]
    factor = jnp.exp(cum_decay) * opened[None, :]
    weighted = (
        q_rows.reshape(tok_rows, head_count, head_width).astype(jnp.float32)
        * head_width ** (-0.5)
        * factor.T[:, :, None]
    )
    cot_float = cot_rows.astype(jnp.float32)
    return jnp.einsum(
        "thd,the->hde",
        weighted,
        cot_float.reshape(tok_rows, head_count, head_width),
        precision=PRECISE,
    )


def pack(decay, term):
    lane = jnp.broadcast_to(decay[:, None, None], (term.shape[0], 1, term.shape[2]))
    return jnp.concatenate([term, lane], axis=1)


def both_scans(decay, fwd_term, bwd_term, count):
    rows = fwd_term.shape[1]
    scans = []
    for term in (fwd_term, bwd_term):
        scans.append([decay, term, jnp.ones_like(decay), jnp.zeros_like(term)])
    shift = 1
    while shift < count:
        got = [
            passed_along(pack(agg_a, agg_b), "ctx", shift * sign)
            for (agg_a, agg_b, _, _), sign in zip(scans, (1, -1))
        ]
        for index, received in enumerate(got):
            agg_a, agg_b, ex_a, ex_b = scans[index]
            r_b, r_a = received[:, :rows], received[:, rows, 0]
            ex_b = ex_a[:, None, None] * r_b + ex_b
            ex_a = ex_a * r_a
            agg_b = agg_a[:, None, None] * r_b + agg_b
            agg_a = agg_a * r_a
            scans[index] = [agg_a, agg_b, ex_a, ex_b]
        shift *= 2
    return scans[0][3], scans[1][3]


def gain_sum_kernel(part_ref, total_ref, slots, send_sem, recv_sem):
    count = slots.shape[0]
    me = lax.axis_index("ctx")
    row, col = lax.axis_index("dp"), lax.axis_index("head")

    def peer_of(step):
        return lax.rem(me + step, count)

    barrier = pltpu.get_barrier_semaphore()
    for step in range(1, count):
        pl.semaphore_signal(
            barrier, inc=1, device_id=(row, peer_of(step), col), device_id_type=pl.DeviceIdType.MESH
        )
    pl.semaphore_wait(barrier, count - 1)

    copies = []
    for step in range(1, count):
        peer = peer_of(step)
        copy = pltpu.make_async_remote_copy(
            src_ref=part_ref,
            dst_ref=slots.at[me],
            send_sem=send_sem.at[peer],
            recv_sem=recv_sem.at[me],
            device_id=(row, peer, col),
            device_id_type=pl.DeviceIdType.MESH,
        )
        copy.start()
        copies.append(copy)
    slots[me] = part_ref[...]
    for step in range(1, count):
        copies[step - 1].wait_send()
        source = lax.rem(me + count - step, count)
        pltpu.make_async_remote_copy(
            src_ref=part_ref,
            dst_ref=slots.at[source],
            send_sem=send_sem.at[source],
            recv_sem=recv_sem.at[source],
            device_id=(row, source, col),
            device_id_type=pl.DeviceIdType.MESH,
        ).wait_recv()
    total = slots[0]
    for index in range(1, count):
        total = total + slots[index]
    total_ref[...] = total


def gain_sum(part, count):
    return pl.pallas_call(
        gain_sum_kernel,
        out_shape=jax.ShapeDtypeStruct(part.shape, part.dtype),
        in_specs=[pl.BlockSpec(memory_space=pltpu.VMEM)],
        out_specs=pl.BlockSpec(memory_space=pltpu.VMEM),
        scratch_shapes=[
            pltpu.VMEM((count,) + part.shape, part.dtype),
            pltpu.SemaphoreType.DMA((count,)),
            pltpu.SemaphoreType.DMA((count,)),
        ],
        compiler_params=pltpu.CompilerParams(collective_id=0, has_side_effects=True),
    )(part)


def scan_kernel(fwd_ref, bwd_ref, fwd_out, bwd_out, aggs, exs, slots, send_sem, recv_sem):
    count = lax.axis_size("ctx")
    me = lax.axis_index("ctx")
    row, col = lax.axis_index("dp"), lax.axis_index("head")
    rows = fwd_out.shape[1]
    shifts = []
    shift = 1
    while shift < count:
        shifts.append(shift)
        shift *= 2

    def device(index):
        return (row, index, col)

    barrier = pltpu.get_barrier_semaphore()
    for shift in shifts:
        for peer, present in ((me + shift, me + shift < count), (me - shift, me >= shift)):
            @pl.when(present)
            def _():
                pl.semaphore_signal(
                    barrier, inc=1, device_id=device(peer), device_id_type=pl.DeviceIdType.MESH
                )

    def at_least(bound):
        span = (count - 1) // bound + 1
        return (me // bound + span - 1) // span

    peers = 0
    for shift in shifts:
        peers = peers + at_least(shift) + 1 - at_least(count - shift)
    pl.semaphore_wait(barrier, peers)

    aggs[0] = fwd_ref[...]
    aggs[1] = bwd_ref[...]
    exs[...] = jnp.zeros_like(exs)
    exs[:, :, rows:, :] = jnp.ones_like(exs[:, :, rows:, :])

    for round_index, shift in enumerate(shifts):
        sends = (me + shift < count, me >= shift)
        targets = (me + shift, me - shift)
        sources = (me - shift, me + shift)

        def copy_of(side, peer):
            return pltpu.make_async_remote_copy(
                src_ref=aggs.at[side],
                dst_ref=slots.at[side, round_index],
                send_sem=send_sem.at[side, round_index],
                recv_sem=recv_sem.at[side, round_index],
                device_id=device(peer),
                device_id_type=pl.DeviceIdType.MESH,
            )

        for side in range(2):
            @pl.when(sends[side])
            def _():
                copy_of(side, targets[side]).start()

        for side in range(2):
            @pl.when(sends[side])
            def _():
                copy_of(side, targets[side]).wait_send()

        for side in range(2):
            @pl.when(sends[1 - side])
            def _():
                copy_of(side, sources[side]).wait_recv()
                got = slots[side, round_index]
                ex = exs[side]
                agg = aggs[side]
                ex_a = ex[:, rows:rows + 1, :]
                agg_a = agg[:, rows:rows + 1, :]
                exs[side, :, :rows, :] = ex_a * got[:, :rows, :] + ex[:, :rows, :]
                exs[side, :, rows:, :] = ex[:, rows:, :] * got[:, rows:, :]
                aggs[side, :, :rows, :] = agg_a * got[:, :rows, :] + agg[:, :rows, :]
                aggs[side, :, rows:, :] = agg[:, rows:, :] * got[:, rows:, :]

    fwd_out[...] = exs[0, :, :rows, :]
    bwd_out[...] = exs[1, :, :rows, :]


def both_scans_kernel(decay, fwd_term, bwd_term, count):
    heads, rows, width = fwd_term.shape
    rounds = max(1, (count - 1).bit_length())
    lane = jnp.broadcast_to(decay[:, None, None], (heads, 8, width))
    fwd = jnp.concatenate([fwd_term, lane], axis=1)
    bwd = jnp.concatenate([bwd_term, lane], axis=1)
    packed = fwd.shape
    out = jax.ShapeDtypeStruct(fwd_term.shape, jnp.float32)
    return pl.pallas_call(
        scan_kernel,
        out_shape=(out, out),
        in_specs=[pl.BlockSpec(memory_space=pltpu.VMEM)] * 2,
        out_specs=(pl.BlockSpec(memory_space=pltpu.VMEM),) * 2,
        scratch_shapes=[
            pltpu.VMEM((2,) + packed, jnp.float32),
            pltpu.VMEM((2,) + packed, jnp.float32),
            pltpu.VMEM((2, rounds) + packed, jnp.float32),
            pltpu.SemaphoreType.DMA((2, rounds)),
            pltpu.SemaphoreType.DMA((2, rounds)),
        ],
        compiler_params=pltpu.CompilerParams(collective_id=1, has_side_effects=True),
    )(fwd, bwd)


def start_flags(doc_lengths, first_pos, num_rows):
    starts = jnp.cumsum(doc_lengths, dtype=jnp.int32) - doc_lengths
    positions = first_pos + jnp.arange(num_rows, dtype=jnp.int32)
    matches = jnp.any(positions[:, None] == starts[None, :], axis=1)
    return matches.astype(jnp.float32)


def make_step(key_gain, head_width):
    q_scale = head_width ** (-0.5)

    def block_step(carried, inputs):
        q_block, k_block, v_block, gate_block, flag_block = inputs
        k_bf = (k_block.astype(jnp.float32) * key_gain[None]).astype(jnp.bfloat16)
        q_float = q_block.astype(jnp.float32) * q_scale
        k_float = lax.optimization_barrier(k_bf).astype(jnp.float32)
        v_float = v_block.astype(jnp.float32)
        segment = jnp.cumsum(flag_block)
        positions = jnp.arange(flag_block.shape[0])
        same_doc = (segment[:, None] == segment[None, :]) & (
            positions[:, None] >= positions[None, :]
        )
        cum_decay = jnp.cumsum(gate_block, axis=1)
        exponent = cum_decay[:, :, None] - cum_decay[:, None, :]
        decays = jnp.where(same_doc[None], jnp.exp(jnp.where(same_doc[None], exponent, 0.0)), 0.0)
        scores = jnp.einsum("thd,shd->hts", q_block, k_bf, preferred_element_type=jnp.float32)
        weights = (scores * q_scale * decays).astype(jnp.bfloat16)
        within = jnp.einsum("hts,she->the", weights, v_block, preferred_element_type=jnp.float32)
        opened = (segment == 0).astype(cum_decay.dtype)
        carry_in = jnp.exp(cum_decay) * opened[None, :]
        across = (
            jnp.einsum("thd,hde->the", q_float, carried, precision=PRECISE) * carry_in.T[:, :, None]
        )
        tail_mask = (segment == segment[-1]).astype(cum_decay.dtype)
        to_end = jnp.exp(cum_decay[:, -1:] - cum_decay) * tail_mask[None, :]
        written = jnp.einsum(
            "shd,she->hde", k_float * to_end.T[:, :, None], v_float, precision=PRECISE
        )
        end_state = carried * carry_in[:, -1][:, None, None] + written
        return (end_state, within + across)

    return block_step


def run_blocks(q_rows, k_rows, v_rows, gate_rows, flags, key_gain, start_state):
    num_rows = q_rows.shape[0]
    head_count = key_gain.shape[0]
    head_width = key_gain.shape[1]
    num_blocks = num_rows // BLOCK

    def to_blocks(tensor):
        return tensor.reshape(num_blocks, BLOCK, head_count, head_width)

    gate_blocks = gate_rows.reshape(head_count, num_blocks, BLOCK).transpose(1, 0, 2)
    flag_blocks = flags.reshape(num_blocks, BLOCK)
    end_state, outputs = lax.scan(
        make_step(key_gain, head_width),
        start_state,
        (to_blocks(q_rows), to_blocks(k_rows), to_blocks(v_rows), gate_blocks, flag_blocks),
    )
    return (outputs.reshape(num_rows, head_count * head_width), end_state)


def shards(queries, keys_raw, values, gates, lengths, key_gain, cotangent):
    tok_rows = queries.shape[1]
    head_count = key_gain.shape[0]
    head_width = key_gain.shape[1]
    flags = start_flags(lengths[0], lax.axis_index("ctx") * tok_rows, tok_rows)
    q_rows, k_rows, v_rows, gate_rows = (queries[0], keys_raw[0], values[0], gates[0])
    segment = jnp.cumsum(flags)
    opened = (segment == 0).astype(jnp.float32)
    tail_mask = (segment == segment[-1]).astype(jnp.float32)
    cum_decay = jnp.cumsum(gate_rows, axis=1)
    shard_decay = jnp.exp(cum_decay[:, -1]) * opened[-1]
    to_end = jnp.exp(cum_decay[:, -1:] - cum_decay) * tail_mask[None, :]
    k_bf = (
        k_rows.reshape(tok_rows, head_count, head_width).astype(jnp.float32) * key_gain[None]
    ).astype(jnp.bfloat16)
    k_float = lax.optimization_barrier(k_bf).astype(jnp.float32)
    v_float = v_rows.reshape(tok_rows, head_count, head_width).astype(jnp.float32)
    local_end = jnp.einsum(
        "shd,she->hde", k_float * to_end.T[:, :, None], v_float, precision=PRECISE
    )
    ctx_size = lax.axis_size("ctx")
    local_grad = local_incoming_grad(q_rows, cotangent[0], cum_decay, opened, head_count, head_width)
    state_in, later_grad = both_scans_kernel(shard_decay, local_end, local_grad, ctx_size)

    def forward(q_part, k_part, v_part, gate_part, gain_part):
        return run_blocks(q_part, k_part, v_part, gate_part, flags, gain_part, state_in)

    (primal, end_state), pullback = jax.vjp(forward, q_rows, k_rows, v_rows, gate_rows, key_gain)
    cot_float = cotangent[0].astype(jnp.float32)
    grad_q, grad_k, grad_v, grad_a, gain_term = pullback((cot_float, later_grad))
    gain_half = lax.psum_scatter(gain_term, "dp", scatter_dimension=1, tiled=True)
    grad_gain = gain_sum(gain_half, ctx_size)
    return (
        primal.astype(jnp.bfloat16)[None],
        grad_q[None],
        grad_k[None],
        grad_v[None],
        grad_a[None],
        grad_gain,
    )


def solution(mesh):
    placed = (
        P("dp", "ctx", "head"),
        P("dp", "ctx", "head"),
        P("dp", "ctx", "head"),
        P("dp", "head", "ctx"),
        P("dp", None),
        P("head", None),
        P("dp", "ctx", "head"),
    )
    return jax.shard_map(
        shards,
        mesh=mesh,
        in_specs=placed,
        out_specs=(
            P("dp", "ctx", "head"),
            P("dp", "ctx", "head"),
            P("dp", "ctx", "head"),
            P("dp", "ctx", "head"),
            P("dp", "head", "ctx"),
            P("head", "dp"),
        ),
        check_vma=False,
    )
```

```python
import jax
import jax.numpy as jnp
from jax import lax
from jax.sharding import PartitionSpec as P
from jax.experimental import pallas as pl
from jax.experimental.pallas import tpu as pltpu

BLOCK = 512


PRECISE = lax.Precision.HIGHEST


def passed_along(value, axis, steps):
    count = lax.axis_size(axis)
    first, last = (max(0, -steps), min(count, count - steps))
    return lax.ppermute(value, axis, [(source, source + steps) for source in range(first, last)])


def local_incoming_grad(q_rows, cot_rows, cum_decay, opened, head_count, head_width):
    tok_rows = q_rows.shape[0]
    factor = jnp.exp(cum_decay) * opened[None, :]
    weighted = (
        q_rows.reshape(tok_rows, head_count, head_width).astype(jnp.float32)
        * head_width ** (-0.5)
        * factor.T[:, :, None]
    )
    cot_float = cot_rows.astype(jnp.float32)
    return jnp.einsum(
        "thd,the->hde",
        weighted,
        cot_float.reshape(tok_rows, head_count, head_width),
        precision=PRECISE,
    )


def pack(decay, term):
    lane = jnp.broadcast_to(decay[:, None, None], (term.shape[0], 1, term.shape[2]))
    return jnp.concatenate([term, lane], axis=1)


def both_scans(decay, fwd_term, bwd_term, count):
    rows = fwd_term.shape[1]
    scans = []
    for term in (fwd_term, bwd_term):
        scans.append([decay, term, jnp.ones_like(decay), jnp.zeros_like(term)])
    shift = 1
    while shift < count:
        got = [
            passed_along(pack(agg_a, agg_b), "ctx", shift * sign)
            for (agg_a, agg_b, _, _), sign in zip(scans, (1, -1))
        ]
        for index, received in enumerate(got):
            agg_a, agg_b, ex_a, ex_b = scans[index]
            r_b, r_a = received[:, :rows], received[:, rows, 0]
            ex_b = ex_a[:, None, None] * r_b + ex_b
            ex_a = ex_a * r_a
            agg_b = agg_a[:, None, None] * r_b + agg_b
            agg_a = agg_a * r_a
            scans[index] = [agg_a, agg_b, ex_a, ex_b]
        shift *= 2
    return scans[0][3], scans[1][3]


def gain_sum_kernel(part_ref, total_ref, pair_slot, slots, pair_sem, send_sem, recv_sem):
    count = slots.shape[0]
    me = lax.axis_index("ctx")
    row, col = lax.axis_index("dp"), lax.axis_index("head")
    other = 1 - row

    def peer_of(step):
        return lax.rem(me + step, count)

    barrier = pltpu.get_barrier_semaphore()
    pl.semaphore_signal(
        barrier, inc=1, device_id=(other, me, col), device_id_type=pl.DeviceIdType.MESH
    )
    for step in range(1, count):
        pl.semaphore_signal(
            barrier, inc=1, device_id=(row, peer_of(step), col), device_id_type=pl.DeviceIdType.MESH
        )
    pl.semaphore_wait(barrier, count)

    pair = pltpu.make_async_remote_copy(
        src_ref=part_ref.at[other],
        dst_ref=pair_slot,
        send_sem=pair_sem.at[0],
        recv_sem=pair_sem.at[1],
        device_id=(other, me, col),
        device_id_type=pl.DeviceIdType.MESH,
    )
    pair.start()
    pair.wait_send()
    pair.wait_recv()
    slots[me] = part_ref[row] + pair_slot[...]

    copies = []
    for step in range(1, count):
        peer = peer_of(step)
        copy = pltpu.make_async_remote_copy(
            src_ref=slots.at[me],
            dst_ref=slots.at[me],
            send_sem=send_sem.at[peer],
            recv_sem=recv_sem.at[me],
            device_id=(row, peer, col),
            device_id_type=pl.DeviceIdType.MESH,
        )
        copy.start()
        copies.append(copy)
    for step in range(1, count):
        copies[step - 1].wait_send()
        source = lax.rem(me + count - step, count)
        pltpu.make_async_remote_copy(
            src_ref=slots.at[source],
            dst_ref=slots.at[source],
            send_sem=send_sem.at[source],
            recv_sem=recv_sem.at[source],
            device_id=(row, source, col),
            device_id_type=pl.DeviceIdType.MESH,
        ).wait_recv()
    total = slots[0]
    for index in range(1, count):
        total = total + slots[index]
    total_ref[...] = total


def gain_sum(part, count):
    heads, width = part.shape
    halves = part.reshape(heads, 2, width // 2).transpose(1, 0, 2)
    shape = halves.shape[1:]
    return pl.pallas_call(
        gain_sum_kernel,
        out_shape=jax.ShapeDtypeStruct(shape, part.dtype),
        in_specs=[pl.BlockSpec(memory_space=pltpu.VMEM)],
        out_specs=pl.BlockSpec(memory_space=pltpu.VMEM),
        scratch_shapes=[
            pltpu.VMEM(shape, part.dtype),
            pltpu.VMEM((count,) + shape, part.dtype),
            pltpu.SemaphoreType.DMA((2,)),
            pltpu.SemaphoreType.DMA((count,)),
            pltpu.SemaphoreType.DMA((count,)),
        ],
        compiler_params=pltpu.CompilerParams(collective_id=0, has_side_effects=True),
    )(halves)


def scan_kernel(fwd_ref, bwd_ref, fwd_out, bwd_out, aggs, exs, slots, send_sem, recv_sem):
    count = lax.axis_size("ctx")
    me = lax.axis_index("ctx")
    row, col = lax.axis_index("dp"), lax.axis_index("head")
    rows = fwd_out.shape[1]
    shifts = []
    shift = 1
    while shift < count:
        shifts.append(shift)
        shift *= 2

    def device(index):
        return (row, index, col)

    barrier = pltpu.get_barrier_semaphore()
    for shift in shifts:
        for peer, present in ((me + shift, me + shift < count), (me - shift, me >= shift)):
            @pl.when(present)
            def _():
                pl.semaphore_signal(
                    barrier, inc=1, device_id=device(peer), device_id_type=pl.DeviceIdType.MESH
                )

    def at_least(bound):
        span = (count - 1) // bound + 1
        return (me // bound + span - 1) // span

    peers = 0
    for shift in shifts:
        peers = peers + at_least(shift) + 1 - at_least(count - shift)
    pl.semaphore_wait(barrier, peers)

    aggs[0] = fwd_ref[...]
    aggs[1] = bwd_ref[...]
    exs[...] = jnp.zeros_like(exs)
    exs[:, :, rows:, :] = jnp.ones_like(exs[:, :, rows:, :])

    for round_index, shift in enumerate(shifts):
        sends = (me + shift < count, me >= shift)
        targets = (me + shift, me - shift)
        sources = (me - shift, me + shift)

        def copy_of(side, peer):
            return pltpu.make_async_remote_copy(
                src_ref=aggs.at[side],
                dst_ref=slots.at[side, round_index],
                send_sem=send_sem.at[side, round_index],
                recv_sem=recv_sem.at[side, round_index],
                device_id=device(peer),
                device_id_type=pl.DeviceIdType.MESH,
            )

        for side in range(2):
            @pl.when(sends[side])
            def _():
                copy_of(side, targets[side]).start()

        for side in range(2):
            @pl.when(sends[side])
            def _():
                copy_of(side, targets[side]).wait_send()

        for side in range(2):
            @pl.when(sends[1 - side])
            def _():
                copy_of(side, sources[side]).wait_recv()
                got = slots[side, round_index]
                ex = exs[side]
                agg = aggs[side]
                ex_a = ex[:, rows:rows + 1, :]
                agg_a = agg[:, rows:rows + 1, :]
                exs[side, :, :rows, :] = ex_a * got[:, :rows, :] + ex[:, :rows, :]
                exs[side, :, rows:, :] = ex[:, rows:, :] * got[:, rows:, :]
                aggs[side, :, :rows, :] = agg_a * got[:, :rows, :] + agg[:, :rows, :]
                aggs[side, :, rows:, :] = agg[:, rows:, :] * got[:, rows:, :]

    fwd_out[...] = exs[0, :, :rows, :]
    bwd_out[...] = exs[1, :, :rows, :]


def both_scans_kernel(decay, fwd_term, bwd_term, count):
    heads, rows, width = fwd_term.shape
    rounds = max(1, (count - 1).bit_length())
    lane = jnp.broadcast_to(decay[:, None, None], (heads, 8, width))
    fwd = jnp.concatenate([fwd_term, lane], axis=1)
    bwd = jnp.concatenate([bwd_term, lane], axis=1)
    packed = fwd.shape
    out = jax.ShapeDtypeStruct(fwd_term.shape, jnp.float32)
    return pl.pallas_call(
        scan_kernel,
        out_shape=(out, out),
        in_specs=[pl.BlockSpec(memory_space=pltpu.VMEM)] * 2,
        out_specs=(pl.BlockSpec(memory_space=pltpu.VMEM),) * 2,
        scratch_shapes=[
            pltpu.VMEM((2,) + packed, jnp.float32),
            pltpu.VMEM((2,) + packed, jnp.float32),
            pltpu.VMEM((2, rounds) + packed, jnp.float32),
            pltpu.SemaphoreType.DMA((2, rounds)),
            pltpu.SemaphoreType.DMA((2, rounds)),
        ],
        compiler_params=pltpu.CompilerParams(collective_id=1, has_side_effects=True),
    )(fwd, bwd)


def start_flags(doc_lengths, first_pos, num_rows):
    starts = jnp.cumsum(doc_lengths, dtype=jnp.int32) - doc_lengths
    positions = first_pos + jnp.arange(num_rows, dtype=jnp.int32)
    matches = jnp.any(positions[:, None] == starts[None, :], axis=1)
    return matches.astype(jnp.float32)


def make_step(key_gain, head_width):
    q_scale = head_width ** (-0.5)

    def block_step(carried, inputs):
        q_block, k_block, v_block, gate_block, flag_block = inputs
        k_bf = (k_block.astype(jnp.float32) * key_gain[None]).astype(jnp.bfloat16)
        q_float = q_block.astype(jnp.float32) * q_scale
        k_float = lax.optimization_barrier(k_bf).astype(jnp.float32)
        v_float = v_block.astype(jnp.float32)
        segment = jnp.cumsum(flag_block)
        positions = jnp.arange(flag_block.shape[0])
        same_doc = (segment[:, None] == segment[None, :]) & (
            positions[:, None] >= positions[None, :]
        )
        cum_decay = jnp.cumsum(gate_block, axis=1)
        exponent = cum_decay[:, :, None] - cum_decay[:, None, :]
        decays = jnp.where(same_doc[None], jnp.exp(jnp.where(same_doc[None], exponent, 0.0)), 0.0)
        scores = jnp.einsum("thd,shd->hts", q_block, k_bf, preferred_element_type=jnp.float32)
        weights = (scores * q_scale * decays).astype(jnp.bfloat16)
        within = jnp.einsum("hts,she->the", weights, v_block, preferred_element_type=jnp.float32)
        opened = (segment == 0).astype(cum_decay.dtype)
        carry_in = jnp.exp(cum_decay) * opened[None, :]
        across = (
            jnp.einsum("thd,hde->the", q_float, carried, precision=PRECISE) * carry_in.T[:, :, None]
        )
        tail_mask = (segment == segment[-1]).astype(cum_decay.dtype)
        to_end = jnp.exp(cum_decay[:, -1:] - cum_decay) * tail_mask[None, :]
        written = jnp.einsum(
            "shd,she->hde", k_float * to_end.T[:, :, None], v_float, precision=PRECISE
        )
        end_state = carried * carry_in[:, -1][:, None, None] + written
        return (end_state, within + across)

    return block_step


def run_blocks(q_rows, k_rows, v_rows, gate_rows, flags, key_gain, start_state):
    num_rows = q_rows.shape[0]
    head_count = key_gain.shape[0]
    head_width = key_gain.shape[1]
    num_blocks = num_rows // BLOCK

    def to_blocks(tensor):
        return tensor.reshape(num_blocks, BLOCK, head_count, head_width)

    gate_blocks = gate_rows.reshape(head_count, num_blocks, BLOCK).transpose(1, 0, 2)
    flag_blocks = flags.reshape(num_blocks, BLOCK)
    end_state, outputs = lax.scan(
        jax.checkpoint(make_step(key_gain, head_width)),
        start_state,
        (to_blocks(q_rows), to_blocks(k_rows), to_blocks(v_rows), gate_blocks, flag_blocks),
    )
    return (outputs.reshape(num_rows, head_count * head_width), end_state)


def shards(queries, keys_raw, values, gates, lengths, key_gain, cotangent):
    tok_rows = queries.shape[1]
    head_count = key_gain.shape[0]
    head_width = key_gain.shape[1]
    flags = start_flags(lengths[0], lax.axis_index("ctx") * tok_rows, tok_rows)
    q_rows, k_rows, v_rows, gate_rows = (queries[0], keys_raw[0], values[0], gates[0])
    segment = jnp.cumsum(flags)
    opened = (segment == 0).astype(jnp.float32)
    tail_mask = (segment == segment[-1]).astype(jnp.float32)
    cum_decay = jnp.cumsum(gate_rows, axis=1)
    shard_decay = jnp.exp(cum_decay[:, -1]) * opened[-1]
    to_end = jnp.exp(cum_decay[:, -1:] - cum_decay) * tail_mask[None, :]
    k_bf = (
        k_rows.reshape(tok_rows, head_count, head_width).astype(jnp.float32) * key_gain[None]
    ).astype(jnp.bfloat16)
    k_float = lax.optimization_barrier(k_bf).astype(jnp.float32)
    v_float = v_rows.reshape(tok_rows, head_count, head_width).astype(jnp.float32)
    local_end = jnp.einsum(
        "shd,she->hde", k_float * to_end.T[:, :, None], v_float, precision=PRECISE
    )
    ctx_size = lax.axis_size("ctx")
    local_grad = local_incoming_grad(q_rows, cotangent[0], cum_decay, opened, head_count, head_width)
    state_in, later_grad = both_scans_kernel(shard_decay, local_end, local_grad, ctx_size)

    def forward(q_part, k_part, v_part, gate_part, gain_part):
        return run_blocks(q_part, k_part, v_part, gate_part, flags, gain_part, state_in)

    (primal, end_state), pullback = jax.vjp(forward, q_rows, k_rows, v_rows, gate_rows, key_gain)
    cot_float = cotangent[0].astype(jnp.float32)
    grad_q, grad_k, grad_v, grad_a, gain_term = pullback((cot_float, later_grad))
    grad_gain = gain_sum(gain_term, ctx_size)
    return (
        primal.astype(jnp.bfloat16)[None],
        grad_q[None],
        grad_k[None],
        grad_v[None],
        grad_a[None],
        grad_gain,
    )


def solution(mesh):
    placed = (
        P("dp", "ctx", "head"),
        P("dp", "ctx", "head"),
        P("dp", "ctx", "head"),
        P("dp", "head", "ctx"),
        P("dp", None),
        P("head", None),
        P("dp", "ctx", "head"),
    )
    return jax.shard_map(
        shards,
        mesh=mesh,
        in_specs=placed,
        out_specs=(
            P("dp", "ctx", "head"),
            P("dp", "ctx", "head"),
            P("dp", "ctx", "head"),
            P("dp", "ctx", "head"),
            P("dp", "head", "ctx"),
            P("head", "dp"),
        ),
        check_vma=False,
    )
```

```python
import jax
import jax.numpy as jnp
from jax import lax
from jax.sharding import PartitionSpec as P
from jax.experimental import pallas as pl
from jax.experimental.pallas import tpu as pltpu

BLOCK = 512


PRECISE = lax.Precision.HIGHEST


def passed_along(value, axis, steps):
    count = lax.axis_size(axis)
    first, last = (max(0, -steps), min(count, count - steps))
    return lax.ppermute(value, axis, [(source, source + steps) for source in range(first, last)])


def local_incoming_grad(q_rows, cot_rows, cum_decay, opened, head_count, head_width):
    tok_rows = q_rows.shape[0]
    factor = jnp.exp(cum_decay) * opened[None, :]
    weighted = (
        q_rows.reshape(tok_rows, head_count, head_width).astype(jnp.float32)
        * head_width ** (-0.5)
        * factor.T[:, :, None]
    )
    cot_float = cot_rows.astype(jnp.float32)
    return jnp.einsum(
        "thd,the->hde",
        weighted,
        cot_float.reshape(tok_rows, head_count, head_width),
        precision=PRECISE,
    )


def pack(decay, term):
    lane = jnp.broadcast_to(decay[:, None, None], (term.shape[0], 1, term.shape[2]))
    return jnp.concatenate([term, lane], axis=1)


def both_scans(decay, fwd_term, bwd_term, count):
    rows = fwd_term.shape[1]
    scans = []
    for term in (fwd_term, bwd_term):
        scans.append([decay, term, jnp.ones_like(decay), jnp.zeros_like(term)])
    shift = 1
    while shift < count:
        got = [
            passed_along(pack(agg_a, agg_b), "ctx", shift * sign)
            for (agg_a, agg_b, _, _), sign in zip(scans, (1, -1))
        ]
        for index, received in enumerate(got):
            agg_a, agg_b, ex_a, ex_b = scans[index]
            r_b, r_a = received[:, :rows], received[:, rows, 0]
            ex_b = ex_a[:, None, None] * r_b + ex_b
            ex_a = ex_a * r_a
            agg_b = agg_a[:, None, None] * r_b + agg_b
            agg_a = agg_a * r_a
            scans[index] = [agg_a, agg_b, ex_a, ex_b]
        shift *= 2
    return scans[0][3], scans[1][3]


def gain_sum_kernel(part_ref, total_ref, pair_slot, slots, pair_sem, send_sem, recv_sem):
    count = slots.shape[0]
    me = lax.axis_index("ctx")
    row, col = lax.axis_index("dp"), lax.axis_index("head")
    other = 1 - row

    def peer_of(step):
        return lax.rem(me + step, count)

    barrier = pltpu.get_barrier_semaphore()
    pl.semaphore_signal(
        barrier, inc=1, device_id=(other, me, col), device_id_type=pl.DeviceIdType.MESH
    )
    for step in range(1, count):
        pl.semaphore_signal(
            barrier, inc=1, device_id=(row, peer_of(step), col), device_id_type=pl.DeviceIdType.MESH
        )
    pl.semaphore_wait(barrier, count)

    pair = pltpu.make_async_remote_copy(
        src_ref=part_ref.at[other],
        dst_ref=pair_slot,
        send_sem=pair_sem.at[0],
        recv_sem=pair_sem.at[1],
        device_id=(other, me, col),
        device_id_type=pl.DeviceIdType.MESH,
    )
    pair.start()
    pair.wait_send()
    pair.wait_recv()
    slots[me] = part_ref[row] + pair_slot[...]

    copies = []
    for step in range(1, count):
        peer = peer_of(step)
        copy = pltpu.make_async_remote_copy(
            src_ref=slots.at[me],
            dst_ref=slots.at[me],
            send_sem=send_sem.at[peer],
            recv_sem=recv_sem.at[me],
            device_id=(row, peer, col),
            device_id_type=pl.DeviceIdType.MESH,
        )
        copy.start()
        copies.append(copy)
    for step in range(1, count):
        copies[step - 1].wait_send()
        source = lax.rem(me + count - step, count)
        pltpu.make_async_remote_copy(
            src_ref=slots.at[source],
            dst_ref=slots.at[source],
            send_sem=send_sem.at[source],
            recv_sem=recv_sem.at[source],
            device_id=(row, source, col),
            device_id_type=pl.DeviceIdType.MESH,
        ).wait_recv()
    total = slots[0]
    for index in range(1, count):
        total = total + slots[index]
    total_ref[...] = total


def gain_sum(part, count):
    heads, width = part.shape
    halves = part.reshape(heads, 2, width // 2).transpose(1, 0, 2)
    shape = halves.shape[1:]
    return pl.pallas_call(
        gain_sum_kernel,
        out_shape=jax.ShapeDtypeStruct(shape, part.dtype),
        in_specs=[pl.BlockSpec(memory_space=pltpu.VMEM)],
        out_specs=pl.BlockSpec(memory_space=pltpu.VMEM),
        scratch_shapes=[
            pltpu.VMEM(shape, part.dtype),
            pltpu.VMEM((count,) + shape, part.dtype),
            pltpu.SemaphoreType.DMA((2,)),
            pltpu.SemaphoreType.DMA((count,)),
            pltpu.SemaphoreType.DMA((count,)),
        ],
        compiler_params=pltpu.CompilerParams(collective_id=0, has_side_effects=True),
    )(halves)


def scan_kernel(fwd_ref, bwd_ref, fwd_out, bwd_out, aggs, exs, slots, send_sem, recv_sem):
    count = lax.axis_size("ctx")
    me = lax.axis_index("ctx")
    row, col = lax.axis_index("dp"), lax.axis_index("head")
    heads, rows = fwd_out.shape[0], fwd_out.shape[1]
    shifts = []
    shift = 1
    while shift < count:
        shifts.append(shift)
        shift *= 2
    rounds = len(shifts)

    def device(index):
        return (row, index, col)

    barrier = pltpu.get_barrier_semaphore()
    for shift in shifts:
        for peer, present in ((me + shift, me + shift < count), (me - shift, me >= shift)):
            @pl.when(present)
            def _():
                pl.semaphore_signal(
                    barrier, inc=1, device_id=device(peer), device_id_type=pl.DeviceIdType.MESH
                )

    def at_least(bound):
        span = (count - 1) // bound + 1
        return (me // bound + span - 1) // span

    peers = 0
    for shift in shifts:
        peers = peers + at_least(shift) + 1 - at_least(count - shift)
    pl.semaphore_wait(barrier, peers)

    def sends(side, step):
        return me + shifts[step] < count if side == 0 else me >= shifts[step]

    def target(side, step):
        return me + shifts[step] if side == 0 else me - shifts[step]

    def source(side, step):
        return me - shifts[step] if side == 0 else me + shifts[step]

    inputs = (fwd_ref, bwd_ref)

    def held(side, step):
        return inputs[side] if step == 0 else aggs.at[side, step % 2]

    def copy_of(side, step, head, peer):
        return pltpu.make_async_remote_copy(
            src_ref=held(side, step).at[head],
            dst_ref=slots.at[side, step, head],
            send_sem=send_sem.at[side, step, head],
            recv_sem=recv_sem.at[side, step, head],
            device_id=device(peer),
            device_id_type=pl.DeviceIdType.MESH,
        )

    def send(side, step, head):
        @pl.when(sends(side, step))
        def _():
            copy_of(side, step, head, target(side, step)).start()

    def sent(side, step, head):
        @pl.when(sends(side, step))
        def _():
            copy_of(side, step, head, target(side, step)).wait_send()

    exs[...] = jnp.zeros_like(exs)
    exs[:, :, rows:, :] = jnp.ones_like(exs[:, :, rows:, :])
    for head in range(heads):
        for side in range(2):
            send(side, 0, head)

    for step in range(rounds):
        for head in range(heads):
            for side in range(2):
                current = held(side, step).at[head]
                later = aggs.at[side, (step + 1) % 2, head]
                has_next = step + 1 < rounds

                @pl.when(sends(1 - side, step))
                def _():
                    copy_of(side, step, head, source(side, step)).wait_recv()
                    got = slots[side, step, head]
                    if has_next:
                        if step >= 1:
                            sent(side, step - 1, head)
                        agg = current[...]
                        agg_a = agg[rows:rows + 1, :]
                        later[:rows, :] = agg_a * got[:rows, :] + agg[:rows, :]
                        later[rows:, :] = agg[rows:, :] * got[rows:, :]
                    ex = exs[side, head]
                    ex_a = ex[rows:rows + 1, :]
                    exs[side, head, :rows, :] = ex_a * got[:rows, :] + ex[:rows, :]
                    exs[side, head, rows:, :] = ex[rows:, :] * got[rows:, :]

                if has_next:
                    @pl.when(jnp.logical_not(sends(1 - side, step)))
                    def _():
                        if step >= 1:
                            sent(side, step - 1, head)
                        later[...] = current[...]

                    send(side, step + 1, head)

    for step in range(max(0, rounds - 2), rounds):
        for head in range(heads):
            for side in range(2):
                sent(side, step, head)

    fwd_out[...] = exs[0, :, :rows, :]
    bwd_out[...] = exs[1, :, :rows, :]


def both_scans_kernel(decay, fwd_term, bwd_term, count):
    heads, rows, width = fwd_term.shape
    rounds = max(1, (count - 1).bit_length())
    lane = jnp.broadcast_to(decay[:, None, None], (heads, 8, width))
    fwd = jnp.concatenate([fwd_term, lane], axis=1)
    bwd = jnp.concatenate([bwd_term, lane], axis=1)
    packed = fwd.shape
    out = jax.ShapeDtypeStruct(fwd_term.shape, jnp.float32)
    return pl.pallas_call(
        scan_kernel,
        out_shape=(out, out),
        in_specs=[pl.BlockSpec(memory_space=pltpu.VMEM)] * 2,
        out_specs=(pl.BlockSpec(memory_space=pltpu.VMEM),) * 2,
        scratch_shapes=[
            pltpu.VMEM((2, 2) + packed, jnp.float32),
            pltpu.VMEM((2,) + packed, jnp.float32),
            pltpu.VMEM((2, rounds) + packed, jnp.float32),
            pltpu.SemaphoreType.DMA((2, rounds, heads)),
            pltpu.SemaphoreType.DMA((2, rounds, heads)),
        ],
        compiler_params=pltpu.CompilerParams(collective_id=1, has_side_effects=True),
    )(fwd, bwd)


def start_flags(doc_lengths, first_pos, num_rows):
    starts = jnp.cumsum(doc_lengths, dtype=jnp.int32) - doc_lengths
    positions = first_pos + jnp.arange(num_rows, dtype=jnp.int32)
    matches = jnp.any(positions[:, None] == starts[None, :], axis=1)
    return matches.astype(jnp.float32)


def make_step(key_gain, head_width):
    q_scale = head_width ** (-0.5)

    def block_step(carried, inputs):
        q_block, k_block, v_block, gate_block, flag_block = inputs
        k_bf = (k_block.astype(jnp.float32) * key_gain[None]).astype(jnp.bfloat16)
        q_float = q_block.astype(jnp.float32) * q_scale
        k_float = lax.optimization_barrier(k_bf).astype(jnp.float32)
        v_float = v_block.astype(jnp.float32)
        segment = jnp.cumsum(flag_block)
        positions = jnp.arange(flag_block.shape[0])
        same_doc = (segment[:, None] == segment[None, :]) & (
            positions[:, None] >= positions[None, :]
        )
        cum_decay = jnp.cumsum(gate_block, axis=1)
        exponent = cum_decay[:, :, None] - cum_decay[:, None, :]
        decays = jnp.where(same_doc[None], jnp.exp(jnp.where(same_doc[None], exponent, 0.0)), 0.0)
        scores = jnp.einsum("thd,shd->hts", q_block, k_bf, preferred_element_type=jnp.float32)
        weights = (scores * q_scale * decays).astype(jnp.bfloat16)
        within = jnp.einsum("hts,she->the", weights, v_block, preferred_element_type=jnp.float32)
        opened = (segment == 0).astype(cum_decay.dtype)
        carry_in = jnp.exp(cum_decay) * opened[None, :]
        across = (
            jnp.einsum("thd,hde->the", q_float, carried, precision=PRECISE) * carry_in.T[:, :, None]
        )
        tail_mask = (segment == segment[-1]).astype(cum_decay.dtype)
        to_end = jnp.exp(cum_decay[:, -1:] - cum_decay) * tail_mask[None, :]
        written = jnp.einsum(
            "shd,she->hde", k_float * to_end.T[:, :, None], v_float, precision=PRECISE
        )
        end_state = carried * carry_in[:, -1][:, None, None] + written
        return (end_state, within + across)

    return block_step


def run_blocks(q_rows, k_rows, v_rows, gate_rows, flags, key_gain, start_state):
    num_rows = q_rows.shape[0]
    head_count = key_gain.shape[0]
    head_width = key_gain.shape[1]
    num_blocks = num_rows // BLOCK

    def to_blocks(tensor):
        return tensor.reshape(num_blocks, BLOCK, head_count, head_width)

    gate_blocks = gate_rows.reshape(head_count, num_blocks, BLOCK).transpose(1, 0, 2)
    flag_blocks = flags.reshape(num_blocks, BLOCK)
    end_state, outputs = lax.scan(
        jax.checkpoint(make_step(key_gain, head_width)),
        start_state,
        (to_blocks(q_rows), to_blocks(k_rows), to_blocks(v_rows), gate_blocks, flag_blocks),
    )
    return (outputs.reshape(num_rows, head_count * head_width), end_state)


def shards(queries, keys_raw, values, gates, lengths, key_gain, cotangent):
    tok_rows = queries.shape[1]
    head_count = key_gain.shape[0]
    head_width = key_gain.shape[1]
    flags = start_flags(lengths[0], lax.axis_index("ctx") * tok_rows, tok_rows)
    q_rows, k_rows, v_rows, gate_rows = (queries[0], keys_raw[0], values[0], gates[0])
    segment = jnp.cumsum(flags)
    opened = (segment == 0).astype(jnp.float32)
    tail_mask = (segment == segment[-1]).astype(jnp.float32)
    cum_decay = jnp.cumsum(gate_rows, axis=1)
    shard_decay = jnp.exp(cum_decay[:, -1]) * opened[-1]
    to_end = jnp.exp(cum_decay[:, -1:] - cum_decay) * tail_mask[None, :]
    k_bf = (
        k_rows.reshape(tok_rows, head_count, head_width).astype(jnp.float32) * key_gain[None]
    ).astype(jnp.bfloat16)
    k_float = lax.optimization_barrier(k_bf).astype(jnp.float32)
    v_float = v_rows.reshape(tok_rows, head_count, head_width).astype(jnp.float32)
    local_end = jnp.einsum(
        "shd,she->hde", k_float * to_end.T[:, :, None], v_float, precision=PRECISE
    )
    ctx_size = lax.axis_size("ctx")
    local_grad = local_incoming_grad(q_rows, cotangent[0], cum_decay, opened, head_count, head_width)
    state_in, later_grad = both_scans_kernel(shard_decay, local_end, local_grad, ctx_size)

    def forward(q_part, k_part, v_part, gate_part, gain_part):
        return run_blocks(q_part, k_part, v_part, gate_part, flags, gain_part, state_in)

    (primal, end_state), pullback = jax.vjp(forward, q_rows, k_rows, v_rows, gate_rows, key_gain)
    cot_float = cotangent[0].astype(jnp.float32)
    grad_q, grad_k, grad_v, grad_a, gain_term = pullback((cot_float, later_grad))
    grad_gain = gain_sum(gain_term, ctx_size)
    return (
        primal.astype(jnp.bfloat16)[None],
        grad_q[None],
        grad_k[None],
        grad_v[None],
        grad_a[None],
        grad_gain,
    )


def solution(mesh):
    placed = (
        P("dp", "ctx", "head"),
        P("dp", "ctx", "head"),
        P("dp", "ctx", "head"),
        P("dp", "head", "ctx"),
        P("dp", None),
        P("head", None),
        P("dp", "ctx", "head"),
    )
    return jax.shard_map(
        shards,
        mesh=mesh,
        in_specs=placed,
        out_specs=(
            P("dp", "ctx", "head"),
            P("dp", "ctx", "head"),
            P("dp", "ctx", "head"),
            P("dp", "ctx", "head"),
            P("dp", "head", "ctx"),
            P("head", "dp"),
        ),
        check_vma=False,
    )
```

```python
import jax
import jax.numpy as jnp
from jax import lax
from jax.sharding import PartitionSpec as P
from jax.experimental import pallas as pl
from jax.experimental.pallas import tpu as pltpu

BLOCK = 512


PRECISE = lax.Precision.HIGHEST


def passed_along(value, axis, steps):
    count = lax.axis_size(axis)
    first, last = (max(0, -steps), min(count, count - steps))
    return lax.ppermute(value, axis, [(source, source + steps) for source in range(first, last)])


def local_incoming_grad(q_rows, cot_rows, cum_decay, opened, head_count, head_width):
    tok_rows = q_rows.shape[0]
    factor = jnp.exp(cum_decay) * opened[None, :]
    weighted = (
        q_rows.reshape(tok_rows, head_count, head_width).astype(jnp.float32)
        * head_width ** (-0.5)
        * factor.T[:, :, None]
    )
    cot_float = cot_rows.astype(jnp.float32)
    return jnp.einsum(
        "thd,the->hde",
        weighted,
        cot_float.reshape(tok_rows, head_count, head_width),
        precision=PRECISE,
    )


def pack(decay, term):
    lane = jnp.broadcast_to(decay[:, None, None], (term.shape[0], 1, term.shape[2]))
    return jnp.concatenate([term, lane], axis=1)


def both_scans(decay, fwd_term, bwd_term, count):
    rows = fwd_term.shape[1]
    scans = []
    for term in (fwd_term, bwd_term):
        scans.append([decay, term, jnp.ones_like(decay), jnp.zeros_like(term)])
    shift = 1
    while shift < count:
        got = [
            passed_along(pack(agg_a, agg_b), "ctx", shift * sign)
            for (agg_a, agg_b, _, _), sign in zip(scans, (1, -1))
        ]
        for index, received in enumerate(got):
            agg_a, agg_b, ex_a, ex_b = scans[index]
            r_b, r_a = received[:, :rows], received[:, rows, 0]
            ex_b = ex_a[:, None, None] * r_b + ex_b
            ex_a = ex_a * r_a
            agg_b = agg_a[:, None, None] * r_b + agg_b
            agg_a = agg_a * r_a
            scans[index] = [agg_a, agg_b, ex_a, ex_b]
        shift *= 2
    return scans[0][3], scans[1][3]


def gain_sum_kernel(part_ref, total_ref, pair_slot, slots, pair_sem, send_sem, recv_sem):
    count = slots.shape[0]
    me = lax.axis_index("ctx")
    row, col = lax.axis_index("dp"), lax.axis_index("head")
    other = 1 - row

    def peer_of(step):
        return lax.rem(me + step, count)

    barrier = pltpu.get_barrier_semaphore()
    pl.semaphore_signal(
        barrier, inc=1, device_id=(other, me, col), device_id_type=pl.DeviceIdType.MESH
    )
    for step in range(1, count):
        pl.semaphore_signal(
            barrier, inc=1, device_id=(row, peer_of(step), col), device_id_type=pl.DeviceIdType.MESH
        )
    pl.semaphore_wait(barrier, count)

    pair = pltpu.make_async_remote_copy(
        src_ref=part_ref.at[other],
        dst_ref=pair_slot,
        send_sem=pair_sem.at[0],
        recv_sem=pair_sem.at[1],
        device_id=(other, me, col),
        device_id_type=pl.DeviceIdType.MESH,
    )
    pair.start()
    pair.wait_send()
    pair.wait_recv()
    slots[me] = part_ref[row] + pair_slot[...]

    copies = []
    for step in range(1, count):
        peer = peer_of(step)
        copy = pltpu.make_async_remote_copy(
            src_ref=slots.at[me],
            dst_ref=slots.at[me],
            send_sem=send_sem.at[peer],
            recv_sem=recv_sem.at[me],
            device_id=(row, peer, col),
            device_id_type=pl.DeviceIdType.MESH,
        )
        copy.start()
        copies.append(copy)
    for step in range(1, count):
        copies[step - 1].wait_send()
        source = lax.rem(me + count - step, count)
        pltpu.make_async_remote_copy(
            src_ref=slots.at[source],
            dst_ref=slots.at[source],
            send_sem=send_sem.at[source],
            recv_sem=recv_sem.at[source],
            device_id=(row, source, col),
            device_id_type=pl.DeviceIdType.MESH,
        ).wait_recv()
    total = slots[0]
    for index in range(1, count):
        total = total + slots[index]
    total_ref[...] = total


def gain_sum(part, count):
    heads, width = part.shape
    halves = part.reshape(heads, 2, width // 2).transpose(1, 0, 2)
    shape = halves.shape[1:]
    return pl.pallas_call(
        gain_sum_kernel,
        out_shape=jax.ShapeDtypeStruct(shape, part.dtype),
        in_specs=[pl.BlockSpec(memory_space=pltpu.VMEM)],
        out_specs=pl.BlockSpec(memory_space=pltpu.VMEM),
        scratch_shapes=[
            pltpu.VMEM(shape, part.dtype),
            pltpu.VMEM((count,) + shape, part.dtype),
            pltpu.SemaphoreType.DMA((2,)),
            pltpu.SemaphoreType.DMA((count,)),
            pltpu.SemaphoreType.DMA((count,)),
        ],
        compiler_params=pltpu.CompilerParams(collective_id=0, has_side_effects=True),
    )(halves)


def scan_kernel(fwd_ref, bwd_ref, fwd_out, bwd_out, aggs, exs, slots, send_sem, recv_sem):
    count = lax.axis_size("ctx")
    me = lax.axis_index("ctx")
    row, col = lax.axis_index("dp"), lax.axis_index("head")
    rows = fwd_out.shape[1]
    shifts = []
    shift = 1
    while shift < count:
        shifts.append(shift)
        shift *= 2

    def device(index):
        return (row, index, col)

    barrier = pltpu.get_barrier_semaphore()
    for shift in shifts:
        for peer, present in ((me + shift, me + shift < count), (me - shift, me >= shift)):
            @pl.when(present)
            def _():
                pl.semaphore_signal(
                    barrier, inc=1, device_id=device(peer), device_id_type=pl.DeviceIdType.MESH
                )

    def at_least(bound):
        span = (count - 1) // bound + 1
        return (me // bound + span - 1) // span

    peers = 0
    for shift in shifts:
        peers = peers + at_least(shift) + 1 - at_least(count - shift)
    pl.semaphore_wait(barrier, peers)

    aggs[0] = fwd_ref[...]
    aggs[1] = bwd_ref[...]
    exs[...] = jnp.zeros_like(exs)
    exs[:, :, rows:, :] = jnp.ones_like(exs[:, :, rows:, :])

    for round_index, shift in enumerate(shifts):
        sends = (me + shift < count, me >= shift)
        targets = (me + shift, me - shift)
        sources = (me - shift, me + shift)

        def copy_of(side, peer):
            return pltpu.make_async_remote_copy(
                src_ref=aggs.at[side],
                dst_ref=slots.at[side, round_index],
                send_sem=send_sem.at[side, round_index],
                recv_sem=recv_sem.at[side, round_index],
                device_id=device(peer),
                device_id_type=pl.DeviceIdType.MESH,
            )

        for side in range(2):
            @pl.when(sends[side])
            def _():
                copy_of(side, targets[side]).start()

        for side in range(2):
            @pl.when(sends[side])
            def _():
                copy_of(side, targets[side]).wait_send()

        for side in range(2):
            @pl.when(sends[1 - side])
            def _():
                copy_of(side, sources[side]).wait_recv()
                got = slots[side, round_index]
                ex = exs[side]
                agg = aggs[side]
                ex_a = ex[:, rows:rows + 1, :]
                agg_a = agg[:, rows:rows + 1, :]
                exs[side, :, :rows, :] = ex_a * got[:, :rows, :] + ex[:, :rows, :]
                exs[side, :, rows:, :] = ex[:, rows:, :] * got[:, rows:, :]
                aggs[side, :, :rows, :] = agg_a * got[:, :rows, :] + agg[:, :rows, :]
                aggs[side, :, rows:, :] = agg[:, rows:, :] * got[:, rows:, :]

    fwd_out[...] = exs[0, :, :rows, :]
    bwd_out[...] = exs[1, :, :rows, :]


def both_scans_kernel(decay, fwd_term, bwd_term, count):
    heads, rows, width = fwd_term.shape
    rounds = max(1, (count - 1).bit_length())
    lane = jnp.broadcast_to(decay[:, None, None], (heads, 8, width))
    fwd = jnp.concatenate([fwd_term, lane], axis=1)
    bwd = jnp.concatenate([bwd_term, lane], axis=1)
    packed = fwd.shape
    out = jax.ShapeDtypeStruct(fwd_term.shape, jnp.float32)
    return pl.pallas_call(
        scan_kernel,
        out_shape=(out, out),
        in_specs=[pl.BlockSpec(memory_space=pltpu.VMEM)] * 2,
        out_specs=(pl.BlockSpec(memory_space=pltpu.VMEM),) * 2,
        scratch_shapes=[
            pltpu.VMEM((2,) + packed, jnp.float32),
            pltpu.VMEM((2,) + packed, jnp.float32),
            pltpu.VMEM((2, rounds) + packed, jnp.float32),
            pltpu.SemaphoreType.DMA((2, rounds)),
            pltpu.SemaphoreType.DMA((2, rounds)),
        ],
        compiler_params=pltpu.CompilerParams(collective_id=1, has_side_effects=True),
    )(fwd, bwd)


def start_flags(doc_lengths, first_pos, num_rows):
    starts = jnp.cumsum(doc_lengths, dtype=jnp.int32) - doc_lengths
    positions = first_pos + jnp.arange(num_rows, dtype=jnp.int32)
    matches = jnp.any(positions[:, None] == starts[None, :], axis=1)
    return matches.astype(jnp.float32)


def make_step(key_gain, head_width):
    q_scale = head_width ** (-0.5)

    def block_step(carried, inputs):
        q_block, k_block, v_block, gate_block, flag_block = inputs
        k_bf = (k_block.astype(jnp.float32) * key_gain[None]).astype(jnp.bfloat16)
        q_float = q_block.astype(jnp.float32) * q_scale
        k_float = lax.optimization_barrier(k_bf).astype(jnp.float32)
        v_float = v_block.astype(jnp.float32)
        segment = jnp.cumsum(flag_block)
        positions = jnp.arange(flag_block.shape[0])
        same_doc = (segment[:, None] == segment[None, :]) & (
            positions[:, None] >= positions[None, :]
        )
        cum_decay = jnp.cumsum(gate_block, axis=1)
        exponent = cum_decay[:, :, None] - cum_decay[:, None, :]
        decays = jnp.where(same_doc[None], jnp.exp(jnp.where(same_doc[None], exponent, 0.0)), 0.0)
        scores = jnp.einsum("thd,shd->hts", q_block, k_bf, preferred_element_type=jnp.float32)
        weights = (scores * q_scale * decays).astype(jnp.bfloat16)
        within = jnp.einsum("hts,she->the", weights, v_block, preferred_element_type=jnp.float32)
        opened = (segment == 0).astype(cum_decay.dtype)
        carry_in = jnp.exp(cum_decay) * opened[None, :]
        across = (
            jnp.einsum("thd,hde->the", q_float, carried, precision=PRECISE) * carry_in.T[:, :, None]
        )
        tail_mask = (segment == segment[-1]).astype(cum_decay.dtype)
        to_end = jnp.exp(cum_decay[:, -1:] - cum_decay) * tail_mask[None, :]
        written = jnp.einsum(
            "shd,she->hde", k_float * to_end.T[:, :, None], v_float, precision=PRECISE
        )
        end_state = carried * carry_in[:, -1][:, None, None] + written
        return (end_state, within + across)

    return block_step


def run_blocks(q_rows, k_rows, v_rows, gate_rows, flags, key_gain, start_state):
    num_rows = q_rows.shape[0]
    head_count = key_gain.shape[0]
    head_width = key_gain.shape[1]
    num_blocks = num_rows // BLOCK

    def to_blocks(tensor):
        return tensor.reshape(num_blocks, BLOCK, head_count, head_width)

    gate_blocks = gate_rows.reshape(head_count, num_blocks, BLOCK).transpose(1, 0, 2)
    flag_blocks = flags.reshape(num_blocks, BLOCK)
    end_state, outputs = lax.scan(
        jax.checkpoint(make_step(key_gain, head_width)),
        start_state,
        (to_blocks(q_rows), to_blocks(k_rows), to_blocks(v_rows), gate_blocks, flag_blocks),
        unroll=True,
    )
    return (outputs.reshape(num_rows, head_count * head_width), end_state)


def shards(queries, keys_raw, values, gates, lengths, key_gain, cotangent):
    tok_rows = queries.shape[1]
    head_count = key_gain.shape[0]
    head_width = key_gain.shape[1]
    flags = start_flags(lengths[0], lax.axis_index("ctx") * tok_rows, tok_rows)
    q_rows, k_rows, v_rows, gate_rows = (queries[0], keys_raw[0], values[0], gates[0])
    segment = jnp.cumsum(flags)
    opened = (segment == 0).astype(jnp.float32)
    tail_mask = (segment == segment[-1]).astype(jnp.float32)
    cum_decay = jnp.cumsum(gate_rows, axis=1)
    shard_decay = jnp.exp(cum_decay[:, -1]) * opened[-1]
    to_end = jnp.exp(cum_decay[:, -1:] - cum_decay) * tail_mask[None, :]
    k_bf = (
        k_rows.reshape(tok_rows, head_count, head_width).astype(jnp.float32) * key_gain[None]
    ).astype(jnp.bfloat16)
    k_float = lax.optimization_barrier(k_bf).astype(jnp.float32)
    v_float = v_rows.reshape(tok_rows, head_count, head_width).astype(jnp.float32)
    local_end = jnp.einsum(
        "shd,she->hde", k_float * to_end.T[:, :, None], v_float, precision=PRECISE
    )
    ctx_size = lax.axis_size("ctx")
    local_grad = local_incoming_grad(q_rows, cotangent[0], cum_decay, opened, head_count, head_width)
    state_in, later_grad = both_scans_kernel(shard_decay, local_end, local_grad, ctx_size)

    def forward(q_part, k_part, v_part, gate_part, gain_part):
        return run_blocks(q_part, k_part, v_part, gate_part, flags, gain_part, state_in)

    (primal, end_state), pullback = jax.vjp(forward, q_rows, k_rows, v_rows, gate_rows, key_gain)
    cot_float = cotangent[0].astype(jnp.float32)
    grad_q, grad_k, grad_v, grad_a, gain_term = pullback((cot_float, later_grad))
    grad_gain = gain_sum(gain_term, ctx_size)
    return (
        primal.astype(jnp.bfloat16)[None],
        grad_q[None],
        grad_k[None],
        grad_v[None],
        grad_a[None],
        grad_gain,
    )


def solution(mesh):
    placed = (
        P("dp", "ctx", "head"),
        P("dp", "ctx", "head"),
        P("dp", "ctx", "head"),
        P("dp", "head", "ctx"),
        P("dp", None),
        P("head", None),
        P("dp", "ctx", "head"),
    )
    return jax.shard_map(
        shards,
        mesh=mesh,
        in_specs=placed,
        out_specs=(
            P("dp", "ctx", "head"),
            P("dp", "ctx", "head"),
            P("dp", "ctx", "head"),
            P("dp", "ctx", "head"),
            P("dp", "head", "ctx"),
            P("head", "dp"),
        ),
        check_vma=False,
    )
```

```python
import jax
import jax.numpy as jnp
from jax import lax
from jax.sharding import PartitionSpec as P
from jax.experimental import pallas as pl
from jax.experimental.pallas import tpu as pltpu

BLOCK = 512


PRECISE = lax.Precision.HIGHEST


def passed_along(value, axis, steps):
    count = lax.axis_size(axis)
    first, last = (max(0, -steps), min(count, count - steps))
    return lax.ppermute(value, axis, [(source, source + steps) for source in range(first, last)])


def local_incoming_grad(q_rows, cot_rows, cum_decay, opened, head_count, head_width):
    tok_rows = q_rows.shape[0]
    factor = jnp.exp(cum_decay) * opened[None, :]
    weighted = (
        q_rows.reshape(tok_rows, head_count, head_width).astype(jnp.float32)
        * head_width ** (-0.5)
        * factor.T[:, :, None]
    )
    cot_float = cot_rows.astype(jnp.float32)
    return jnp.einsum(
        "thd,the->hde",
        weighted,
        cot_float.reshape(tok_rows, head_count, head_width),
        precision=PRECISE,
    )


def pack(decay, term):
    lane = jnp.broadcast_to(decay[:, None, None], (term.shape[0], 1, term.shape[2]))
    return jnp.concatenate([term, lane], axis=1)


def both_scans(decay, fwd_term, bwd_term, count):
    rows = fwd_term.shape[1]
    scans = []
    for term in (fwd_term, bwd_term):
        scans.append([decay, term, jnp.ones_like(decay), jnp.zeros_like(term)])
    shift = 1
    while shift < count:
        got = [
            passed_along(pack(agg_a, agg_b), "ctx", shift * sign)
            for (agg_a, agg_b, _, _), sign in zip(scans, (1, -1))
        ]
        for index, received in enumerate(got):
            agg_a, agg_b, ex_a, ex_b = scans[index]
            r_b, r_a = received[:, :rows], received[:, rows, 0]
            ex_b = ex_a[:, None, None] * r_b + ex_b
            ex_a = ex_a * r_a
            agg_b = agg_a[:, None, None] * r_b + agg_b
            agg_a = agg_a * r_a
            scans[index] = [agg_a, agg_b, ex_a, ex_b]
        shift *= 2
    return scans[0][3], scans[1][3]


def gain_sum_kernel(part_ref, total_ref, pair_slot, accs, slots, pair_sem, send_sem, recv_sem):
    count = lax.axis_size("ctx")
    me = lax.axis_index("ctx")
    row, col = lax.axis_index("dp"), lax.axis_index("head")
    other = 1 - row
    rounds = slots.shape[0]
    shifts = [1 << step for step in range(rounds)]

    def partner(shift):
        return me + shift - 2 * shift * ((me // shift) % 2)

    barrier = pltpu.get_barrier_semaphore()
    pl.semaphore_signal(
        barrier, inc=1, device_id=(other, me, col), device_id_type=pl.DeviceIdType.MESH
    )
    for shift in shifts:
        pl.semaphore_signal(
            barrier, inc=1, device_id=(row, partner(shift), col), device_id_type=pl.DeviceIdType.MESH
        )
    pl.semaphore_wait(barrier, rounds + 1)

    pair = pltpu.make_async_remote_copy(
        src_ref=part_ref.at[other],
        dst_ref=pair_slot,
        send_sem=pair_sem.at[0],
        recv_sem=pair_sem.at[1],
        device_id=(other, me, col),
        device_id_type=pl.DeviceIdType.MESH,
    )
    pair.start()
    pair.wait_send()
    pair.wait_recv()
    accs[0] = part_ref[row] + pair_slot[...]

    for step, shift in enumerate(shifts):
        copy = pltpu.make_async_remote_copy(
            src_ref=accs.at[step],
            dst_ref=slots.at[step],
            send_sem=send_sem.at[step],
            recv_sem=recv_sem.at[step],
            device_id=(row, partner(shift), col),
            device_id_type=pl.DeviceIdType.MESH,
        )
        copy.start()
        copy.wait_send()
        copy.wait_recv()
        accs[step + 1] = accs[step] + slots[step]
    total_ref[...] = accs[rounds]


def gain_sum(part, count):
    heads, width = part.shape
    halves = part.reshape(heads, 2, width // 2).transpose(1, 0, 2)
    shape = halves.shape[1:]
    rounds = max(1, (count - 1).bit_length())
    return pl.pallas_call(
        gain_sum_kernel,
        out_shape=jax.ShapeDtypeStruct(shape, part.dtype),
        in_specs=[pl.BlockSpec(memory_space=pltpu.VMEM)],
        out_specs=pl.BlockSpec(memory_space=pltpu.VMEM),
        scratch_shapes=[
            pltpu.VMEM(shape, part.dtype),
            pltpu.VMEM((rounds + 1,) + shape, part.dtype),
            pltpu.VMEM((rounds,) + shape, part.dtype),
            pltpu.SemaphoreType.DMA((2,)),
            pltpu.SemaphoreType.DMA((rounds,)),
            pltpu.SemaphoreType.DMA((rounds,)),
        ],
        compiler_params=pltpu.CompilerParams(collective_id=0, has_side_effects=True),
    )(halves)


def scan_kernel(fwd_ref, bwd_ref, fwd_out, bwd_out, aggs, exs, slots, send_sem, recv_sem):
    count = lax.axis_size("ctx")
    me = lax.axis_index("ctx")
    row, col = lax.axis_index("dp"), lax.axis_index("head")
    rows = fwd_out.shape[1]
    shifts = []
    shift = 1
    while shift < count:
        shifts.append(shift)
        shift *= 2

    def device(index):
        return (row, index, col)

    barrier = pltpu.get_barrier_semaphore()
    for shift in shifts:
        for peer, present in ((me + shift, me + shift < count), (me - shift, me >= shift)):
            @pl.when(present)
            def _():
                pl.semaphore_signal(
                    barrier, inc=1, device_id=device(peer), device_id_type=pl.DeviceIdType.MESH
                )

    def at_least(bound):
        span = (count - 1) // bound + 1
        return (me // bound + span - 1) // span

    peers = 0
    for shift in shifts:
        peers = peers + at_least(shift) + 1 - at_least(count - shift)
    pl.semaphore_wait(barrier, peers)

    aggs[0] = fwd_ref[...]
    aggs[1] = bwd_ref[...]
    exs[...] = jnp.zeros_like(exs)
    exs[:, :, rows:, :] = jnp.ones_like(exs[:, :, rows:, :])

    for round_index, shift in enumerate(shifts):
        sends = (me + shift < count, me >= shift)
        targets = (me + shift, me - shift)
        sources = (me - shift, me + shift)

        def copy_of(side, peer):
            return pltpu.make_async_remote_copy(
                src_ref=aggs.at[side],
                dst_ref=slots.at[side, round_index],
                send_sem=send_sem.at[side, round_index],
                recv_sem=recv_sem.at[side, round_index],
                device_id=device(peer),
                device_id_type=pl.DeviceIdType.MESH,
            )

        for side in range(2):
            @pl.when(sends[side])
            def _():
                copy_of(side, targets[side]).start()

        for side in range(2):
            @pl.when(sends[side])
            def _():
                copy_of(side, targets[side]).wait_send()

        for side in range(2):
            @pl.when(sends[1 - side])
            def _():
                copy_of(side, sources[side]).wait_recv()
                got = slots[side, round_index]
                ex = exs[side]
                agg = aggs[side]
                ex_a = ex[:, rows:rows + 1, :]
                agg_a = agg[:, rows:rows + 1, :]
                exs[side, :, :rows, :] = ex_a * got[:, :rows, :] + ex[:, :rows, :]
                exs[side, :, rows:, :] = ex[:, rows:, :] * got[:, rows:, :]
                aggs[side, :, :rows, :] = agg_a * got[:, :rows, :] + agg[:, :rows, :]
                aggs[side, :, rows:, :] = agg[:, rows:, :] * got[:, rows:, :]

    fwd_out[...] = exs[0, :, :rows, :]
    bwd_out[...] = exs[1, :, :rows, :]


def both_scans_kernel(decay, fwd_term, bwd_term, count):
    heads, rows, width = fwd_term.shape
    rounds = max(1, (count - 1).bit_length())
    lane = jnp.broadcast_to(decay[:, None, None], (heads, 8, width))
    fwd = jnp.concatenate([fwd_term, lane], axis=1)
    bwd = jnp.concatenate([bwd_term, lane], axis=1)
    packed = fwd.shape
    out = jax.ShapeDtypeStruct(fwd_term.shape, jnp.float32)
    return pl.pallas_call(
        scan_kernel,
        out_shape=(out, out),
        in_specs=[pl.BlockSpec(memory_space=pltpu.VMEM)] * 2,
        out_specs=(pl.BlockSpec(memory_space=pltpu.VMEM),) * 2,
        scratch_shapes=[
            pltpu.VMEM((2,) + packed, jnp.float32),
            pltpu.VMEM((2,) + packed, jnp.float32),
            pltpu.VMEM((2, rounds) + packed, jnp.float32),
            pltpu.SemaphoreType.DMA((2, rounds)),
            pltpu.SemaphoreType.DMA((2, rounds)),
        ],
        compiler_params=pltpu.CompilerParams(collective_id=1, has_side_effects=True),
    )(fwd, bwd)


def start_flags(doc_lengths, first_pos, num_rows):
    starts = jnp.cumsum(doc_lengths, dtype=jnp.int32) - doc_lengths
    positions = first_pos + jnp.arange(num_rows, dtype=jnp.int32)
    matches = jnp.any(positions[:, None] == starts[None, :], axis=1)
    return matches.astype(jnp.float32)


def make_step(key_gain, head_width):
    q_scale = head_width ** (-0.5)

    def block_step(carried, inputs):
        q_block, k_block, v_block, gate_block, flag_block = inputs
        k_bf = (k_block.astype(jnp.float32) * key_gain[None]).astype(jnp.bfloat16)
        q_float = q_block.astype(jnp.float32) * q_scale
        k_float = lax.optimization_barrier(k_bf).astype(jnp.float32)
        v_float = v_block.astype(jnp.float32)
        segment = jnp.cumsum(flag_block)
        positions = jnp.arange(flag_block.shape[0])
        same_doc = (segment[:, None] == segment[None, :]) & (
            positions[:, None] >= positions[None, :]
        )
        cum_decay = jnp.cumsum(gate_block, axis=1)
        exponent = cum_decay[:, :, None] - cum_decay[:, None, :]
        decays = jnp.where(same_doc[None], jnp.exp(jnp.where(same_doc[None], exponent, 0.0)), 0.0)
        scores = jnp.einsum("thd,shd->hts", q_block, k_bf, preferred_element_type=jnp.float32)
        weights = (scores * q_scale * decays).astype(jnp.bfloat16)
        within = jnp.einsum("hts,she->the", weights, v_block, preferred_element_type=jnp.float32)
        opened = (segment == 0).astype(cum_decay.dtype)
        carry_in = jnp.exp(cum_decay) * opened[None, :]
        across = (
            jnp.einsum("thd,hde->the", q_float, carried, precision=PRECISE) * carry_in.T[:, :, None]
        )
        tail_mask = (segment == segment[-1]).astype(cum_decay.dtype)
        to_end = jnp.exp(cum_decay[:, -1:] - cum_decay) * tail_mask[None, :]
        written = jnp.einsum(
            "shd,she->hde", k_float * to_end.T[:, :, None], v_float, precision=PRECISE
        )
        end_state = carried * carry_in[:, -1][:, None, None] + written
        return (end_state, within + across)

    return block_step


def run_blocks(q_rows, k_rows, v_rows, gate_rows, flags, key_gain, start_state):
    num_rows = q_rows.shape[0]
    head_count = key_gain.shape[0]
    head_width = key_gain.shape[1]
    num_blocks = num_rows // BLOCK

    def to_blocks(tensor):
        return tensor.reshape(num_blocks, BLOCK, head_count, head_width)

    gate_blocks = gate_rows.reshape(head_count, num_blocks, BLOCK).transpose(1, 0, 2)
    flag_blocks = flags.reshape(num_blocks, BLOCK)
    end_state, outputs = lax.scan(
        jax.checkpoint(make_step(key_gain, head_width)),
        start_state,
        (to_blocks(q_rows), to_blocks(k_rows), to_blocks(v_rows), gate_blocks, flag_blocks),
    )
    return (outputs.reshape(num_rows, head_count * head_width), end_state)


def shards(queries, keys_raw, values, gates, lengths, key_gain, cotangent):
    tok_rows = queries.shape[1]
    head_count = key_gain.shape[0]
    head_width = key_gain.shape[1]
    flags = start_flags(lengths[0], lax.axis_index("ctx") * tok_rows, tok_rows)
    q_rows, k_rows, v_rows, gate_rows = (queries[0], keys_raw[0], values[0], gates[0])
    segment = jnp.cumsum(flags)
    opened = (segment == 0).astype(jnp.float32)
    tail_mask = (segment == segment[-1]).astype(jnp.float32)
    cum_decay = jnp.cumsum(gate_rows, axis=1)
    shard_decay = jnp.exp(cum_decay[:, -1]) * opened[-1]
    to_end = jnp.exp(cum_decay[:, -1:] - cum_decay) * tail_mask[None, :]
    k_bf = (
        k_rows.reshape(tok_rows, head_count, head_width).astype(jnp.float32) * key_gain[None]
    ).astype(jnp.bfloat16)
    k_float = lax.optimization_barrier(k_bf).astype(jnp.float32)
    v_float = v_rows.reshape(tok_rows, head_count, head_width).astype(jnp.float32)
    local_end = jnp.einsum(
        "shd,she->hde", k_float * to_end.T[:, :, None], v_float, precision=PRECISE
    )
    ctx_size = lax.axis_size("ctx")
    local_grad = local_incoming_grad(q_rows, cotangent[0], cum_decay, opened, head_count, head_width)
    state_in, later_grad = both_scans_kernel(shard_decay, local_end, local_grad, ctx_size)

    def forward(q_part, k_part, v_part, gate_part, gain_part):
        return run_blocks(q_part, k_part, v_part, gate_part, flags, gain_part, state_in)

    (primal, end_state), pullback = jax.vjp(forward, q_rows, k_rows, v_rows, gate_rows, key_gain)
    cot_float = cotangent[0].astype(jnp.float32)
    grad_q, grad_k, grad_v, grad_a, gain_term = pullback((cot_float, later_grad))
    grad_gain = gain_sum(gain_term, ctx_size)
    return (
        primal.astype(jnp.bfloat16)[None],
        grad_q[None],
        grad_k[None],
        grad_v[None],
        grad_a[None],
        grad_gain,
    )


def solution(mesh):
    placed = (
        P("dp", "ctx", "head"),
        P("dp", "ctx", "head"),
        P("dp", "ctx", "head"),
        P("dp", "head", "ctx"),
        P("dp", None),
        P("head", None),
        P("dp", "ctx", "head"),
    )
    return jax.shard_map(
        shards,
        mesh=mesh,
        in_specs=placed,
        out_specs=(
            P("dp", "ctx", "head"),
            P("dp", "ctx", "head"),
            P("dp", "ctx", "head"),
            P("dp", "ctx", "head"),
            P("dp", "head", "ctx"),
            P("head", "dp"),
        ),
        check_vma=False,
    )
```

```python
import jax
import jax.numpy as jnp
from jax import lax
from jax.sharding import PartitionSpec as P
from jax.experimental import pallas as pl
from jax.experimental.pallas import tpu as pltpu

BLOCK = 512


PRECISE = lax.Precision.HIGH


def passed_along(value, axis, steps):
    count = lax.axis_size(axis)
    first, last = (max(0, -steps), min(count, count - steps))
    return lax.ppermute(value, axis, [(source, source + steps) for source in range(first, last)])


def local_incoming_grad(q_rows, cot_rows, cum_decay, opened, head_count, head_width):
    tok_rows = q_rows.shape[0]
    factor = jnp.exp(cum_decay) * opened[None, :]
    weighted = (
        q_rows.reshape(tok_rows, head_count, head_width).astype(jnp.float32)
        * head_width ** (-0.5)
        * factor.T[:, :, None]
    )
    cot_float = cot_rows.astype(jnp.float32)
    return jnp.einsum(
        "thd,the->hde",
        weighted,
        cot_float.reshape(tok_rows, head_count, head_width),
        precision=PRECISE,
    )


def pack(decay, term):
    lane = jnp.broadcast_to(decay[:, None, None], (term.shape[0], 1, term.shape[2]))
    return jnp.concatenate([term, lane], axis=1)


def both_scans(decay, fwd_term, bwd_term, count):
    rows = fwd_term.shape[1]
    scans = []
    for term in (fwd_term, bwd_term):
        scans.append([decay, term, jnp.ones_like(decay), jnp.zeros_like(term)])
    shift = 1
    while shift < count:
        got = [
            passed_along(pack(agg_a, agg_b), "ctx", shift * sign)
            for (agg_a, agg_b, _, _), sign in zip(scans, (1, -1))
        ]
        for index, received in enumerate(got):
            agg_a, agg_b, ex_a, ex_b = scans[index]
            r_b, r_a = received[:, :rows], received[:, rows, 0]
            ex_b = ex_a[:, None, None] * r_b + ex_b
            ex_a = ex_a * r_a
            agg_b = agg_a[:, None, None] * r_b + agg_b
            agg_a = agg_a * r_a
            scans[index] = [agg_a, agg_b, ex_a, ex_b]
        shift *= 2
    return scans[0][3], scans[1][3]


def gain_sum_kernel(part_ref, total_ref, pair_slot, slots, pair_sem, send_sem, recv_sem):
    count = slots.shape[0]
    me = lax.axis_index("ctx")
    row, col = lax.axis_index("dp"), lax.axis_index("head")
    other = 1 - row

    def peer_of(step):
        return lax.rem(me + step, count)

    barrier = pltpu.get_barrier_semaphore()
    pl.semaphore_signal(
        barrier, inc=1, device_id=(other, me, col), device_id_type=pl.DeviceIdType.MESH
    )
    for step in range(1, count):
        pl.semaphore_signal(
            barrier, inc=1, device_id=(row, peer_of(step), col), device_id_type=pl.DeviceIdType.MESH
        )
    pl.semaphore_wait(barrier, count)

    pair = pltpu.make_async_remote_copy(
        src_ref=part_ref.at[other],
        dst_ref=pair_slot,
        send_sem=pair_sem.at[0],
        recv_sem=pair_sem.at[1],
        device_id=(other, me, col),
        device_id_type=pl.DeviceIdType.MESH,
    )
    pair.start()
    pair.wait_send()
    pair.wait_recv()
    slots[me] = part_ref[row] + pair_slot[...]

    copies = []
    for step in range(1, count):
        peer = peer_of(step)
        copy = pltpu.make_async_remote_copy(
            src_ref=slots.at[me],
            dst_ref=slots.at[me],
            send_sem=send_sem.at[peer],
            recv_sem=recv_sem.at[me],
            device_id=(row, peer, col),
            device_id_type=pl.DeviceIdType.MESH,
        )
        copy.start()
        copies.append(copy)
    for step in range(1, count):
        copies[step - 1].wait_send()
        source = lax.rem(me + count - step, count)
        pltpu.make_async_remote_copy(
            src_ref=slots.at[source],
            dst_ref=slots.at[source],
            send_sem=send_sem.at[source],
            recv_sem=recv_sem.at[source],
            device_id=(row, source, col),
            device_id_type=pl.DeviceIdType.MESH,
        ).wait_recv()
    total = slots[0]
    for index in range(1, count):
        total = total + slots[index]
    total_ref[...] = total


def gain_sum(part, count):
    heads, width = part.shape
    halves = part.reshape(heads, 2, width // 2).transpose(1, 0, 2)
    shape = halves.shape[1:]
    return pl.pallas_call(
        gain_sum_kernel,
        out_shape=jax.ShapeDtypeStruct(shape, part.dtype),
        in_specs=[pl.BlockSpec(memory_space=pltpu.VMEM)],
        out_specs=pl.BlockSpec(memory_space=pltpu.VMEM),
        scratch_shapes=[
            pltpu.VMEM(shape, part.dtype),
            pltpu.VMEM((count,) + shape, part.dtype),
            pltpu.SemaphoreType.DMA((2,)),
            pltpu.SemaphoreType.DMA((count,)),
            pltpu.SemaphoreType.DMA((count,)),
        ],
        compiler_params=pltpu.CompilerParams(collective_id=0, has_side_effects=True),
    )(halves)


def scan_kernel(fwd_ref, bwd_ref, fwd_out, bwd_out, aggs, exs, slots, send_sem, recv_sem):
    count = lax.axis_size("ctx")
    me = lax.axis_index("ctx")
    row, col = lax.axis_index("dp"), lax.axis_index("head")
    rows = fwd_out.shape[1]
    shifts = []
    shift = 1
    while shift < count:
        shifts.append(shift)
        shift *= 2

    def device(index):
        return (row, index, col)

    barrier = pltpu.get_barrier_semaphore()
    for shift in shifts:
        for peer, present in ((me + shift, me + shift < count), (me - shift, me >= shift)):
            @pl.when(present)
            def _():
                pl.semaphore_signal(
                    barrier, inc=1, device_id=device(peer), device_id_type=pl.DeviceIdType.MESH
                )

    def at_least(bound):
        span = (count - 1) // bound + 1
        return (me // bound + span - 1) // span

    peers = 0
    for shift in shifts:
        peers = peers + at_least(shift) + 1 - at_least(count - shift)
    pl.semaphore_wait(barrier, peers)

    aggs[0] = fwd_ref[...]
    aggs[1] = bwd_ref[...]
    exs[...] = jnp.zeros_like(exs)
    exs[:, :, rows:, :] = jnp.ones_like(exs[:, :, rows:, :])

    for round_index, shift in enumerate(shifts):
        sends = (me + shift < count, me >= shift)
        targets = (me + shift, me - shift)
        sources = (me - shift, me + shift)

        def copy_of(side, peer):
            return pltpu.make_async_remote_copy(
                src_ref=aggs.at[side],
                dst_ref=slots.at[side, round_index],
                send_sem=send_sem.at[side, round_index],
                recv_sem=recv_sem.at[side, round_index],
                device_id=device(peer),
                device_id_type=pl.DeviceIdType.MESH,
            )

        for side in range(2):
            @pl.when(sends[side])
            def _():
                copy_of(side, targets[side]).start()

        for side in range(2):
            @pl.when(sends[side])
            def _():
                copy_of(side, targets[side]).wait_send()

        for side in range(2):
            @pl.when(sends[1 - side])
            def _():
                copy_of(side, sources[side]).wait_recv()
                got = slots[side, round_index]
                ex = exs[side]
                agg = aggs[side]
                ex_a = ex[:, rows:rows + 1, :]
                agg_a = agg[:, rows:rows + 1, :]
                exs[side, :, :rows, :] = ex_a * got[:, :rows, :] + ex[:, :rows, :]
                exs[side, :, rows:, :] = ex[:, rows:, :] * got[:, rows:, :]
                aggs[side, :, :rows, :] = agg_a * got[:, :rows, :] + agg[:, :rows, :]
                aggs[side, :, rows:, :] = agg[:, rows:, :] * got[:, rows:, :]

    fwd_out[...] = exs[0, :, :rows, :]
    bwd_out[...] = exs[1, :, :rows, :]


def both_scans_kernel(decay, fwd_term, bwd_term, count):
    heads, rows, width = fwd_term.shape
    rounds = max(1, (count - 1).bit_length())
    lane = jnp.broadcast_to(decay[:, None, None], (heads, 8, width))
    fwd = jnp.concatenate([fwd_term, lane], axis=1)
    bwd = jnp.concatenate([bwd_term, lane], axis=1)
    packed = fwd.shape
    out = jax.ShapeDtypeStruct(fwd_term.shape, jnp.float32)
    return pl.pallas_call(
        scan_kernel,
        out_shape=(out, out),
        in_specs=[pl.BlockSpec(memory_space=pltpu.VMEM)] * 2,
        out_specs=(pl.BlockSpec(memory_space=pltpu.VMEM),) * 2,
        scratch_shapes=[
            pltpu.VMEM((2,) + packed, jnp.float32),
            pltpu.VMEM((2,) + packed, jnp.float32),
            pltpu.VMEM((2, rounds) + packed, jnp.float32),
            pltpu.SemaphoreType.DMA((2, rounds)),
            pltpu.SemaphoreType.DMA((2, rounds)),
        ],
        compiler_params=pltpu.CompilerParams(collective_id=1, has_side_effects=True),
    )(fwd, bwd)


def start_flags(doc_lengths, first_pos, num_rows):
    starts = jnp.cumsum(doc_lengths, dtype=jnp.int32) - doc_lengths
    positions = first_pos + jnp.arange(num_rows, dtype=jnp.int32)
    matches = jnp.any(positions[:, None] == starts[None, :], axis=1)
    return matches.astype(jnp.float32)


def make_step(key_gain, head_width):
    q_scale = head_width ** (-0.5)

    def block_step(carried, inputs):
        q_block, k_block, v_block, gate_block, flag_block = inputs
        k_bf = (k_block.astype(jnp.float32) * key_gain[None]).astype(jnp.bfloat16)
        q_float = q_block.astype(jnp.float32) * q_scale
        k_float = lax.optimization_barrier(k_bf).astype(jnp.float32)
        v_float = v_block.astype(jnp.float32)
        segment = jnp.cumsum(flag_block)
        positions = jnp.arange(flag_block.shape[0])
        same_doc = (segment[:, None] == segment[None, :]) & (
            positions[:, None] >= positions[None, :]
        )
        cum_decay = jnp.cumsum(gate_block, axis=1)
        exponent = cum_decay[:, :, None] - cum_decay[:, None, :]
        decays = jnp.where(same_doc[None], jnp.exp(jnp.where(same_doc[None], exponent, 0.0)), 0.0)
        scores = jnp.einsum("thd,shd->hts", q_block, k_bf, preferred_element_type=jnp.float32)
        weights = (scores * q_scale * decays).astype(jnp.bfloat16)
        within = jnp.einsum("hts,she->the", weights, v_block, preferred_element_type=jnp.float32)
        opened = (segment == 0).astype(cum_decay.dtype)
        carry_in = jnp.exp(cum_decay) * opened[None, :]
        across = (
            jnp.einsum("thd,hde->the", q_float, carried, precision=PRECISE) * carry_in.T[:, :, None]
        )
        tail_mask = (segment == segment[-1]).astype(cum_decay.dtype)
        to_end = jnp.exp(cum_decay[:, -1:] - cum_decay) * tail_mask[None, :]
        written = jnp.einsum(
            "shd,she->hde", k_float * to_end.T[:, :, None], v_float, precision=PRECISE
        )
        end_state = carried * carry_in[:, -1][:, None, None] + written
        return (end_state, within + across)

    return block_step


def run_blocks(q_rows, k_rows, v_rows, gate_rows, flags, key_gain, start_state):
    num_rows = q_rows.shape[0]
    head_count = key_gain.shape[0]
    head_width = key_gain.shape[1]
    num_blocks = num_rows // BLOCK

    def to_blocks(tensor):
        return tensor.reshape(num_blocks, BLOCK, head_count, head_width)

    gate_blocks = gate_rows.reshape(head_count, num_blocks, BLOCK).transpose(1, 0, 2)
    flag_blocks = flags.reshape(num_blocks, BLOCK)
    end_state, outputs = lax.scan(
        jax.checkpoint(make_step(key_gain, head_width)),
        start_state,
        (to_blocks(q_rows), to_blocks(k_rows), to_blocks(v_rows), gate_blocks, flag_blocks),
    )
    return (outputs.reshape(num_rows, head_count * head_width), end_state)


def shards(queries, keys_raw, values, gates, lengths, key_gain, cotangent):
    tok_rows = queries.shape[1]
    head_count = key_gain.shape[0]
    head_width = key_gain.shape[1]
    flags = start_flags(lengths[0], lax.axis_index("ctx") * tok_rows, tok_rows)
    q_rows, k_rows, v_rows, gate_rows = (queries[0], keys_raw[0], values[0], gates[0])
    segment = jnp.cumsum(flags)
    opened = (segment == 0).astype(jnp.float32)
    tail_mask = (segment == segment[-1]).astype(jnp.float32)
    cum_decay = jnp.cumsum(gate_rows, axis=1)
    shard_decay = jnp.exp(cum_decay[:, -1]) * opened[-1]
    to_end = jnp.exp(cum_decay[:, -1:] - cum_decay) * tail_mask[None, :]
    k_bf = (
        k_rows.reshape(tok_rows, head_count, head_width).astype(jnp.float32) * key_gain[None]
    ).astype(jnp.bfloat16)
    k_float = lax.optimization_barrier(k_bf).astype(jnp.float32)
    v_float = v_rows.reshape(tok_rows, head_count, head_width).astype(jnp.float32)
    local_end = jnp.einsum(
        "shd,she->hde", k_float * to_end.T[:, :, None], v_float, precision=PRECISE
    )
    ctx_size = lax.axis_size("ctx")
    local_grad = local_incoming_grad(q_rows, cotangent[0], cum_decay, opened, head_count, head_width)
    state_in, later_grad = both_scans_kernel(shard_decay, local_end, local_grad, ctx_size)

    def forward(q_part, k_part, v_part, gate_part, gain_part):
        return run_blocks(q_part, k_part, v_part, gate_part, flags, gain_part, state_in)

    (primal, end_state), pullback = jax.vjp(forward, q_rows, k_rows, v_rows, gate_rows, key_gain)
    cot_float = cotangent[0].astype(jnp.float32)
    grad_q, grad_k, grad_v, grad_a, gain_term = pullback((cot_float, later_grad))
    grad_gain = gain_sum(gain_term, ctx_size)
    return (
        primal.astype(jnp.bfloat16)[None],
        grad_q[None],
        grad_k[None],
        grad_v[None],
        grad_a[None],
        grad_gain,
    )


def solution(mesh):
    placed = (
        P("dp", "ctx", "head"),
        P("dp", "ctx", "head"),
        P("dp", "ctx", "head"),
        P("dp", "head", "ctx"),
        P("dp", None),
        P("head", None),
        P("dp", "ctx", "head"),
    )
    return jax.shard_map(
        shards,
        mesh=mesh,
        in_specs=placed,
        out_specs=(
            P("dp", "ctx", "head"),
            P("dp", "ctx", "head"),
            P("dp", "ctx", "head"),
            P("dp", "ctx", "head"),
            P("dp", "head", "ctx"),
            P("head", "dp"),
        ),
        check_vma=False,
    )
```

```python
import jax
import jax.numpy as jnp
from jax import lax
from jax.sharding import PartitionSpec as P
from jax.experimental import pallas as pl
from jax.experimental.pallas import tpu as pltpu

BLOCK = 512


PRECISE = lax.Precision.HIGH


def passed_along(value, axis, steps):
    count = lax.axis_size(axis)
    first, last = (max(0, -steps), min(count, count - steps))
    return lax.ppermute(value, axis, [(source, source + steps) for source in range(first, last)])


def local_incoming_grad(q_rows, cot_rows, cum_decay, opened, head_count, head_width):
    tok_rows = q_rows.shape[0]
    factor = jnp.exp(cum_decay) * opened[None, :]
    weighted = (
        q_rows.reshape(tok_rows, head_count, head_width).astype(jnp.float32)
        * head_width ** (-0.5)
        * factor.T[:, :, None]
    )
    cot_float = cot_rows.astype(jnp.float32)
    return jnp.einsum(
        "thd,the->hde",
        weighted,
        cot_float.reshape(tok_rows, head_count, head_width),
        precision=PRECISE,
    )


def pack(decay, term):
    lane = jnp.broadcast_to(decay[:, None, None], (term.shape[0], 1, term.shape[2]))
    return jnp.concatenate([term, lane], axis=1)


def both_scans(decay, fwd_term, bwd_term, count):
    rows = fwd_term.shape[1]
    scans = []
    for term in (fwd_term, bwd_term):
        scans.append([decay, term, jnp.ones_like(decay), jnp.zeros_like(term)])
    shift = 1
    while shift < count:
        got = [
            passed_along(pack(agg_a, agg_b), "ctx", shift * sign)
            for (agg_a, agg_b, _, _), sign in zip(scans, (1, -1))
        ]
        for index, received in enumerate(got):
            agg_a, agg_b, ex_a, ex_b = scans[index]
            r_b, r_a = received[:, :rows], received[:, rows, 0]
            ex_b = ex_a[:, None, None] * r_b + ex_b
            ex_a = ex_a * r_a
            agg_b = agg_a[:, None, None] * r_b + agg_b
            agg_a = agg_a * r_a
            scans[index] = [agg_a, agg_b, ex_a, ex_b]
        shift *= 2
    return scans[0][3], scans[1][3]


def gain_sum_kernel(part_ref, total_ref, pair_slot, near, far, pair_sem, send_sem, recv_sem):
    group = near.shape[0]
    outer = far.shape[0]
    me = lax.axis_index("ctx")
    row, col = lax.axis_index("dp"), lax.axis_index("head")
    other = 1 - row
    inner, upper = me % group, me // group

    def near_peer(index):
        return upper * group + index

    def far_peer(index):
        return index * group + inner

    def device(index):
        return (row, index, col)

    barrier = pltpu.get_barrier_semaphore()
    pl.semaphore_signal(
        barrier, inc=1, device_id=(other, me, col), device_id_type=pl.DeviceIdType.MESH
    )
    for step in range(1, group):
        pl.semaphore_signal(
            barrier, inc=1, device_id=device(near_peer((inner + step) % group)),
            device_id_type=pl.DeviceIdType.MESH,
        )
    for step in range(1, outer):
        pl.semaphore_signal(
            barrier, inc=1, device_id=device(far_peer((upper + step) % outer)),
            device_id_type=pl.DeviceIdType.MESH,
        )
    pl.semaphore_wait(barrier, group + outer - 1)

    pair = pltpu.make_async_remote_copy(
        src_ref=part_ref.at[other],
        dst_ref=pair_slot,
        send_sem=pair_sem.at[0],
        recv_sem=pair_sem.at[1],
        device_id=(other, me, col),
        device_id_type=pl.DeviceIdType.MESH,
    )
    pair.start()
    pair.wait_send()
    pair.wait_recv()
    near[inner] = part_ref[row] + pair_slot[...]

    for level, (slots, size, position, peer_at) in enumerate(
        ((near, group, inner, near_peer), (far, outer, upper, far_peer))
    ):
        if level == 1:
            total = near[0]
            for index in range(1, group):
                total = total + near[index]
            far[upper] = total
        copies = []
        for step in range(1, size):
            peer = peer_at((position + step) % size)
            copy = pltpu.make_async_remote_copy(
                src_ref=slots.at[position],
                dst_ref=slots.at[position],
                send_sem=send_sem.at[level, (position + step) % size],
                recv_sem=recv_sem.at[level, position],
                device_id=device(peer),
                device_id_type=pl.DeviceIdType.MESH,
            )
            copy.start()
            copies.append(copy)
        for step in range(1, size):
            copies[step - 1].wait_send()
            source = (position + size - step) % size
            pltpu.make_async_remote_copy(
                src_ref=slots.at[source],
                dst_ref=slots.at[source],
                send_sem=send_sem.at[level, source],
                recv_sem=recv_sem.at[level, source],
                device_id=device(peer_at(source)),
                device_id_type=pl.DeviceIdType.MESH,
            ).wait_recv()
    total = far[0]
    for index in range(1, outer):
        total = total + far[index]
    total_ref[...] = total


def gain_sum(part, count):
    heads, width = part.shape
    halves = part.reshape(heads, 2, width // 2).transpose(1, 0, 2)
    shape = halves.shape[1:]
    group = 4 if count % 4 == 0 else count
    outer = count // group
    return pl.pallas_call(
        gain_sum_kernel,
        out_shape=jax.ShapeDtypeStruct(shape, part.dtype),
        in_specs=[pl.BlockSpec(memory_space=pltpu.VMEM)],
        out_specs=pl.BlockSpec(memory_space=pltpu.VMEM),
        scratch_shapes=[
            pltpu.VMEM(shape, part.dtype),
            pltpu.VMEM((group,) + shape, part.dtype),
            pltpu.VMEM((outer,) + shape, part.dtype),
            pltpu.SemaphoreType.DMA((2,)),
            pltpu.SemaphoreType.DMA((2, max(group, outer))),
            pltpu.SemaphoreType.DMA((2, max(group, outer))),
        ],
        compiler_params=pltpu.CompilerParams(collective_id=0, has_side_effects=True),
    )(halves)


def scan_kernel(fwd_ref, bwd_ref, fwd_out, bwd_out, aggs, exs, slots, send_sem, recv_sem):
    count = lax.axis_size("ctx")
    me = lax.axis_index("ctx")
    row, col = lax.axis_index("dp"), lax.axis_index("head")
    rows = fwd_out.shape[1]
    shifts = []
    shift = 1
    while shift < count:
        shifts.append(shift)
        shift *= 2

    def device(index):
        return (row, index, col)

    barrier = pltpu.get_barrier_semaphore()
    for shift in shifts:
        for peer, present in ((me + shift, me + shift < count), (me - shift, me >= shift)):
            @pl.when(present)
            def _():
                pl.semaphore_signal(
                    barrier, inc=1, device_id=device(peer), device_id_type=pl.DeviceIdType.MESH
                )

    def at_least(bound):
        span = (count - 1) // bound + 1
        return (me // bound + span - 1) // span

    peers = 0
    for shift in shifts:
        peers = peers + at_least(shift) + 1 - at_least(count - shift)
    pl.semaphore_wait(barrier, peers)

    aggs[0] = fwd_ref[...]
    aggs[1] = bwd_ref[...]
    exs[...] = jnp.zeros_like(exs)
    exs[:, :, rows:, :] = jnp.ones_like(exs[:, :, rows:, :])

    for round_index, shift in enumerate(shifts):
        sends = (me + shift < count, me >= shift)
        targets = (me + shift, me - shift)
        sources = (me - shift, me + shift)

        def copy_of(side, peer):
            return pltpu.make_async_remote_copy(
                src_ref=aggs.at[side],
                dst_ref=slots.at[side, round_index],
                send_sem=send_sem.at[side, round_index],
                recv_sem=recv_sem.at[side, round_index],
                device_id=device(peer),
                device_id_type=pl.DeviceIdType.MESH,
            )

        for side in range(2):
            @pl.when(sends[side])
            def _():
                copy_of(side, targets[side]).start()

        for side in range(2):
            @pl.when(sends[side])
            def _():
                copy_of(side, targets[side]).wait_send()

        for side in range(2):
            @pl.when(sends[1 - side])
            def _():
                copy_of(side, sources[side]).wait_recv()
                got = slots[side, round_index]
                ex = exs[side]
                agg = aggs[side]
                ex_a = ex[:, rows:rows + 1, :]
                agg_a = agg[:, rows:rows + 1, :]
                exs[side, :, :rows, :] = ex_a * got[:, :rows, :] + ex[:, :rows, :]
                exs[side, :, rows:, :] = ex[:, rows:, :] * got[:, rows:, :]
                aggs[side, :, :rows, :] = agg_a * got[:, :rows, :] + agg[:, :rows, :]
                aggs[side, :, rows:, :] = agg[:, rows:, :] * got[:, rows:, :]

    fwd_out[...] = exs[0, :, :rows, :]
    bwd_out[...] = exs[1, :, :rows, :]


def both_scans_kernel(decay, fwd_term, bwd_term, count):
    heads, rows, width = fwd_term.shape
    rounds = max(1, (count - 1).bit_length())
    lane = jnp.broadcast_to(decay[:, None, None], (heads, 8, width))
    fwd = jnp.concatenate([fwd_term, lane], axis=1)
    bwd = jnp.concatenate([bwd_term, lane], axis=1)
    packed = fwd.shape
    out = jax.ShapeDtypeStruct(fwd_term.shape, jnp.float32)
    return pl.pallas_call(
        scan_kernel,
        out_shape=(out, out),
        in_specs=[pl.BlockSpec(memory_space=pltpu.VMEM)] * 2,
        out_specs=(pl.BlockSpec(memory_space=pltpu.VMEM),) * 2,
        scratch_shapes=[
            pltpu.VMEM((2,) + packed, jnp.float32),
            pltpu.VMEM((2,) + packed, jnp.float32),
            pltpu.VMEM((2, rounds) + packed, jnp.float32),
            pltpu.SemaphoreType.DMA((2, rounds)),
            pltpu.SemaphoreType.DMA((2, rounds)),
        ],
        compiler_params=pltpu.CompilerParams(collective_id=1, has_side_effects=True),
    )(fwd, bwd)


def start_flags(doc_lengths, first_pos, num_rows):
    starts = jnp.cumsum(doc_lengths, dtype=jnp.int32) - doc_lengths
    positions = first_pos + jnp.arange(num_rows, dtype=jnp.int32)
    matches = jnp.any(positions[:, None] == starts[None, :], axis=1)
    return matches.astype(jnp.float32)


def make_step(key_gain, head_width):
    q_scale = head_width ** (-0.5)

    def block_step(carried, inputs):
        q_block, k_block, v_block, gate_block, flag_block = inputs
        k_bf = (k_block.astype(jnp.float32) * key_gain[None]).astype(jnp.bfloat16)
        q_float = q_block.astype(jnp.float32) * q_scale
        k_float = lax.optimization_barrier(k_bf).astype(jnp.float32)
        v_float = v_block.astype(jnp.float32)
        segment = jnp.cumsum(flag_block)
        positions = jnp.arange(flag_block.shape[0])
        same_doc = (segment[:, None] == segment[None, :]) & (
            positions[:, None] >= positions[None, :]
        )
        cum_decay = jnp.cumsum(gate_block, axis=1)
        exponent = cum_decay[:, :, None] - cum_decay[:, None, :]
        decays = jnp.where(same_doc[None], jnp.exp(jnp.where(same_doc[None], exponent, 0.0)), 0.0)
        scores = jnp.einsum("thd,shd->hts", q_block, k_bf, preferred_element_type=jnp.float32)
        weights = (scores * q_scale * decays).astype(jnp.bfloat16)
        within = jnp.einsum("hts,she->the", weights, v_block, preferred_element_type=jnp.float32)
        opened = (segment == 0).astype(cum_decay.dtype)
        carry_in = jnp.exp(cum_decay) * opened[None, :]
        across = (
            jnp.einsum("thd,hde->the", q_float, carried, precision=PRECISE) * carry_in.T[:, :, None]
        )
        tail_mask = (segment == segment[-1]).astype(cum_decay.dtype)
        to_end = jnp.exp(cum_decay[:, -1:] - cum_decay) * tail_mask[None, :]
        written = jnp.einsum(
            "shd,she->hde", k_float * to_end.T[:, :, None], v_float, precision=PRECISE
        )
        end_state = carried * carry_in[:, -1][:, None, None] + written
        return (end_state, within + across)

    return block_step


def run_blocks(q_rows, k_rows, v_rows, gate_rows, flags, key_gain, start_state):
    num_rows = q_rows.shape[0]
    head_count = key_gain.shape[0]
    head_width = key_gain.shape[1]
    num_blocks = num_rows // BLOCK

    def to_blocks(tensor):
        return tensor.reshape(num_blocks, BLOCK, head_count, head_width)

    gate_blocks = gate_rows.reshape(head_count, num_blocks, BLOCK).transpose(1, 0, 2)
    flag_blocks = flags.reshape(num_blocks, BLOCK)
    end_state, outputs = lax.scan(
        jax.checkpoint(make_step(key_gain, head_width)),
        start_state,
        (to_blocks(q_rows), to_blocks(k_rows), to_blocks(v_rows), gate_blocks, flag_blocks),
    )
    return (outputs.reshape(num_rows, head_count * head_width), end_state)


def shards(queries, keys_raw, values, gates, lengths, key_gain, cotangent):
    tok_rows = queries.shape[1]
    head_count = key_gain.shape[0]
    head_width = key_gain.shape[1]
    flags = start_flags(lengths[0], lax.axis_index("ctx") * tok_rows, tok_rows)
    q_rows, k_rows, v_rows, gate_rows = (queries[0], keys_raw[0], values[0], gates[0])
    segment = jnp.cumsum(flags)
    opened = (segment == 0).astype(jnp.float32)
    tail_mask = (segment == segment[-1]).astype(jnp.float32)
    cum_decay = jnp.cumsum(gate_rows, axis=1)
    shard_decay = jnp.exp(cum_decay[:, -1]) * opened[-1]
    to_end = jnp.exp(cum_decay[:, -1:] - cum_decay) * tail_mask[None, :]
    k_bf = (
        k_rows.reshape(tok_rows, head_count, head_width).astype(jnp.float32) * key_gain[None]
    ).astype(jnp.bfloat16)
    k_float = lax.optimization_barrier(k_bf).astype(jnp.float32)
    v_float = v_rows.reshape(tok_rows, head_count, head_width).astype(jnp.float32)
    local_end = jnp.einsum(
        "shd,she->hde", k_float * to_end.T[:, :, None], v_float, precision=PRECISE
    )
    ctx_size = lax.axis_size("ctx")
    local_grad = local_incoming_grad(q_rows, cotangent[0], cum_decay, opened, head_count, head_width)
    state_in, later_grad = both_scans_kernel(shard_decay, local_end, local_grad, ctx_size)

    def forward(q_part, k_part, v_part, gate_part, gain_part):
        return run_blocks(q_part, k_part, v_part, gate_part, flags, gain_part, state_in)

    (primal, end_state), pullback = jax.vjp(forward, q_rows, k_rows, v_rows, gate_rows, key_gain)
    cot_float = cotangent[0].astype(jnp.float32)
    grad_q, grad_k, grad_v, grad_a, gain_term = pullback((cot_float, later_grad))
    grad_gain = gain_sum(gain_term, ctx_size)
    return (
        primal.astype(jnp.bfloat16)[None],
        grad_q[None],
        grad_k[None],
        grad_v[None],
        grad_a[None],
        grad_gain,
    )


def solution(mesh):
    placed = (
        P("dp", "ctx", "head"),
        P("dp", "ctx", "head"),
        P("dp", "ctx", "head"),
        P("dp", "head", "ctx"),
        P("dp", None),
        P("head", None),
        P("dp", "ctx", "head"),
    )
    return jax.shard_map(
        shards,
        mesh=mesh,
        in_specs=placed,
        out_specs=(
            P("dp", "ctx", "head"),
            P("dp", "ctx", "head"),
            P("dp", "ctx", "head"),
            P("dp", "ctx", "head"),
            P("dp", "head", "ctx"),
            P("head", "dp"),
        ),
        check_vma=False,
    )
```

```python
import jax
import jax.numpy as jnp
from jax import lax
from jax.sharding import PartitionSpec as P
from jax.experimental import pallas as pl
from jax.experimental.pallas import tpu as pltpu

BLOCK = 512


PRECISE = lax.Precision.DEFAULT


def passed_along(value, axis, steps):
    count = lax.axis_size(axis)
    first, last = (max(0, -steps), min(count, count - steps))
    return lax.ppermute(value, axis, [(source, source + steps) for source in range(first, last)])


def local_incoming_grad(q_rows, cot_rows, cum_decay, opened, head_count, head_width):
    tok_rows = q_rows.shape[0]
    factor = jnp.exp(cum_decay) * opened[None, :]
    weighted = (
        q_rows.reshape(tok_rows, head_count, head_width).astype(jnp.float32)
        * head_width ** (-0.5)
        * factor.T[:, :, None]
    )
    cot_float = cot_rows.astype(jnp.float32)
    return jnp.einsum(
        "thd,the->hde",
        weighted,
        cot_float.reshape(tok_rows, head_count, head_width),
        precision=PRECISE,
    )


def pack(decay, term):
    lane = jnp.broadcast_to(decay[:, None, None], (term.shape[0], 1, term.shape[2]))
    return jnp.concatenate([term, lane], axis=1)


def both_scans(decay, fwd_term, bwd_term, count):
    rows = fwd_term.shape[1]
    scans = []
    for term in (fwd_term, bwd_term):
        scans.append([decay, term, jnp.ones_like(decay), jnp.zeros_like(term)])
    shift = 1
    while shift < count:
        got = [
            passed_along(pack(agg_a, agg_b), "ctx", shift * sign)
            for (agg_a, agg_b, _, _), sign in zip(scans, (1, -1))
        ]
        for index, received in enumerate(got):
            agg_a, agg_b, ex_a, ex_b = scans[index]
            r_b, r_a = received[:, :rows], received[:, rows, 0]
            ex_b = ex_a[:, None, None] * r_b + ex_b
            ex_a = ex_a * r_a
            agg_b = agg_a[:, None, None] * r_b + agg_b
            agg_a = agg_a * r_a
            scans[index] = [agg_a, agg_b, ex_a, ex_b]
        shift *= 2
    return scans[0][3], scans[1][3]


def gain_sum_kernel(part_ref, total_ref, pair_slot, slots, pair_sem, send_sem, recv_sem):
    count = slots.shape[0]
    me = lax.axis_index("ctx")
    row, col = lax.axis_index("dp"), lax.axis_index("head")
    other = 1 - row

    def peer_of(step):
        return lax.rem(me + step, count)

    barrier = pltpu.get_barrier_semaphore()
    pl.semaphore_signal(
        barrier, inc=1, device_id=(other, me, col), device_id_type=pl.DeviceIdType.MESH
    )
    for step in range(1, count):
        pl.semaphore_signal(
            barrier, inc=1, device_id=(row, peer_of(step), col), device_id_type=pl.DeviceIdType.MESH
        )
    pl.semaphore_wait(barrier, count)

    pair = pltpu.make_async_remote_copy(
        src_ref=part_ref.at[other],
        dst_ref=pair_slot,
        send_sem=pair_sem.at[0],
        recv_sem=pair_sem.at[1],
        device_id=(other, me, col),
        device_id_type=pl.DeviceIdType.MESH,
    )
    pair.start()
    pair.wait_send()
    pair.wait_recv()
    slots[me] = part_ref[row] + pair_slot[...]

    copies = []
    for step in range(1, count):
        peer = peer_of(step)
        copy = pltpu.make_async_remote_copy(
            src_ref=slots.at[me],
            dst_ref=slots.at[me],
            send_sem=send_sem.at[peer],
            recv_sem=recv_sem.at[me],
            device_id=(row, peer, col),
            device_id_type=pl.DeviceIdType.MESH,
        )
        copy.start()
        copies.append(copy)
    for step in range(1, count):
        copies[step - 1].wait_send()
        source = lax.rem(me + count - step, count)
        pltpu.make_async_remote_copy(
            src_ref=slots.at[source],
            dst_ref=slots.at[source],
            send_sem=send_sem.at[source],
            recv_sem=recv_sem.at[source],
            device_id=(row, source, col),
            device_id_type=pl.DeviceIdType.MESH,
        ).wait_recv()
    total = slots[0]
    for index in range(1, count):
        total = total + slots[index]
    total_ref[...] = total


def gain_sum(part, count):
    heads, width = part.shape
    halves = part.reshape(heads, 2, width // 2).transpose(1, 0, 2)
    shape = halves.shape[1:]
    return pl.pallas_call(
        gain_sum_kernel,
        out_shape=jax.ShapeDtypeStruct(shape, part.dtype),
        in_specs=[pl.BlockSpec(memory_space=pltpu.VMEM)],
        out_specs=pl.BlockSpec(memory_space=pltpu.VMEM),
        scratch_shapes=[
            pltpu.VMEM(shape, part.dtype),
            pltpu.VMEM((count,) + shape, part.dtype),
            pltpu.SemaphoreType.DMA((2,)),
            pltpu.SemaphoreType.DMA((count,)),
            pltpu.SemaphoreType.DMA((count,)),
        ],
        compiler_params=pltpu.CompilerParams(collective_id=0, has_side_effects=True),
    )(halves)


def scan_kernel(fwd_ref, bwd_ref, fwd_out, bwd_out, aggs, exs, slots, send_sem, recv_sem):
    count = lax.axis_size("ctx")
    me = lax.axis_index("ctx")
    row, col = lax.axis_index("dp"), lax.axis_index("head")
    rows = fwd_out.shape[1]
    shifts = []
    shift = 1
    while shift < count:
        shifts.append(shift)
        shift *= 2

    def device(index):
        return (row, index, col)

    barrier = pltpu.get_barrier_semaphore()
    for shift in shifts:
        for peer, present in ((me + shift, me + shift < count), (me - shift, me >= shift)):
            @pl.when(present)
            def _():
                pl.semaphore_signal(
                    barrier, inc=1, device_id=device(peer), device_id_type=pl.DeviceIdType.MESH
                )

    def at_least(bound):
        span = (count - 1) // bound + 1
        return (me // bound + span - 1) // span

    peers = 0
    for shift in shifts:
        peers = peers + at_least(shift) + 1 - at_least(count - shift)
    pl.semaphore_wait(barrier, peers)

    aggs[0] = fwd_ref[...]
    aggs[1] = bwd_ref[...]
    exs[...] = jnp.zeros_like(exs)
    exs[:, :, rows:, :] = jnp.ones_like(exs[:, :, rows:, :])

    for round_index, shift in enumerate(shifts):
        sends = (me + shift < count, me >= shift)
        targets = (me + shift, me - shift)
        sources = (me - shift, me + shift)

        def copy_of(side, peer):
            return pltpu.make_async_remote_copy(
                src_ref=aggs.at[side],
                dst_ref=slots.at[side, round_index],
                send_sem=send_sem.at[side, round_index],
                recv_sem=recv_sem.at[side, round_index],
                device_id=device(peer),
                device_id_type=pl.DeviceIdType.MESH,
            )

        for side in range(2):
            @pl.when(sends[side])
            def _():
                copy_of(side, targets[side]).start()

        for side in range(2):
            @pl.when(sends[side])
            def _():
                copy_of(side, targets[side]).wait_send()

        for side in range(2):
            @pl.when(sends[1 - side])
            def _():
                copy_of(side, sources[side]).wait_recv()
                got = slots[side, round_index]
                ex = exs[side]
                agg = aggs[side]
                ex_a = ex[:, rows:rows + 1, :]
                agg_a = agg[:, rows:rows + 1, :]
                exs[side, :, :rows, :] = ex_a * got[:, :rows, :] + ex[:, :rows, :]
                exs[side, :, rows:, :] = ex[:, rows:, :] * got[:, rows:, :]
                aggs[side, :, :rows, :] = agg_a * got[:, :rows, :] + agg[:, :rows, :]
                aggs[side, :, rows:, :] = agg[:, rows:, :] * got[:, rows:, :]

    fwd_out[...] = exs[0, :, :rows, :]
    bwd_out[...] = exs[1, :, :rows, :]


def both_scans_kernel(decay, fwd_term, bwd_term, count):
    heads, rows, width = fwd_term.shape
    rounds = max(1, (count - 1).bit_length())
    lane = jnp.broadcast_to(decay[:, None, None], (heads, 8, width))
    fwd = jnp.concatenate([fwd_term, lane], axis=1)
    bwd = jnp.concatenate([bwd_term, lane], axis=1)
    packed = fwd.shape
    out = jax.ShapeDtypeStruct(fwd_term.shape, jnp.float32)
    return pl.pallas_call(
        scan_kernel,
        out_shape=(out, out),
        in_specs=[pl.BlockSpec(memory_space=pltpu.VMEM)] * 2,
        out_specs=(pl.BlockSpec(memory_space=pltpu.VMEM),) * 2,
        scratch_shapes=[
            pltpu.VMEM((2,) + packed, jnp.float32),
            pltpu.VMEM((2,) + packed, jnp.float32),
            pltpu.VMEM((2, rounds) + packed, jnp.float32),
            pltpu.SemaphoreType.DMA((2, rounds)),
            pltpu.SemaphoreType.DMA((2, rounds)),
        ],
        compiler_params=pltpu.CompilerParams(collective_id=1, has_side_effects=True),
    )(fwd, bwd)


def start_flags(doc_lengths, first_pos, num_rows):
    starts = jnp.cumsum(doc_lengths, dtype=jnp.int32) - doc_lengths
    positions = first_pos + jnp.arange(num_rows, dtype=jnp.int32)
    matches = jnp.any(positions[:, None] == starts[None, :], axis=1)
    return matches.astype(jnp.float32)


def make_step(key_gain, head_width):
    q_scale = head_width ** (-0.5)

    def block_step(carried, inputs):
        q_block, k_block, v_block, gate_block, flag_block = inputs
        k_bf = (k_block.astype(jnp.float32) * key_gain[None]).astype(jnp.bfloat16)
        q_float = q_block.astype(jnp.float32) * q_scale
        k_float = lax.optimization_barrier(k_bf).astype(jnp.float32)
        v_float = v_block.astype(jnp.float32)
        segment = jnp.cumsum(flag_block)
        positions = jnp.arange(flag_block.shape[0])
        same_doc = (segment[:, None] == segment[None, :]) & (
            positions[:, None] >= positions[None, :]
        )
        cum_decay = jnp.cumsum(gate_block, axis=1)
        exponent = cum_decay[:, :, None] - cum_decay[:, None, :]
        decays = jnp.where(same_doc[None], jnp.exp(jnp.where(same_doc[None], exponent, 0.0)), 0.0)
        scores = jnp.einsum("thd,shd->hts", q_block, k_bf, preferred_element_type=jnp.float32)
        weights = (scores * q_scale * decays).astype(jnp.bfloat16)
        within = jnp.einsum("hts,she->the", weights, v_block, preferred_element_type=jnp.float32)
        opened = (segment == 0).astype(cum_decay.dtype)
        carry_in = jnp.exp(cum_decay) * opened[None, :]
        across = (
            jnp.einsum("thd,hde->the", q_float, carried, precision=PRECISE) * carry_in.T[:, :, None]
        )
        tail_mask = (segment == segment[-1]).astype(cum_decay.dtype)
        to_end = jnp.exp(cum_decay[:, -1:] - cum_decay) * tail_mask[None, :]
        written = jnp.einsum(
            "shd,she->hde", k_float * to_end.T[:, :, None], v_float, precision=PRECISE
        )
        end_state = carried * carry_in[:, -1][:, None, None] + written
        return (end_state, within + across)

    return block_step


def run_blocks(q_rows, k_rows, v_rows, gate_rows, flags, key_gain, start_state):
    num_rows = q_rows.shape[0]
    head_count = key_gain.shape[0]
    head_width = key_gain.shape[1]
    num_blocks = num_rows // BLOCK

    def to_blocks(tensor):
        return tensor.reshape(num_blocks, BLOCK, head_count, head_width)

    gate_blocks = gate_rows.reshape(head_count, num_blocks, BLOCK).transpose(1, 0, 2)
    flag_blocks = flags.reshape(num_blocks, BLOCK)
    end_state, outputs = lax.scan(
        jax.checkpoint(make_step(key_gain, head_width)),
        start_state,
        (to_blocks(q_rows), to_blocks(k_rows), to_blocks(v_rows), gate_blocks, flag_blocks),
    )
    return (outputs.reshape(num_rows, head_count * head_width), end_state)


def shards(queries, keys_raw, values, gates, lengths, key_gain, cotangent):
    tok_rows = queries.shape[1]
    head_count = key_gain.shape[0]
    head_width = key_gain.shape[1]
    flags = start_flags(lengths[0], lax.axis_index("ctx") * tok_rows, tok_rows)
    q_rows, k_rows, v_rows, gate_rows = (queries[0], keys_raw[0], values[0], gates[0])
    segment = jnp.cumsum(flags)
    opened = (segment == 0).astype(jnp.float32)
    tail_mask = (segment == segment[-1]).astype(jnp.float32)
    cum_decay = jnp.cumsum(gate_rows, axis=1)
    shard_decay = jnp.exp(cum_decay[:, -1]) * opened[-1]
    to_end = jnp.exp(cum_decay[:, -1:] - cum_decay) * tail_mask[None, :]
    k_bf = (
        k_rows.reshape(tok_rows, head_count, head_width).astype(jnp.float32) * key_gain[None]
    ).astype(jnp.bfloat16)
    k_float = lax.optimization_barrier(k_bf).astype(jnp.float32)
    v_float = v_rows.reshape(tok_rows, head_count, head_width).astype(jnp.float32)
    local_end = jnp.einsum(
        "shd,she->hde", k_float * to_end.T[:, :, None], v_float, precision=PRECISE
    )
    ctx_size = lax.axis_size("ctx")
    local_grad = local_incoming_grad(q_rows, cotangent[0], cum_decay, opened, head_count, head_width)
    state_in, later_grad = both_scans_kernel(shard_decay, local_end, local_grad, ctx_size)

    def forward(q_part, k_part, v_part, gate_part, gain_part):
        return run_blocks(q_part, k_part, v_part, gate_part, flags, gain_part, state_in)

    (primal, end_state), pullback = jax.vjp(forward, q_rows, k_rows, v_rows, gate_rows, key_gain)
    cot_float = cotangent[0].astype(jnp.float32)
    grad_q, grad_k, grad_v, grad_a, gain_term = pullback((cot_float, later_grad))
    grad_gain = gain_sum(gain_term, ctx_size)
    return (
        primal.astype(jnp.bfloat16)[None],
        grad_q[None],
        grad_k[None],
        grad_v[None],
        grad_a[None],
        grad_gain,
    )


def solution(mesh):
    placed = (
        P("dp", "ctx", "head"),
        P("dp", "ctx", "head"),
        P("dp", "ctx", "head"),
        P("dp", "head", "ctx"),
        P("dp", None),
        P("head", None),
        P("dp", "ctx", "head"),
    )
    return jax.shard_map(
        shards,
        mesh=mesh,
        in_specs=placed,
        out_specs=(
            P("dp", "ctx", "head"),
            P("dp", "ctx", "head"),
            P("dp", "ctx", "head"),
            P("dp", "ctx", "head"),
            P("dp", "head", "ctx"),
            P("head", "dp"),
        ),
        check_vma=False,
    )
```

```python
import jax
import jax.numpy as jnp
from jax import lax
from jax.sharding import PartitionSpec as P
from jax.experimental import pallas as pl
from jax.experimental.pallas import tpu as pltpu

BLOCK = 512


PRECISE = lax.Precision.HIGH


def passed_along(value, axis, steps):
    count = lax.axis_size(axis)
    first, last = (max(0, -steps), min(count, count - steps))
    return lax.ppermute(value, axis, [(source, source + steps) for source in range(first, last)])


def local_incoming_grad(q_rows, cot_rows, cum_decay, opened, head_count, head_width):
    tok_rows = q_rows.shape[0]
    factor = jnp.exp(cum_decay) * opened[None, :]
    weighted = (
        q_rows.reshape(tok_rows, head_count, head_width).astype(jnp.float32)
        * head_width ** (-0.5)
        * factor.T[:, :, None]
    )
    cot_float = cot_rows.astype(jnp.float32)
    return jnp.einsum(
        "thd,the->hde",
        weighted,
        cot_float.reshape(tok_rows, head_count, head_width),
        precision=PRECISE,
    )


def pack(decay, term):
    lane = jnp.broadcast_to(decay[:, None, None], (term.shape[0], 1, term.shape[2]))
    return jnp.concatenate([term, lane], axis=1)


def both_scans(decay, fwd_term, bwd_term, count):
    rows = fwd_term.shape[1]
    scans = []
    for term in (fwd_term, bwd_term):
        scans.append([decay, term, jnp.ones_like(decay), jnp.zeros_like(term)])
    shift = 1
    while shift < count:
        got = [
            passed_along(pack(agg_a, agg_b), "ctx", shift * sign)
            for (agg_a, agg_b, _, _), sign in zip(scans, (1, -1))
        ]
        for index, received in enumerate(got):
            agg_a, agg_b, ex_a, ex_b = scans[index]
            r_b, r_a = received[:, :rows], received[:, rows, 0]
            ex_b = ex_a[:, None, None] * r_b + ex_b
            ex_a = ex_a * r_a
            agg_b = agg_a[:, None, None] * r_b + agg_b
            agg_a = agg_a * r_a
            scans[index] = [agg_a, agg_b, ex_a, ex_b]
        shift *= 2
    return scans[0][3], scans[1][3]


def gain_sum_kernel(part_ref, total_ref, pair_slot, slots, pair_sem, send_sem, recv_sem):
    count = slots.shape[0]
    me = lax.axis_index("ctx")
    row, col = lax.axis_index("dp"), lax.axis_index("head")
    other = 1 - row

    def peer_of(step):
        return lax.rem(me + step, count)

    barrier = pltpu.get_barrier_semaphore()
    pl.semaphore_signal(
        barrier, inc=1, device_id=(other, me, col), device_id_type=pl.DeviceIdType.MESH
    )
    for step in range(1, count):
        pl.semaphore_signal(
            barrier, inc=1, device_id=(row, peer_of(step), col), device_id_type=pl.DeviceIdType.MESH
        )
    pl.semaphore_wait(barrier, count)

    pair = pltpu.make_async_remote_copy(
        src_ref=part_ref.at[other],
        dst_ref=pair_slot,
        send_sem=pair_sem.at[0],
        recv_sem=pair_sem.at[1],
        device_id=(other, me, col),
        device_id_type=pl.DeviceIdType.MESH,
    )
    pair.start()
    pair.wait_send()
    pair.wait_recv()
    slots[me] = part_ref[row] + pair_slot[...]

    copies = []
    for step in range(1, count):
        peer = peer_of(step)
        copy = pltpu.make_async_remote_copy(
            src_ref=slots.at[me],
            dst_ref=slots.at[me],
            send_sem=send_sem.at[peer],
            recv_sem=recv_sem.at[me],
            device_id=(row, peer, col),
            device_id_type=pl.DeviceIdType.MESH,
        )
        copy.start()
        copies.append(copy)
    for step in range(1, count):
        copies[step - 1].wait_send()
        source = lax.rem(me + count - step, count)
        pltpu.make_async_remote_copy(
            src_ref=slots.at[source],
            dst_ref=slots.at[source],
            send_sem=send_sem.at[source],
            recv_sem=recv_sem.at[source],
            device_id=(row, source, col),
            device_id_type=pl.DeviceIdType.MESH,
        ).wait_recv()
    total = slots[0]
    for index in range(1, count):
        total = total + slots[index]
    total_ref[...] = total


def gain_sum(part, count):
    heads, width = part.shape
    halves = part.reshape(heads, 2, width // 2).transpose(1, 0, 2)
    shape = halves.shape[1:]
    return pl.pallas_call(
        gain_sum_kernel,
        out_shape=jax.ShapeDtypeStruct(shape, part.dtype),
        in_specs=[pl.BlockSpec(memory_space=pltpu.VMEM)],
        out_specs=pl.BlockSpec(memory_space=pltpu.VMEM),
        scratch_shapes=[
            pltpu.VMEM(shape, part.dtype),
            pltpu.VMEM((count,) + shape, part.dtype),
            pltpu.SemaphoreType.DMA((2,)),
            pltpu.SemaphoreType.DMA((count,)),
            pltpu.SemaphoreType.DMA((count,)),
        ],
        compiler_params=pltpu.CompilerParams(collective_id=0, has_side_effects=True),
    )(halves)


def scan_kernel(fwd_ref, bwd_ref, fwd_out, bwd_out, aggs, exs, slots, send_sem, recv_sem):
    count = lax.axis_size("ctx")
    me = lax.axis_index("ctx")
    row, col = lax.axis_index("dp"), lax.axis_index("head")
    rows = fwd_out.shape[1]
    shifts = []
    shift = 1
    while shift < count:
        shifts.append(shift)
        shift *= 2

    def device(index):
        return (row, index, col)

    barrier = pltpu.get_barrier_semaphore()
    for shift in shifts:
        for peer, present in ((me + shift, me + shift < count), (me - shift, me >= shift)):
            @pl.when(present)
            def _():
                pl.semaphore_signal(
                    barrier, inc=1, device_id=device(peer), device_id_type=pl.DeviceIdType.MESH
                )

    def at_least(bound):
        span = (count - 1) // bound + 1
        return (me // bound + span - 1) // span

    peers = 0
    for shift in shifts:
        peers = peers + at_least(shift) + 1 - at_least(count - shift)
    pl.semaphore_wait(barrier, peers)

    aggs[0] = fwd_ref[...]
    aggs[1] = bwd_ref[...]
    exs[...] = jnp.zeros_like(exs)
    exs[:, :, rows:, :] = jnp.ones_like(exs[:, :, rows:, :])

    for round_index, shift in enumerate(shifts):
        sends = (me + shift < count, me >= shift)
        targets = (me + shift, me - shift)
        sources = (me - shift, me + shift)

        last = round_index == len(shifts) - 1
        span = pl.ds(0, rows) if last else slice(None)

        def copy_of(side, peer):
            return pltpu.make_async_remote_copy(
                src_ref=aggs.at[side, :, span, :],
                dst_ref=slots.at[side, round_index, :, span, :],
                send_sem=send_sem.at[side, round_index],
                recv_sem=recv_sem.at[side, round_index],
                device_id=device(peer),
                device_id_type=pl.DeviceIdType.MESH,
            )

        for side in range(2):
            @pl.when(sends[side])
            def _():
                copy_of(side, targets[side]).start()

        for side in range(2):
            @pl.when(sends[side])
            def _():
                copy_of(side, targets[side]).wait_send()

        for side in range(2):
            @pl.when(sends[1 - side])
            def _():
                copy_of(side, sources[side]).wait_recv()
                got = slots[side, round_index, :, span, :]
                ex = exs[side]
                agg = aggs[side]
                ex_a = ex[:, rows:rows + 1, :]
                agg_a = agg[:, rows:rows + 1, :]
                exs[side, :, :rows, :] = ex_a * got[:, :rows, :] + ex[:, :rows, :]
                if not last:
                    exs[side, :, rows:, :] = ex[:, rows:, :] * got[:, rows:, :]
                    aggs[side, :, :rows, :] = agg_a * got[:, :rows, :] + agg[:, :rows, :]
                    aggs[side, :, rows:, :] = agg[:, rows:, :] * got[:, rows:, :]

    fwd_out[...] = exs[0, :, :rows, :]
    bwd_out[...] = exs[1, :, :rows, :]


def both_scans_kernel(decay, fwd_term, bwd_term, count):
    heads, rows, width = fwd_term.shape
    rounds = max(1, (count - 1).bit_length())
    lane = jnp.broadcast_to(decay[:, None, None], (heads, 8, width))
    fwd = jnp.concatenate([fwd_term, lane], axis=1)
    bwd = jnp.concatenate([bwd_term, lane], axis=1)
    packed = fwd.shape
    out = jax.ShapeDtypeStruct(fwd_term.shape, jnp.float32)
    return pl.pallas_call(
        scan_kernel,
        out_shape=(out, out),
        in_specs=[pl.BlockSpec(memory_space=pltpu.VMEM)] * 2,
        out_specs=(pl.BlockSpec(memory_space=pltpu.VMEM),) * 2,
        scratch_shapes=[
            pltpu.VMEM((2,) + packed, jnp.float32),
            pltpu.VMEM((2,) + packed, jnp.float32),
            pltpu.VMEM((2, rounds) + packed, jnp.float32),
            pltpu.SemaphoreType.DMA((2, rounds)),
            pltpu.SemaphoreType.DMA((2, rounds)),
        ],
        compiler_params=pltpu.CompilerParams(collective_id=1, has_side_effects=True),
    )(fwd, bwd)


def start_flags(doc_lengths, first_pos, num_rows):
    starts = jnp.cumsum(doc_lengths, dtype=jnp.int32) - doc_lengths
    positions = first_pos + jnp.arange(num_rows, dtype=jnp.int32)
    matches = jnp.any(positions[:, None] == starts[None, :], axis=1)
    return matches.astype(jnp.float32)


def make_step(key_gain, head_width):
    q_scale = head_width ** (-0.5)

    def block_step(carried, inputs):
        q_block, k_block, v_block, gate_block, flag_block = inputs
        k_bf = (k_block.astype(jnp.float32) * key_gain[None]).astype(jnp.bfloat16)
        q_float = q_block.astype(jnp.float32) * q_scale
        k_float = lax.optimization_barrier(k_bf).astype(jnp.float32)
        v_float = v_block.astype(jnp.float32)
        segment = jnp.cumsum(flag_block)
        positions = jnp.arange(flag_block.shape[0])
        same_doc = (segment[:, None] == segment[None, :]) & (
            positions[:, None] >= positions[None, :]
        )
        cum_decay = jnp.cumsum(gate_block, axis=1)
        exponent = cum_decay[:, :, None] - cum_decay[:, None, :]
        decays = jnp.where(same_doc[None], jnp.exp(jnp.where(same_doc[None], exponent, 0.0)), 0.0)
        scores = jnp.einsum("thd,shd->hts", q_block, k_bf, preferred_element_type=jnp.float32)
        weights = (scores * q_scale * decays).astype(jnp.bfloat16)
        within = jnp.einsum("hts,she->the", weights, v_block, preferred_element_type=jnp.float32)
        opened = (segment == 0).astype(cum_decay.dtype)
        carry_in = jnp.exp(cum_decay) * opened[None, :]
        across = (
            jnp.einsum("thd,hde->the", q_float, carried, precision=PRECISE) * carry_in.T[:, :, None]
        )
        tail_mask = (segment == segment[-1]).astype(cum_decay.dtype)
        to_end = jnp.exp(cum_decay[:, -1:] - cum_decay) * tail_mask[None, :]
        written = jnp.einsum(
            "shd,she->hde", k_float * to_end.T[:, :, None], v_float, precision=PRECISE
        )
        end_state = carried * carry_in[:, -1][:, None, None] + written
        return (end_state, within + across)

    return block_step


def run_blocks(q_rows, k_rows, v_rows, gate_rows, flags, key_gain, start_state):
    num_rows = q_rows.shape[0]
    head_count = key_gain.shape[0]
    head_width = key_gain.shape[1]
    num_blocks = num_rows // BLOCK

    def to_blocks(tensor):
        return tensor.reshape(num_blocks, BLOCK, head_count, head_width)

    gate_blocks = gate_rows.reshape(head_count, num_blocks, BLOCK).transpose(1, 0, 2)
    flag_blocks = flags.reshape(num_blocks, BLOCK)
    end_state, outputs = lax.scan(
        jax.checkpoint(make_step(key_gain, head_width)),
        start_state,
        (to_blocks(q_rows), to_blocks(k_rows), to_blocks(v_rows), gate_blocks, flag_blocks),
    )
    return (outputs.reshape(num_rows, head_count * head_width), end_state)


def shards(queries, keys_raw, values, gates, lengths, key_gain, cotangent):
    tok_rows = queries.shape[1]
    head_count = key_gain.shape[0]
    head_width = key_gain.shape[1]
    flags = start_flags(lengths[0], lax.axis_index("ctx") * tok_rows, tok_rows)
    q_rows, k_rows, v_rows, gate_rows = (queries[0], keys_raw[0], values[0], gates[0])
    segment = jnp.cumsum(flags)
    opened = (segment == 0).astype(jnp.float32)
    tail_mask = (segment == segment[-1]).astype(jnp.float32)
    cum_decay = jnp.cumsum(gate_rows, axis=1)
    shard_decay = jnp.exp(cum_decay[:, -1]) * opened[-1]
    to_end = jnp.exp(cum_decay[:, -1:] - cum_decay) * tail_mask[None, :]
    k_bf = (
        k_rows.reshape(tok_rows, head_count, head_width).astype(jnp.float32) * key_gain[None]
    ).astype(jnp.bfloat16)
    k_float = lax.optimization_barrier(k_bf).astype(jnp.float32)
    v_float = v_rows.reshape(tok_rows, head_count, head_width).astype(jnp.float32)
    local_end = jnp.einsum(
        "shd,she->hde", k_float * to_end.T[:, :, None], v_float, precision=PRECISE
    )
    ctx_size = lax.axis_size("ctx")
    local_grad = local_incoming_grad(q_rows, cotangent[0], cum_decay, opened, head_count, head_width)
    state_in, later_grad = both_scans_kernel(shard_decay, local_end, local_grad, ctx_size)

    def forward(q_part, k_part, v_part, gate_part, gain_part):
        return run_blocks(q_part, k_part, v_part, gate_part, flags, gain_part, state_in)

    (primal, end_state), pullback = jax.vjp(forward, q_rows, k_rows, v_rows, gate_rows, key_gain)
    cot_float = cotangent[0].astype(jnp.float32)
    grad_q, grad_k, grad_v, grad_a, gain_term = pullback((cot_float, later_grad))
    grad_gain = gain_sum(gain_term, ctx_size)
    return (
        primal.astype(jnp.bfloat16)[None],
        grad_q[None],
        grad_k[None],
        grad_v[None],
        grad_a[None],
        grad_gain,
    )


def solution(mesh):
    placed = (
        P("dp", "ctx", "head"),
        P("dp", "ctx", "head"),
        P("dp", "ctx", "head"),
        P("dp", "head", "ctx"),
        P("dp", None),
        P("head", None),
        P("dp", "ctx", "head"),
    )
    return jax.shard_map(
        shards,
        mesh=mesh,
        in_specs=placed,
        out_specs=(
            P("dp", "ctx", "head"),
            P("dp", "ctx", "head"),
            P("dp", "ctx", "head"),
            P("dp", "ctx", "head"),
            P("dp", "head", "ctx"),
            P("head", "dp"),
        ),
        check_vma=False,
    )
```

```python
import jax
import jax.numpy as jnp
from jax import lax
from jax.sharding import PartitionSpec as P
from jax.experimental import pallas as pl
from jax.experimental.pallas import tpu as pltpu

BLOCK = 512


PRECISE = lax.Precision.HIGH


def passed_along(value, axis, steps):
    count = lax.axis_size(axis)
    first, last = (max(0, -steps), min(count, count - steps))
    return lax.ppermute(value, axis, [(source, source + steps) for source in range(first, last)])


def local_incoming_grad(q_rows, cot_rows, cum_decay, opened, head_count, head_width):
    tok_rows = q_rows.shape[0]
    factor = jnp.exp(cum_decay) * opened[None, :]
    weighted = (
        q_rows.reshape(tok_rows, head_count, head_width).astype(jnp.float32)
        * head_width ** (-0.5)
        * factor.T[:, :, None]
    )
    cot_float = cot_rows.astype(jnp.float32)
    return jnp.einsum(
        "thd,the->hde",
        weighted,
        cot_float.reshape(tok_rows, head_count, head_width),
        precision=PRECISE,
    )


def pack(decay, term):
    lane = jnp.broadcast_to(decay[:, None, None], (term.shape[0], 1, term.shape[2]))
    return jnp.concatenate([term, lane], axis=1)


def both_scans(decay, fwd_term, bwd_term, count):
    rows = fwd_term.shape[1]
    scans = []
    for term in (fwd_term, bwd_term):
        scans.append([decay, term, jnp.ones_like(decay), jnp.zeros_like(term)])
    shift = 1
    while shift < count:
        got = [
            passed_along(pack(agg_a, agg_b), "ctx", shift * sign)
            for (agg_a, agg_b, _, _), sign in zip(scans, (1, -1))
        ]
        for index, received in enumerate(got):
            agg_a, agg_b, ex_a, ex_b = scans[index]
            r_b, r_a = received[:, :rows], received[:, rows, 0]
            ex_b = ex_a[:, None, None] * r_b + ex_b
            ex_a = ex_a * r_a
            agg_b = agg_a[:, None, None] * r_b + agg_b
            agg_a = agg_a * r_a
            scans[index] = [agg_a, agg_b, ex_a, ex_b]
        shift *= 2
    return scans[0][3], scans[1][3]


def gain_sum_kernel(part_ref, total_ref, pair_slot, slots, pair_sem, send_sem, recv_sem):
    count = slots.shape[0]
    me = lax.axis_index("ctx")
    row, col = lax.axis_index("dp"), lax.axis_index("head")
    other = 1 - row

    def peer_of(step):
        return lax.rem(me + step, count)

    barrier = pltpu.get_barrier_semaphore()
    pl.semaphore_signal(
        barrier, inc=1, device_id=(other, me, col), device_id_type=pl.DeviceIdType.MESH
    )
    for step in range(1, count):
        pl.semaphore_signal(
            barrier, inc=1, device_id=(row, peer_of(step), col), device_id_type=pl.DeviceIdType.MESH
        )
    pl.semaphore_wait(barrier, count)

    pair = pltpu.make_async_remote_copy(
        src_ref=part_ref.at[other],
        dst_ref=pair_slot,
        send_sem=pair_sem.at[0],
        recv_sem=pair_sem.at[1],
        device_id=(other, me, col),
        device_id_type=pl.DeviceIdType.MESH,
    )
    pair.start()
    pair.wait_send()
    pair.wait_recv()
    slots[me] = part_ref[row] + pair_slot[...]

    copies = []
    for step in range(1, count):
        peer = peer_of(step)
        copy = pltpu.make_async_remote_copy(
            src_ref=slots.at[me],
            dst_ref=slots.at[me],
            send_sem=send_sem.at[peer],
            recv_sem=recv_sem.at[me],
            device_id=(row, peer, col),
            device_id_type=pl.DeviceIdType.MESH,
        )
        copy.start()
        copies.append(copy)
    for step in range(1, count):
        copies[step - 1].wait_send()
        source = lax.rem(me + count - step, count)
        pltpu.make_async_remote_copy(
            src_ref=slots.at[source],
            dst_ref=slots.at[source],
            send_sem=send_sem.at[source],
            recv_sem=recv_sem.at[source],
            device_id=(row, source, col),
            device_id_type=pl.DeviceIdType.MESH,
        ).wait_recv()
    total = slots[0]
    for index in range(1, count):
        total = total + slots[index]
    total_ref[...] = total


def gain_sum(part, count):
    heads, width = part.shape
    halves = part.reshape(heads, 2, width // 2).transpose(1, 0, 2)
    shape = halves.shape[1:]
    return pl.pallas_call(
        gain_sum_kernel,
        out_shape=jax.ShapeDtypeStruct(shape, part.dtype),
        in_specs=[pl.BlockSpec(memory_space=pltpu.VMEM)],
        out_specs=pl.BlockSpec(memory_space=pltpu.VMEM),
        scratch_shapes=[
            pltpu.VMEM(shape, part.dtype),
            pltpu.VMEM((count,) + shape, part.dtype),
            pltpu.SemaphoreType.DMA((2,)),
            pltpu.SemaphoreType.DMA((count,)),
            pltpu.SemaphoreType.DMA((count,)),
        ],
        compiler_params=pltpu.CompilerParams(collective_id=0, has_side_effects=True),
    )(halves)


def scan_kernel(fwd_ref, bwd_ref, lane_ref, fwd_out, bwd_out, aggs, exs, slots, send_sem, recv_sem):
    count = lax.axis_size("ctx")
    me = lax.axis_index("ctx")
    row, col = lax.axis_index("dp"), lax.axis_index("head")
    rows = fwd_out.shape[1]
    shifts = []
    shift = 1
    while shift < count:
        shifts.append(shift)
        shift *= 2

    def device(index):
        return (row, index, col)

    barrier = pltpu.get_barrier_semaphore()
    for shift in shifts:
        for peer, present in ((me + shift, me + shift < count), (me - shift, me >= shift)):
            @pl.when(present)
            def _():
                pl.semaphore_signal(
                    barrier, inc=1, device_id=device(peer), device_id_type=pl.DeviceIdType.MESH
                )

    def at_least(bound):
        span = (count - 1) // bound + 1
        return (me // bound + span - 1) // span

    peers = 0
    for shift in shifts:
        peers = peers + at_least(shift) + 1 - at_least(count - shift)
    pl.semaphore_wait(barrier, peers)

    aggs[0, :, :rows, :] = fwd_ref[...]
    aggs[1, :, :rows, :] = bwd_ref[...]
    aggs[0, :, rows:, :] = lane_ref[...]
    aggs[1, :, rows:, :] = lane_ref[...]
    exs[...] = jnp.zeros_like(exs)
    exs[:, :, rows:, :] = jnp.ones_like(exs[:, :, rows:, :])

    for round_index, shift in enumerate(shifts):
        sends = (me + shift < count, me >= shift)
        targets = (me + shift, me - shift)
        sources = (me - shift, me + shift)

        last = round_index == len(shifts) - 1
        span = pl.ds(0, rows) if last else slice(None)

        def copy_of(side, peer):
            return pltpu.make_async_remote_copy(
                src_ref=aggs.at[side, :, span, :],
                dst_ref=slots.at[side, round_index, :, span, :],
                send_sem=send_sem.at[side, round_index],
                recv_sem=recv_sem.at[side, round_index],
                device_id=device(peer),
                device_id_type=pl.DeviceIdType.MESH,
            )

        for side in range(2):
            @pl.when(sends[side])
            def _():
                copy_of(side, targets[side]).start()

        for side in range(2):
            @pl.when(sends[side])
            def _():
                copy_of(side, targets[side]).wait_send()

        for side in range(2):
            @pl.when(sends[1 - side])
            def _():
                copy_of(side, sources[side]).wait_recv()
                got = slots[side, round_index, :, span, :]
                ex = exs[side]
                agg = aggs[side]
                ex_a = ex[:, rows:rows + 1, :]
                agg_a = agg[:, rows:rows + 1, :]
                exs[side, :, :rows, :] = ex_a * got[:, :rows, :] + ex[:, :rows, :]
                if not last:
                    exs[side, :, rows:, :] = ex[:, rows:, :] * got[:, rows:, :]
                    aggs[side, :, :rows, :] = agg_a * got[:, :rows, :] + agg[:, :rows, :]
                    aggs[side, :, rows:, :] = agg[:, rows:, :] * got[:, rows:, :]

    fwd_out[...] = exs[0, :, :rows, :]
    bwd_out[...] = exs[1, :, :rows, :]


def both_scans_kernel(decay, fwd_term, bwd_term, count):
    heads, rows, width = fwd_term.shape
    rounds = max(1, (count - 1).bit_length())
    lane = jnp.broadcast_to(decay[:, None, None], (heads, 8, width))
    packed = (heads, rows + 8, width)
    out = jax.ShapeDtypeStruct(fwd_term.shape, jnp.float32)
    return pl.pallas_call(
        scan_kernel,
        out_shape=(out, out),
        in_specs=[pl.BlockSpec(memory_space=pltpu.VMEM)] * 3,
        out_specs=(pl.BlockSpec(memory_space=pltpu.VMEM),) * 2,
        scratch_shapes=[
            pltpu.VMEM((2,) + packed, jnp.float32),
            pltpu.VMEM((2,) + packed, jnp.float32),
            pltpu.VMEM((2, rounds) + packed, jnp.float32),
            pltpu.SemaphoreType.DMA((2, rounds)),
            pltpu.SemaphoreType.DMA((2, rounds)),
        ],
        compiler_params=pltpu.CompilerParams(collective_id=1, has_side_effects=True),
    )(fwd_term, bwd_term, lane)


def start_flags(doc_lengths, first_pos, num_rows):
    starts = jnp.cumsum(doc_lengths, dtype=jnp.int32) - doc_lengths
    positions = first_pos + jnp.arange(num_rows, dtype=jnp.int32)
    matches = jnp.any(positions[:, None] == starts[None, :], axis=1)
    return matches.astype(jnp.float32)


def make_step(key_gain, head_width):
    q_scale = head_width ** (-0.5)

    def block_step(carried, inputs):
        q_block, k_block, v_block, gate_block, flag_block = inputs
        k_bf = (k_block.astype(jnp.float32) * key_gain[None]).astype(jnp.bfloat16)
        q_float = q_block.astype(jnp.float32) * q_scale
        k_float = lax.optimization_barrier(k_bf).astype(jnp.float32)
        v_float = v_block.astype(jnp.float32)
        segment = jnp.cumsum(flag_block)
        positions = jnp.arange(flag_block.shape[0])
        same_doc = (segment[:, None] == segment[None, :]) & (
            positions[:, None] >= positions[None, :]
        )
        cum_decay = jnp.cumsum(gate_block, axis=1)
        exponent = cum_decay[:, :, None] - cum_decay[:, None, :]
        decays = jnp.where(same_doc[None], jnp.exp(jnp.where(same_doc[None], exponent, 0.0)), 0.0)
        scores = jnp.einsum("thd,shd->hts", q_block, k_bf, preferred_element_type=jnp.float32)
        weights = (scores * q_scale * decays).astype(jnp.bfloat16)
        within = jnp.einsum("hts,she->the", weights, v_block, preferred_element_type=jnp.float32)
        opened = (segment == 0).astype(cum_decay.dtype)
        carry_in = jnp.exp(cum_decay) * opened[None, :]
        across = (
            jnp.einsum("thd,hde->the", q_float, carried, precision=PRECISE) * carry_in.T[:, :, None]
        )
        tail_mask = (segment == segment[-1]).astype(cum_decay.dtype)
        to_end = jnp.exp(cum_decay[:, -1:] - cum_decay) * tail_mask[None, :]
        written = jnp.einsum(
            "shd,she->hde", k_float * to_end.T[:, :, None], v_float, precision=PRECISE
        )
        end_state = carried * carry_in[:, -1][:, None, None] + written
        return (end_state, within + across)

    return block_step


def run_blocks(q_rows, k_rows, v_rows, gate_rows, flags, key_gain, start_state):
    num_rows = q_rows.shape[0]
    head_count = key_gain.shape[0]
    head_width = key_gain.shape[1]
    num_blocks = num_rows // BLOCK

    def to_blocks(tensor):
        return tensor.reshape(num_blocks, BLOCK, head_count, head_width)

    gate_blocks = gate_rows.reshape(head_count, num_blocks, BLOCK).transpose(1, 0, 2)
    flag_blocks = flags.reshape(num_blocks, BLOCK)
    end_state, outputs = lax.scan(
        jax.checkpoint(make_step(key_gain, head_width)),
        start_state,
        (to_blocks(q_rows), to_blocks(k_rows), to_blocks(v_rows), gate_blocks, flag_blocks),
    )
    return (outputs.reshape(num_rows, head_count * head_width), end_state)


def shards(queries, keys_raw, values, gates, lengths, key_gain, cotangent):
    tok_rows = queries.shape[1]
    head_count = key_gain.shape[0]
    head_width = key_gain.shape[1]
    flags = start_flags(lengths[0], lax.axis_index("ctx") * tok_rows, tok_rows)
    q_rows, k_rows, v_rows, gate_rows = (queries[0], keys_raw[0], values[0], gates[0])
    segment = jnp.cumsum(flags)
    opened = (segment == 0).astype(jnp.float32)
    tail_mask = (segment == segment[-1]).astype(jnp.float32)
    cum_decay = jnp.cumsum(gate_rows, axis=1)
    shard_decay = jnp.exp(cum_decay[:, -1]) * opened[-1]
    to_end = jnp.exp(cum_decay[:, -1:] - cum_decay) * tail_mask[None, :]
    k_bf = (
        k_rows.reshape(tok_rows, head_count, head_width).astype(jnp.float32) * key_gain[None]
    ).astype(jnp.bfloat16)
    k_float = lax.optimization_barrier(k_bf).astype(jnp.float32)
    v_float = v_rows.reshape(tok_rows, head_count, head_width).astype(jnp.float32)
    local_end = jnp.einsum(
        "shd,she->hde", k_float * to_end.T[:, :, None], v_float, precision=PRECISE
    )
    ctx_size = lax.axis_size("ctx")
    local_grad = local_incoming_grad(q_rows, cotangent[0], cum_decay, opened, head_count, head_width)
    state_in, later_grad = both_scans_kernel(shard_decay, local_end, local_grad, ctx_size)

    def forward(q_part, k_part, v_part, gate_part, gain_part):
        return run_blocks(q_part, k_part, v_part, gate_part, flags, gain_part, state_in)

    (primal, end_state), pullback = jax.vjp(forward, q_rows, k_rows, v_rows, gate_rows, key_gain)
    cot_float = cotangent[0].astype(jnp.float32)
    grad_q, grad_k, grad_v, grad_a, gain_term = pullback((cot_float, later_grad))
    grad_gain = gain_sum(gain_term, ctx_size)
    return (
        primal.astype(jnp.bfloat16)[None],
        grad_q[None],
        grad_k[None],
        grad_v[None],
        grad_a[None],
        grad_gain,
    )


def solution(mesh):
    placed = (
        P("dp", "ctx", "head"),
        P("dp", "ctx", "head"),
        P("dp", "ctx", "head"),
        P("dp", "head", "ctx"),
        P("dp", None),
        P("head", None),
        P("dp", "ctx", "head"),
    )
    return jax.shard_map(
        shards,
        mesh=mesh,
        in_specs=placed,
        out_specs=(
            P("dp", "ctx", "head"),
            P("dp", "ctx", "head"),
            P("dp", "ctx", "head"),
            P("dp", "ctx", "head"),
            P("dp", "head", "ctx"),
            P("head", "dp"),
        ),
        check_vma=False,
    )
```
